32 devices in a mesh: expert: 8 (over y, x, core), tensor: 4 (over z).
Axes of the slice: x: 2, y: 2, z: 4, core: 2. Of those that a mesh axis runs over, the one named last changes fastest.
Arguments:
- inputs: float32 [7880, 512], P('expert'), may hold values from -6 to 6
- cotangent: float32 [7880, 512], P('expert'), may hold values from -6 to 6
- routes: int32 [2, 7880, 2], P(None, 'expert'), may hold values from 0 to 7, all different within a row
- priority: int32 [2, 7880], P(None, 'expert'), may hold values from 0 to 984, as said below
- attend_in: float32 [2, 3, 512, 512], P(None, None, 'expert', 'tensor'), may hold values from -0.375 to 0.375
- attend_out: float32 [2, 512, 512], P(None, 'tensor', 'expert'), may hold values from -1.5 to 1.5
- router: float32 [2, 512, 8], P(None, None, 'expert'), may hold values from -0.1875 to 0.1875
- norm_gains: float32 [2, 2, 512], P(None, None, 'expert'), may hold values from 0.25 to 1.75
- expert_in: float32 [2, 8, 512, 2048], P(None, 'expert', None, 'tensor'), may hold values from -0.25 to 0.25
- expert_out: float32 [2, 8, 2048, 512], P(None, 'expert', 'tensor'), may hold values from -0.5 to 0.5
Outputs:
- outputs: float32 [7880, 512], P('expert')
- input_grad: float32 [7880, 512], P('expert')
- attend_in_grad: float32 [2, 3, 512, 512], P(None, None, 'expert', 'tensor')
- attend_out_grad: float32 [2, 512, 512], P(None, 'tensor', 'expert')
- router_grad: float32 [2, 512, 8], P(None, None, 'expert')
- gains_grad: float32 [2, 2, 512], P(None, None, 'expert')
- expert_in_grad: float32 [2, 8, 512, 2048], P(None, 'expert', None, 'tensor')
- expert_out_grad: float32 [2, 8, 2048, 512], P(None, 'expert', 'tensor')
The draws below stay inside these ranges and needn't reach their ends.
Inputs may be any that keep to these rules, and one draw needn't show every extreme that they name: `routes`: in each block each token names two different experts, and every expert is named by some token. `priority`: in each block, the values within each device's 985 tokens are a permutation.
All inputs are finite; a program needn't handle non-finite values.
Results may differ from the reference program's by a relative error of at most 0.025.
The reference program's roundings to bfloat16 on the way count: a program that leaves them out, or rounds other values in their place, can miss the bound.
Values may be sent and summed in bfloat16 or wider, within the bound.
A program may use at most 192 MiB of HBM per device.

```python
import jax
import jax.numpy as jnp
from jax import lax

D = 512
HEADS = 8
HEAD_DIM = 64
FF = 2048
SEQ = 197
LAYERS = 2
IMG_DEV = 5
EXPERTS = 8
TOK_DEV = 985
TOKENS = 7880
CAP = 308
N_EXPERT = 8


def draw_priority(key, part):
    blocks = TOKENS // TOK_DEV
    keys_all = jax.random.split(key, LAYERS * blocks)
    perms = jax.vmap(lambda one_key: jax.random.permutation(one_key, TOK_DEV))(keys_all)
    return perms.reshape(LAYERS, TOKENS).astype(jnp.int32)


def level_of(rng, shape, cuts, low, top_value):
    def one(dim, blocks):
        steps = jax.random.uniform(jax.random.fold_in(jax.random.fold_in(rng, 6), dim), (blocks,), jnp.float32, low / len(cuts), top_value / len(cuts))
        return jnp.repeat(jnp.exp(steps), shape[dim] // blocks).reshape((-1,) + (1,) * (len(shape) - dim - 1))

    level = one(*cuts[0])
    for cut in cuts[1:]:
        level = level * one(*cut)
    return level


def different_ones(own_key, rows, count, top, lift):
    ranking = jax.random.permutation(jax.random.fold_in(own_key, 1), count)
    pull = ranking
    for power in range(3):
        pull = pull * pull // count
    pull = pull * lift // count
    chance = jax.random.randint(jax.random.fold_in(own_key, 2), (rows, count), 0, 4096) + pull
    sure = jax.random.permutation(jax.random.fold_in(own_key, 3), rows)[jnp.arange(count) % rows]
    chance = jnp.where(jnp.arange(rows)[:, None] == sure[None, :], 1 << 14, chance)
    score = chance * count + jnp.arange(count)
    return lax.top_k(score.astype(jnp.int32), top)[1].astype(jnp.int32)


def normal_values(rng, dims, width, bound, cuts=(), kind=jnp.bfloat16):
    values = width * jax.random.normal(rng, dims, jnp.float32)
    if cuts:
        values = values * level_of(rng, dims, cuts, -0.22, 0.18)
    return jnp.clip(values, -bound, bound).astype(kind)


def setup_inputs(seed: int = 0) -> dict:
    key_of = jax.random.split(jax.random.key(seed), 11)
    return {
        "inputs": normal_values(key_of[0], (TOKENS, D), 1.0, 6.0, ((0, 8),), jnp.float32),
        "cotangent": normal_values(key_of[1], (TOKENS, D), 1.0, 6.0, ((0, 8),), jnp.float32),
        "routes": different_ones(key_of[2], LAYERS * TOKENS, EXPERTS, 2, 2048).reshape((LAYERS, TOKENS, 2)),
        "priority": draw_priority(jax.random.fold_in(key_of[10], 71), 0),
        "attend_in": normal_values(key_of[4], (LAYERS, 3, D, HEADS * HEAD_DIM), (D // 2) ** -0.5, 0.375, ((2, 8), (3, 4)), jnp.float32),
        "attend_out": normal_values(key_of[5], (LAYERS, HEADS * HEAD_DIM, D), (HEADS * HEAD_DIM // 32) ** -0.5, 1.5, ((1, 4), (2, 8)), jnp.float32),
        "router": normal_values(key_of[6], (LAYERS, D, EXPERTS), (2 * D) ** -0.5, 0.1875, ((2, 8),), jnp.float32),
        "norm_gains": jnp.clip(1.0 + 0.15 * jax.random.normal(key_of[7], (LAYERS, 2, D), jnp.float32), 0.25, 1.75),
        "expert_in": normal_values(key_of[8], (LAYERS, EXPERTS, D, FF), D ** -0.5, 0.25, ((1, 8), (3, 4)), jnp.float32),
        "expert_out": normal_values(key_of[9], (LAYERS, EXPERTS, FF, D), (max(1, 4 * FF // (EXPERTS * EXPERTS))) ** -0.5, 0.5, ((1, 8), (2, 4)), jnp.float32),
    }


@jax.custom_vjp
def low(v):
    return lax.optimization_barrier(v.astype(jnp.bfloat16)).astype(jnp.float32)

@jax.custom_vjp
def low_back(v):
    return v

def low_keep(v):
    return (low(v), None)

def low_pass(kept, grad):
    return (grad,)

def back_keep(v):
    return (v, None)

def back_low(kept, grad):
    return (low(grad),)
low.defvjp(low_keep, low_pass)
low_back.defvjp(back_keep, back_low)
highest = lax.Precision.HIGHEST

def norm_rows(rows_in, gain_row):
    centred = rows_in - lax.optimization_barrier(jnp.mean(rows_in, axis=-1, keepdims=True))
    spread = lax.optimization_barrier(jnp.mean(centred * centred, axis=-1, keepdims=True))
    return centred * lax.rsqrt(spread + 1e-06) * gain_row

def gelu_exact(rows_in):
    return 0.5 * rows_in * (1.0 + lax.erf(rows_in * 0.7071067811865476))

def attend_group(pieces):
    queries, key_rows, values = pieces
    scores = low_back(jnp.einsum('iqhd,ikhd->ihqk', queries, key_rows, precision=highest) * HEAD_DIM ** (-0.5))
    attention = low(jax.nn.softmax(scores, axis=-1))
    return jnp.einsum('ihqk,ikhd->iqhd', attention, values, precision=highest)

def slot_table(routes_now, ranks_now):
    blocks = TOKENS // TOK_DEV
    chosen = routes_now.reshape(blocks, TOK_DEV, 2)
    rank_rows = ranks_now.reshape(blocks, TOK_DEV)
    columns = jnp.arange(EXPERTS, dtype=jnp.int32)
    first_hot = (chosen[:, :, 0, None] == columns).astype(jnp.float32)
    second = (chosen[:, :, 1, None] == columns).astype(jnp.float32)
    earlier = (rank_rows[:, None, :] < rank_rows[:, :, None]).astype(jnp.float32)
    count_first = jnp.einsum('btu,bue->bte', earlier, first_hot, precision=highest)
    count_second = jnp.einsum('btu,bue->bte', earlier, second, precision=highest)
    filled = lax.optimization_barrier(jnp.sum(first_hot, axis=1, keepdims=True))
    slot_first = lax.optimization_barrier(jnp.sum(count_first * first_hot, axis=-1))
    slot_second = lax.optimization_barrier(jnp.sum((filled + count_second) * second, axis=-1))
    return jnp.stack([slot_first, slot_second], axis=-1).astype(jnp.int32).reshape(TOKENS, 2)

def block_forward(stream, weights_now, routes_now, ranks_now):
    in_now, out_now, router_now, gains_now, win_now, wout_now = weights_now
    gains_b = low(gains_now)
    in_b = low(in_now)
    out_b = low(out_now)
    router_b = low(router_now)
    win_b = low(win_now)
    wout_b = low(wout_now)
    normed = low(norm_rows(stream, gains_b[0]))
    projected = [low_back(low(jnp.dot(normed, in_b[part_index], precision=highest))) for part_index in range(3)]
    shaped = tuple((piece_rows.reshape(N_EXPERT, IMG_DEV, SEQ, HEADS, HEAD_DIM) for piece_rows in projected))
    mixed_heads = lax.map(jax.checkpoint(attend_group), shaped)
    mixed_heads = low_back(low(mixed_heads.reshape(TOKENS, HEADS * HEAD_DIM)))
    branch = low_back(jnp.dot(mixed_heads, out_b, precision=highest))
    middle = stream + branch
    normed_two = low(norm_rows(middle, gains_b[1]))
    logits = low_back(jnp.dot(normed_two, router_b, precision=highest))
    probs_all = jax.nn.softmax(logits, axis=-1)
    gate_values = jnp.take_along_axis(probs_all, routes_now, axis=1)
    slot_nums = slot_table(routes_now, ranks_now)
    usable_pairs = slot_nums < CAP
    owner_block = jnp.arange(TOKENS, dtype=jnp.int32) // TOK_DEV
    buffer_size = N_EXPERT * EXPERTS * CAP
    target = jnp.where(usable_pairs, (owner_block[:, None] * EXPERTS + routes_now) * CAP + slot_nums, buffer_size)
    pair_ids = jnp.arange(2 * TOKENS, dtype=jnp.int32)
    source = jnp.full((buffer_size + 1,), 2 * TOKENS, jnp.int32).at[target.reshape(-1)].set(pair_ids)
    token_of = jnp.where(source < 2 * TOKENS, source // 2, TOKENS)[:buffer_size]
    padded = jnp.concatenate([normed_two, jnp.zeros((1, D), jnp.float32)], axis=0)
    dispatched = low_back(padded[token_of])
    per_expert = dispatched.reshape(N_EXPERT, EXPERTS, CAP, D).transpose(1, 0, 2, 3).reshape(EXPERTS, N_EXPERT * CAP, D)
    before = low_back(jnp.einsum('erd,edf->erf', per_expert, win_b, precision=highest))
    hidden = low(gelu_exact(before))
    outputs = low_back(low(jnp.einsum('erf,efd->erd', hidden, wout_b, precision=highest)))
    returned = outputs.reshape(EXPERTS, N_EXPERT, CAP, D).transpose(1, 0, 2, 3).reshape(buffer_size, D)
    returned = jnp.concatenate([returned, jnp.zeros((1, D), jnp.float32)], axis=0)
    picked = returned[target]
    return middle + lax.optimization_barrier(jnp.sum(gate_values[:, :, None] * picked, axis=1))

def reference(inputs, cotangent, routes, priority, attend_in, attend_out, router, norm_gains, expert_in, expert_out):

    def stack_forward(stream, in_all, out_all, router_all, gains_all, win_all, wout_all):
        for layer_index in range(LAYERS):
            weights_now = (in_all[layer_index], out_all[layer_index], router_all[layer_index], gains_all[layer_index], win_all[layer_index], wout_all[layer_index])
            stream = block_forward(stream, weights_now, routes[layer_index], priority[layer_index])
        return stream
    result, pullback = jax.vjp(stack_forward, inputs, attend_in, attend_out, router, norm_gains, expert_in, expert_out)
    gradients = pullback(cotangent)
    return (result, gradients[0], gradients[1], gradients[2], gradients[3], gradients[4], gradients[5], gradients[6])
```

```python
import jax
import jax.numpy as jnp
from jax import lax
from jax.sharding import PartitionSpec as P

HEAD_DIM = 64
SEQ = 197


def norm_rows(rows_in, gain_row):
    centred = rows_in - jnp.mean(rows_in, axis=-1, keepdims=True)
    spread = jnp.mean(centred * centred, axis=-1, keepdims=True)
    return centred * lax.rsqrt(spread + 1e-06) * gain_row


def gelu_exact(rows_in):
    return 0.5 * rows_in * (1.0 + lax.erf(rows_in * 0.7071067811865476))


def contract_rows(left_side, right_side):
    return lax.dot_general(
        left_side, right_side, (((0,), (0,)), ((), ())), preferred_element_type=jnp.float32
    )


def contract_last(left_side, right_side):
    return lax.dot_general(
        left_side, right_side, (((1,), (1,)), ((), ())), preferred_element_type=jnp.float32
    )


def exchange(rows):
    return lax.all_to_all(rows, "expert", split_axis=0, concat_axis=0, tiled=True)


def own_part(rows, width, axis=1):
    return lax.dynamic_slice_in_dim(rows, lax.axis_index("tensor") * width, width, axis=axis)


def slot_plan(chosen, rank_rows, experts, capacity):
    columns = lax.broadcasted_iota(jnp.int32, (1, experts), 1)
    first_hot = (chosen[:, 0:1] == columns).astype(jnp.bfloat16)
    second = (chosen[:, 1:2] == columns).astype(jnp.bfloat16)
    earlier = (rank_rows[None, :] < rank_rows[:, None]).astype(jnp.bfloat16)
    count_first = jnp.dot(earlier, first_hot, preferred_element_type=jnp.float32)
    count_second = jnp.dot(earlier, second, preferred_element_type=jnp.float32)
    first_f = first_hot.astype(jnp.float32)
    second_f = second.astype(jnp.float32)
    filled = jnp.sum(first_f, axis=0, keepdims=True)
    slot_first = jnp.sum(count_first * first_f, axis=1)
    slot_second = jnp.sum((filled + count_second) * second_f, axis=1)
    slot_nums = jnp.stack([slot_first, slot_second], axis=1).astype(jnp.int32)
    target = jnp.where(slot_nums < capacity, chosen * capacity + slot_nums, experts * capacity)
    return (target, first_f, second_f)


def local(
    inputs,
    cotangent,
    routes,
    priority,
    attend_in,
    attend_out,
    router,
    norm_gains,
    expert_in,
    expert_out,
):
    experts = lax.axis_size("expert")
    tokens = inputs.shape[0]
    model_width = inputs.shape[1]
    images = tokens // SEQ
    head_cols = attend_in.shape[3]
    hidden_cols = expert_in.shape[3]
    local_heads = head_cols * lax.axis_size("tensor") // HEAD_DIM
    layers = attend_in.shape[0]
    capacity = max(2, (10 * tokens + 4 * experts - 1) // (4 * experts))
    slots_all = experts * capacity
    score_scale = HEAD_DIM ** (-0.5)
    layer_ids = range(layers)
    gains_full = lax.all_gather(norm_gains.astype(jnp.bfloat16), "expert", axis=2, tiled=True)
    router_full = lax.all_gather(router.astype(jnp.bfloat16), "expert", axis=2, tiled=True)
    in_full = []
    out_full = []
    win_full = []
    wout_full = []
    for layer_index in layer_ids:
        in_part = lax.all_gather(
            attend_in[layer_index].astype(jnp.bfloat16), "tensor", axis=2, tiled=True
        )
        in_full.append(lax.all_gather(in_part, "expert", axis=1, tiled=True))
        out_part = lax.all_gather(
            attend_out[layer_index].astype(jnp.bfloat16), "tensor", axis=0, tiled=True
        )
        out_full.append(lax.all_gather(out_part, "expert", axis=1, tiled=True))
        win_full.append(
            lax.all_gather(
                expert_in[layer_index, 0].astype(jnp.bfloat16), "tensor", axis=1, tiled=True
            )
        )
        wout_full.append(
            lax.all_gather(
                expert_out[layer_index, 0].astype(jnp.bfloat16), "tensor", axis=0, tiled=True
            )
        )
    slot_ids = lax.broadcasted_iota(jnp.int32, (1, slots_all), 1)
    stream = inputs
    stash_list = []
    for layer_index in range(layers):
        gains_now = gains_full[layer_index].astype(jnp.float32)
        normed = norm_rows(stream, gains_now[0]).astype(jnp.bfloat16)
        project = in_full[layer_index]
        triple = jnp.einsum(
            "td,jdh->jth", normed, project, preferred_element_type=jnp.float32
        ).astype(jnp.bfloat16)
        shaped = triple.reshape(3, images, SEQ, local_heads, HEAD_DIM)
        scores = (
            jnp.einsum("iqhd,ikhd->ihqk", shaped[0], shaped[1], preferred_element_type=jnp.float32)
            * score_scale
        )
        log_total = jax.nn.logsumexp(scores, axis=-1, keepdims=True)
        attention = jnp.exp(scores - log_total).astype(jnp.bfloat16)
        mixed_heads = (
            jnp.einsum("ihqk,ikhd->iqhd", attention, shaped[2], preferred_element_type=jnp.float32)
            .astype(jnp.bfloat16)
            .reshape(tokens, -1)
        )
        middle = stream + jnp.dot(
            mixed_heads, out_full[layer_index], preferred_element_type=jnp.float32
        )
        normed_two = norm_rows(middle, gains_now[1]).astype(jnp.bfloat16)
        logits = jnp.dot(normed_two, router_full[layer_index], preferred_element_type=jnp.float32)
        probs_all = jax.nn.softmax(logits, axis=-1)
        chosen = routes[layer_index]
        target, first_f, second_f = slot_plan(chosen, priority[layer_index], experts, capacity)
        gate_values = jnp.stack(
            [jnp.sum(probs_all * first_f, axis=1), jnp.sum(probs_all * second_f, axis=1)], axis=1
        )
        pick_first = (target[:, 0:1] == slot_ids).astype(jnp.bfloat16)
        pick_second = (target[:, 1:2] == slot_ids).astype(jnp.bfloat16)
        pick_both = pick_first + pick_second

        dispatched = contract_rows(pick_both, normed_two).astype(jnp.bfloat16)
        arrived = exchange(dispatched.reshape(experts, capacity, model_width)).reshape(
            slots_all, model_width
        )
        before = jnp.dot(arrived, win_full[layer_index], preferred_element_type=jnp.float32)
        hidden = gelu_exact(before).astype(jnp.bfloat16)
        expert_rows = jnp.dot(
            hidden, wout_full[layer_index], preferred_element_type=jnp.float32
        ).astype(jnp.bfloat16)
        returned = exchange(expert_rows.reshape(experts, capacity, model_width)).reshape(
            slots_all, model_width
        )
        rows_first = jnp.dot(pick_first, returned, preferred_element_type=jnp.float32)
        rows_second = jnp.dot(pick_second, returned, preferred_element_type=jnp.float32)
        output = middle + gate_values[:, 0:1] * rows_first + gate_values[:, 1:2] * rows_second
        stash_list.append(
            (
                stream,
                gains_now,
                normed,
                shaped,
                log_total,
                mixed_heads,
                middle,
                normed_two,
                probs_all,
                gate_values,
                target,
                first_f,
                second_f,
                pick_first,
                pick_second,
                pick_both,
                arrived,
                rows_first,
                rows_second,
            )
        )
        stream = output
    upstream = cotangent
    grads_in, grads_out, grads_router, grads_gain, grads_win, grads_wout = ([], [], [], [], [], [])
    for layer_index in reversed(range(layers)):
        (
            stream_in,
            gains_now,
            normed,
            shaped,
            log_total,
            mixed_heads,
            middle,
            normed_two,
            probs_all,
            gate_values,
            target,
            first_f,
            second_f,
            pick_first,
            pick_second,
            pick_both,
            arrived,
            rows_first,
            rows_second,
        ) = stash_list[layer_index]
        gate_first = jnp.sum(upstream * rows_first, axis=1)
        gate_second = jnp.sum(upstream * rows_second, axis=1)
        scaled_first = (gate_values[:, 0:1] * upstream).astype(jnp.bfloat16)
        scaled_second = (gate_values[:, 1:2] * upstream).astype(jnp.bfloat16)
        grad_slots = (
            contract_rows(pick_first, scaled_first) + contract_rows(pick_second, scaled_second)
        ).astype(jnp.bfloat16)
        grad_arrived = exchange(grad_slots.reshape(experts, capacity, model_width)).reshape(
            slots_all, model_width
        )
        before = jnp.dot(arrived, win_full[layer_index], preferred_element_type=jnp.float32)
        hidden = gelu_exact(before).astype(jnp.bfloat16)
        grads_wout.append(contract_rows(own_part(hidden, hidden_cols), grad_arrived))
        grad_hidden = contract_last(grad_arrived, wout_full[layer_index])
        grad_before = jax.vjp(gelu_exact, before)[1](grad_hidden)[0].astype(jnp.bfloat16)
        grads_win.append(contract_rows(arrived, own_part(grad_before, hidden_cols)))
        grad_rows = contract_last(grad_before, win_full[layer_index]).astype(jnp.bfloat16)
        grad_dispatched = exchange(grad_rows.reshape(experts, capacity, model_width)).reshape(
            slots_all, model_width
        )
        grad_normed = jnp.dot(pick_both, grad_dispatched, preferred_element_type=jnp.float32)
        grad_probs = first_f * gate_first[:, None] + second_f * gate_second[:, None]
        grad_logits = (
            probs_all * (grad_probs - jnp.sum(probs_all * grad_probs, axis=1, keepdims=True))
        ).astype(jnp.bfloat16)
        grads_router.append(contract_rows(normed_two, grad_logits))
        grad_normed = grad_normed + contract_last(grad_logits, router_full[layer_index])
        norm_back = jax.vjp(norm_rows, middle, gains_now[1])[1](grad_normed)
        grad_middle = upstream + norm_back[0]
        grad_branch = grad_middle.astype(jnp.bfloat16)
        grads_out.append(contract_rows(own_part(mixed_heads, head_cols), grad_branch))
        grad_mixed = (
            contract_last(grad_branch, out_full[layer_index])
            .astype(jnp.bfloat16)
            .reshape(images, SEQ, local_heads, HEAD_DIM)
        )
        scores = (
            jnp.einsum("iqhd,ikhd->ihqk", shaped[0], shaped[1], preferred_element_type=jnp.float32)
            * score_scale
        )
        attention_f = jnp.exp(scores - log_total)
        attention = attention_f.astype(jnp.bfloat16)
        grad_value = jnp.einsum(
            "ihqk,iqhd->ikhd", attention, grad_mixed, preferred_element_type=jnp.float32
        ).astype(jnp.bfloat16)
        grad_attention = jnp.einsum(
            "iqhd,ikhd->ihqk", grad_mixed, shaped[2], preferred_element_type=jnp.float32
        )
        grad_scores = (
            attention_f
            * (grad_attention - jnp.sum(attention_f * grad_attention, axis=-1, keepdims=True))
        ).astype(jnp.bfloat16)
        grad_query = (
            jnp.einsum(
                "ihqk,ikhd->iqhd", grad_scores, shaped[1], preferred_element_type=jnp.float32
            )
            * score_scale
        ).astype(jnp.bfloat16)
        grad_key = (
            jnp.einsum(
                "ihqk,iqhd->ikhd", grad_scores, shaped[0], preferred_element_type=jnp.float32
            )
            * score_scale
        ).astype(jnp.bfloat16)
        grad_triple = jnp.stack([grad_query, grad_key, grad_value]).reshape(3, tokens, -1)
        grads_in.append(
            jnp.einsum(
                "td,jth->jdh",
                normed,
                own_part(grad_triple, head_cols, 2),
                preferred_element_type=jnp.float32,
            )
        )
        project = in_full[layer_index]
        grad_normed_one = jnp.einsum(
            "jth,jdh->td", grad_triple, project, preferred_element_type=jnp.float32
        )
        norm_back_one = jax.vjp(norm_rows, stream_in, gains_now[0])[1](grad_normed_one)
        grads_gain.append(jnp.stack([norm_back_one[1], norm_back[1]]))
        upstream = grad_middle + norm_back_one[0]
    in_grad_all = jnp.stack(grads_in[::-1])
    out_grad_all = jnp.stack(grads_out[::-1])
    router_grad_all = jnp.stack(grads_router[::-1])
    gain_grad_all = jnp.stack(grads_gain[::-1])
    reduced = (
        lax.psum_scatter(in_grad_all, "expert", scatter_dimension=2, tiled=True),
        lax.psum_scatter(out_grad_all, "expert", scatter_dimension=2, tiled=True),
        lax.psum_scatter(router_grad_all, "expert", scatter_dimension=2, tiled=True),
        lax.psum_scatter(gain_grad_all, "expert", scatter_dimension=2, tiled=True),
    )
    win_grad_all = jnp.stack(grads_win[::-1])[:, None]
    wout_grad_all = jnp.stack(grads_wout[::-1])[:, None]
    return (
        stream,
        upstream,
        reduced[0],
        reduced[1],
        reduced[2],
        reduced[3],
        win_grad_all,
        wout_grad_all,
    )


def solution(mesh):
    placed = (
        P("expert", None),
        P("expert", None),
        P(None, "expert", None),
        P(None, "expert"),
        P(None, None, "expert", "tensor"),
        P(None, "tensor", "expert"),
        P(None, None, "expert"),
        P(None, None, "expert"),
        P(None, "expert", None, "tensor"),
        P(None, "expert", "tensor", None),
    )
    return jax.shard_map(
        local,
        mesh=mesh,
        in_specs=placed,
        out_specs=(
            P("expert", None),
            P("expert", None),
            P(None, None, "expert", "tensor"),
            P(None, "tensor", "expert"),
            P(None, None, "expert"),
            P(None, None, "expert"),
            P(None, "expert", None, "tensor"),
            P(None, "expert", "tensor", None),
        ),
        check_vma=False,
    )
```

```python
import functools

import jax
import jax.numpy as jnp
from jax import lax
from jax.experimental import pallas as pl
from jax.experimental.pallas import tpu as pltpu
from jax.sharding import PartitionSpec as P

HEAD_DIM = 64
SEQ = 197


def norm_rows(rows_in, gain_row):
    centred = rows_in - jnp.mean(rows_in, axis=-1, keepdims=True)
    spread = jnp.mean(centred * centred, axis=-1, keepdims=True)
    return centred * lax.rsqrt(spread + 1e-06) * gain_row


def gelu_exact(rows_in):
    return 0.5 * rows_in * (1.0 + lax.erf(rows_in * 0.7071067811865476))


def contract_rows(left_side, right_side):
    return lax.dot_general(
        left_side, right_side, (((0,), (0,)), ((), ())), preferred_element_type=jnp.float32
    )


def contract_last(left_side, right_side):
    return lax.dot_general(
        left_side, right_side, (((1,), (1,)), ((), ())), preferred_element_type=jnp.float32
    )


def gelu_parts(rows_in):
    half = 0.5 * (1.0 + lax.erf(rows_in * 0.7071067811865476))
    slope = half + rows_in * (jnp.exp(-0.5 * rows_in * rows_in) * 0.3989422804014327)
    return rows_in * half, slope


def meet_peers(me, peers):
    barrier = pltpu.get_barrier_semaphore()

    def greet(step, carry):
        pl.semaphore_signal(
            barrier,
            inc=1,
            device_id={"expert": lax.rem(me + step, peers)},
            device_id_type=pl.DeviceIdType.MESH,
        )
        return carry

    lax.fori_loop(1, peers, greet, 0)
    pl.semaphore_wait(barrier, peers - 1)


def send_chunk(source, landing, sends, arrivals, step, peer):
    return pltpu.make_async_remote_copy(
        src_ref=source,
        dst_ref=landing,
        send_sem=sends.at[step],
        recv_sem=arrivals.at[step],
        device_id={"expert": peer},
        device_id_type=pl.DeviceIdType.MESH,
    )


def exchange_chunks(peers, work, out_rows, landed, results, back, sems):
    out_send, out_recv, back_send, back_recv = sems
    me = lax.axis_index("expert")
    meet_peers(me, peers)

    def start_out(step, carry):
        peer = lax.rem(me + step, peers)
        send_chunk(out_rows.at[peer], landed.at[me], out_send, out_recv, step, peer).start()
        return carry

    lax.fori_loop(1, peers, start_out, 0)
    landed[me] = out_rows[me]

    def one_chunk(step, carry):
        peer = lax.rem(me + peers - step, peers)

        @pl.when(step > 0)
        def _():
            send_chunk(
                out_rows.at[peer], landed.at[peer], out_send, out_recv, step, peer
            ).wait_recv()

        work(step, peer)

        @pl.when(step > 0)
        def _():
            send_chunk(results.at[step], back.at[me], back_send, back_recv, step, peer).start()

        return carry

    lax.fori_loop(0, peers, one_chunk, 0)
    back[me] = results[0]

    def finish(step, carry):
        ahead = lax.rem(me + step, peers)
        send_chunk(out_rows.at[ahead], landed.at[me], out_send, out_recv, step, ahead).wait_send()
        last = send_chunk(results.at[step], back.at[ahead], back_send, back_recv, step, ahead)
        last.wait_send()
        last.wait_recv()
        return carry

    lax.fori_loop(1, peers, finish, 0)


def forward_kernel(
    peers, parts, rows_ref, win_ref, wout_ref, landed, back, results, total, *sems
):
    width = win_ref.shape[1] // parts

    def work(step, peer):
        chunk = landed[peer]
        for part in range(parts):
            cols = slice(part * width, (part + 1) * width)
            before = jnp.dot(chunk, win_ref[:, cols], preferred_element_type=jnp.float32)
            hidden = gelu_exact(before).astype(jnp.bfloat16)
            term = jnp.dot(hidden, wout_ref[cols, :], preferred_element_type=jnp.float32)
            if part == 0:
                total[...] = term
            elif part < parts - 1:
                total[...] += term
            else:
                results[step] = (total[...] + term).astype(jnp.bfloat16)

    exchange_chunks(peers, work, rows_ref, landed, results, back, sems)


def backward_kernel(
    peers,
    parts,
    rows_ref,
    arrived_ref,
    win_ref,
    wout_ref,
    back,
    win_grad,
    wout_grad,
    landed,
    results,
    total,
    hidden_all,
    before_all,
    *sems,
):
    width = win_ref.shape[1] // parts
    own = lax.axis_index("tensor") * width
    win_grad[...] = jnp.zeros_like(win_grad)
    wout_grad[...] = jnp.zeros_like(wout_grad)

    def work(step, peer):
        chunk = arrived_ref[peer]
        grad_chunk = landed[peer]
        for part in range(parts):
            cols = slice(part * width, (part + 1) * width)
            before = jnp.dot(chunk, win_ref[:, cols], preferred_element_type=jnp.float32)
            value, slope = gelu_parts(before)
            grad_hidden = contract_last(grad_chunk, wout_ref[cols, :])
            grad_before = (grad_hidden * slope).astype(jnp.bfloat16)
            hidden_all[:, cols] = value.astype(jnp.bfloat16)
            before_all[:, cols] = grad_before
            term = contract_last(grad_before, win_ref[:, cols])
            if part == 0:
                total[...] = term
            elif part < parts - 1:
                total[...] += term
            else:
                results[step] = (total[...] + term).astype(jnp.bfloat16)
        mine = pl.ds(pl.multiple_of(own, width), width)
        wout_grad[...] += contract_rows(hidden_all[:, mine], grad_chunk)
        win_grad[...] += contract_rows(chunk, before_all[:, mine])

    exchange_chunks(peers, work, rows_ref, landed, results, back, sems)


def sum_kernel(peers, rows_ref, sum_ref, landed, sends, arrivals):
    me = lax.axis_index("expert")
    meet_peers(me, peers)

    def start_out(step, carry):
        peer = lax.rem(me + step, peers)
        send_chunk(rows_ref.at[peer], landed.at[me], sends, arrivals, step, peer).start()
        return carry

    lax.fori_loop(1, peers, start_out, 0)
    landed[me] = rows_ref[me]

    def finish(step, carry):
        peer = lax.rem(me + peers - step, peers)
        one = send_chunk(rows_ref.at[peer], landed.at[peer], sends, arrivals, step, peer)
        one.wait_send()
        one.wait_recv()
        return carry

    lax.fori_loop(1, peers, finish, 0)
    sum_ref[...] = landed[0].astype(jnp.float32)

    def add_one(source, carry):
        sum_ref[...] += landed[source].astype(jnp.float32)
        return carry

    lax.fori_loop(1, peers, add_one, 0)


def sum_shares(rows):
    peers = rows.shape[0]
    return pl.pallas_call(
        functools.partial(sum_kernel, peers),
        out_shape=jax.ShapeDtypeStruct(rows.shape[1:], jnp.float32),
        in_specs=whole_in_vmem(1),
        out_specs=whole_in_vmem(1)[0],
        scratch_shapes=[pltpu.VMEM(rows.shape, rows.dtype)] + exchange_sems(peers)[:2],
        compiler_params=pltpu.CompilerParams(collective_id=2, has_side_effects=True),
    )(rows)


def whole_in_vmem(count):
    return [pl.BlockSpec(memory_space=pltpu.VMEM)] * count


def exchange_sems(peers):
    return [pltpu.SemaphoreType.DMA((peers,)) for _ in range(4)]


def experts_forward(rows, win, wout, parts):
    peers, capacity, width = rows.shape
    like = jax.ShapeDtypeStruct(rows.shape, jnp.bfloat16)
    return pl.pallas_call(
        functools.partial(forward_kernel, peers, parts),
        out_shape=(like, like),
        in_specs=whole_in_vmem(3),
        out_specs=tuple(whole_in_vmem(2)),
        scratch_shapes=[
            pltpu.VMEM(rows.shape, jnp.bfloat16),
            pltpu.VMEM((capacity, width), jnp.float32),
        ]
        + exchange_sems(peers),
        compiler_params=pltpu.CompilerParams(collective_id=0, has_side_effects=True),
    )(rows, win, wout)


def experts_backward(rows, arrived, win, wout, parts):
    peers, capacity, width = rows.shape
    inner = win.shape[1]
    return pl.pallas_call(
        functools.partial(backward_kernel, peers, parts),
        out_shape=(
            jax.ShapeDtypeStruct(rows.shape, jnp.bfloat16),
            jax.ShapeDtypeStruct((width, inner // parts), jnp.float32),
            jax.ShapeDtypeStruct((inner // parts, width), jnp.float32),
        ),
        in_specs=whole_in_vmem(4),
        out_specs=tuple(whole_in_vmem(3)),
        scratch_shapes=[
            pltpu.VMEM(rows.shape, jnp.bfloat16),
            pltpu.VMEM(rows.shape, jnp.bfloat16),
            pltpu.VMEM((capacity, width), jnp.float32),
            pltpu.VMEM((capacity, inner), jnp.bfloat16),
            pltpu.VMEM((capacity, inner), jnp.bfloat16),
        ]
        + exchange_sems(peers),
        compiler_params=pltpu.CompilerParams(collective_id=1, has_side_effects=True),
    )(rows, arrived, win, wout)


def own_part(rows, width, axis=1):
    return lax.dynamic_slice_in_dim(rows, lax.axis_index("tensor") * width, width, axis=axis)


def slot_plan(chosen, rank_rows, experts, capacity, spacing):
    columns = lax.broadcasted_iota(jnp.int32, (1, experts), 1)
    first_hot = (chosen[:, 0:1] == columns).astype(jnp.bfloat16)
    second = (chosen[:, 1:2] == columns).astype(jnp.bfloat16)
    earlier = (rank_rows[None, :] < rank_rows[:, None]).astype(jnp.bfloat16)
    count_first = jnp.dot(earlier, first_hot, preferred_element_type=jnp.float32)
    count_second = jnp.dot(earlier, second, preferred_element_type=jnp.float32)
    first_f = first_hot.astype(jnp.float32)
    second_f = second.astype(jnp.float32)
    filled = jnp.sum(first_f, axis=0, keepdims=True)
    slot_first = jnp.sum(count_first * first_f, axis=1)
    slot_second = jnp.sum((filled + count_second) * second_f, axis=1)
    slot_nums = jnp.stack([slot_first, slot_second], axis=1).astype(jnp.int32)
    target = jnp.where(slot_nums < capacity, chosen * spacing + slot_nums, experts * spacing)
    return (target, first_f, second_f)


def local(
    inputs,
    cotangent,
    routes,
    priority,
    attend_in,
    attend_out,
    router,
    norm_gains,
    expert_in,
    expert_out,
):
    experts = lax.axis_size("expert")
    tokens = inputs.shape[0]
    model_width = inputs.shape[1]
    images = tokens // SEQ
    head_cols = attend_in.shape[3]
    hidden_cols = expert_in.shape[3]
    local_heads = head_cols * lax.axis_size("tensor") // HEAD_DIM
    layers = attend_in.shape[0]
    capacity = max(2, (10 * tokens + 4 * experts - 1) // (4 * experts))
    spacing = -(-capacity // 16) * 16
    slots_all = experts * spacing
    peers_tensor = lax.axis_size("tensor")
    score_scale = HEAD_DIM ** (-0.5)
    row_share = attend_in.shape[2]
    gain_share = norm_gains.shape[2]
    in_full, out_full, router_full, gains_full, win_full, wout_full = [], [], [], [], [], []
    for layer_index in range(layers):
        out_share = attend_out[layer_index].T[None]
        packed = [
            jnp.concatenate([attend_in[layer_index], out_share], axis=0).reshape(-1),
            router[layer_index].reshape(-1),
            norm_gains[layer_index].reshape(-1),
        ]
        sizes = [piece.shape[0] for piece in packed]
        flat = jnp.concatenate(packed).astype(jnp.bfloat16)
        flat = jnp.pad(flat, (0, -flat.shape[0] % 2048)).reshape(-1, 128)
        across = lax.all_gather(flat, "tensor", axis=0)
        whole = lax.all_gather(across, "expert", axis=0).reshape(experts, peers_tensor, -1)
        mats = whole[:, :, : sizes[0]].reshape(experts, peers_tensor, 4, row_share, head_cols)
        mats = mats.transpose(2, 0, 3, 1, 4).reshape(4, model_width, head_cols * peers_tensor)
        in_full.append(mats[:3])
        out_full.append(mats[3])
        smalls = whole[:, 0, sizes[0] :]
        router_full.append(smalls[:, : sizes[1]].T)
        gains_full.append(
            smalls[:, sizes[1] : sizes[1] + sizes[2]]
            .reshape(experts, 2, gain_share)
            .transpose(1, 0, 2)
            .reshape(2, model_width)
        )
        win_full.append(
            lax.all_gather(
                expert_in[layer_index, 0].astype(jnp.bfloat16), "tensor", axis=1, tiled=True
            )
        )
        wout_full.append(
            lax.all_gather(
                expert_out[layer_index, 0].astype(jnp.bfloat16), "tensor", axis=0, tiled=True
            )
        )
    slot_ids = lax.broadcasted_iota(jnp.int32, (1, slots_all), 1)
    stream = inputs
    stash_list = []
    for layer_index in range(layers):
        gains_now = gains_full[layer_index].astype(jnp.float32)
        normed = norm_rows(stream, gains_now[0]).astype(jnp.bfloat16)
        project = in_full[layer_index]
        triple = jnp.einsum(
            "td,jdh->jth", normed, project, preferred_element_type=jnp.float32
        ).astype(jnp.bfloat16)
        shaped = triple.reshape(3, images, SEQ, local_heads, HEAD_DIM)
        scores = (
            jnp.einsum("iqhd,ikhd->ihqk", shaped[0], shaped[1], preferred_element_type=jnp.float32)
            * score_scale
        )
        log_total = jax.nn.logsumexp(scores, axis=-1, keepdims=True)
        attention = jnp.exp(scores - log_total).astype(jnp.bfloat16)
        mixed_heads = (
            jnp.einsum("ihqk,ikhd->iqhd", attention, shaped[2], preferred_element_type=jnp.float32)
            .astype(jnp.bfloat16)
            .reshape(tokens, -1)
        )
        middle = stream + contract_last(mixed_heads, out_full[layer_index])
        normed_two = norm_rows(middle, gains_now[1]).astype(jnp.bfloat16)
        logits = jnp.dot(normed_two, router_full[layer_index], preferred_element_type=jnp.float32)
        probs_all = jax.nn.softmax(logits, axis=-1)
        chosen = routes[layer_index]
        target, first_f, second_f = slot_plan(
            chosen, priority[layer_index], experts, capacity, spacing
        )
        gate_values = jnp.stack(
            [jnp.sum(probs_all * first_f, axis=1), jnp.sum(probs_all * second_f, axis=1)], axis=1
        )
        pick_first = (target[:, 0:1] == slot_ids).astype(jnp.bfloat16)
        pick_second = (target[:, 1:2] == slot_ids).astype(jnp.bfloat16)
        pick_both = pick_first + pick_second

        dispatched = contract_rows(pick_both, normed_two).astype(jnp.bfloat16)
        arrived, returned = experts_forward(
            dispatched.reshape(experts, spacing, model_width),
            win_full[layer_index],
            wout_full[layer_index],
            peers_tensor,
        )
        returned = returned.reshape(slots_all, model_width)
        rows_first = jnp.dot(pick_first, returned, preferred_element_type=jnp.float32)
        rows_second = jnp.dot(pick_second, returned, preferred_element_type=jnp.float32)
        output = middle + gate_values[:, 0:1] * rows_first + gate_values[:, 1:2] * rows_second
        stash_list.append(
            (
                stream,
                gains_now,
                normed,
                shaped,
                log_total,
                mixed_heads,
                middle,
                normed_two,
                probs_all,
                gate_values,
                target,
                first_f,
                second_f,
                pick_first,
                pick_second,
                pick_both,
                arrived,
                rows_first,
                rows_second,
            )
        )
        stream = output
    upstream = cotangent
    grads_in, grads_out, grads_router, grads_gain, grads_win, grads_wout = ([], [], [], [], [], [])
    grads_shared = []
    for layer_index in reversed(range(layers)):
        (
            stream_in,
            gains_now,
            normed,
            shaped,
            log_total,
            mixed_heads,
            middle,
            normed_two,
            probs_all,
            gate_values,
            target,
            first_f,
            second_f,
            pick_first,
            pick_second,
            pick_both,
            arrived,
            rows_first,
            rows_second,
        ) = stash_list[layer_index]
        gate_first = jnp.sum(upstream * rows_first, axis=1)
        gate_second = jnp.sum(upstream * rows_second, axis=1)
        scaled_first = (gate_values[:, 0:1] * upstream).astype(jnp.bfloat16)
        scaled_second = (gate_values[:, 1:2] * upstream).astype(jnp.bfloat16)
        grad_slots = (
            contract_rows(pick_first, scaled_first) + contract_rows(pick_second, scaled_second)
        ).astype(jnp.bfloat16)
        grad_dispatched, win_grad, wout_grad = experts_backward(
            grad_slots.reshape(experts, spacing, model_width),
            arrived,
            win_full[layer_index],
            wout_full[layer_index],
            peers_tensor,
        )
        grads_win.append(win_grad)
        grads_wout.append(wout_grad)
        grad_dispatched = grad_dispatched.reshape(slots_all, model_width)
        grad_normed = jnp.dot(pick_both, grad_dispatched, preferred_element_type=jnp.float32)
        grad_probs = first_f * gate_first[:, None] + second_f * gate_second[:, None]
        grad_logits = (
            probs_all * (grad_probs - jnp.sum(probs_all * grad_probs, axis=1, keepdims=True))
        ).astype(jnp.bfloat16)
        router_grad = contract_rows(grad_logits, normed_two)
        grad_normed = grad_normed + contract_last(grad_logits, router_full[layer_index])
        norm_back = jax.vjp(norm_rows, middle, gains_now[1])[1](grad_normed)
        grad_middle = upstream + norm_back[0]
        grad_branch = grad_middle.astype(jnp.bfloat16)
        out_grad = contract_rows(grad_branch, own_part(mixed_heads, head_cols))
        grad_mixed = (
            jnp.dot(grad_branch, out_full[layer_index], preferred_element_type=jnp.float32)
            .astype(jnp.bfloat16)
            .reshape(images, SEQ, local_heads, HEAD_DIM)
        )
        scores = (
            jnp.einsum("iqhd,ikhd->ihqk", shaped[0], shaped[1], preferred_element_type=jnp.float32)
            * score_scale
        )
        attention_f = jnp.exp(scores - log_total)
        attention = attention_f.astype(jnp.bfloat16)
        grad_value = jnp.einsum(
            "ihqk,iqhd->ikhd", attention, grad_mixed, preferred_element_type=jnp.float32
        ).astype(jnp.bfloat16)
        grad_attention = jnp.einsum(
            "iqhd,ikhd->ihqk", grad_mixed, shaped[2], preferred_element_type=jnp.float32
        )
        grad_scores = (
            attention_f
            * (grad_attention - jnp.sum(attention_f * grad_attention, axis=-1, keepdims=True))
        ).astype(jnp.bfloat16)
        grad_query = (
            jnp.einsum(
                "ihqk,ikhd->iqhd", grad_scores, shaped[1], preferred_element_type=jnp.float32
            )
            * score_scale
        ).astype(jnp.bfloat16)
        grad_key = (
            jnp.einsum(
                "ihqk,iqhd->ikhd", grad_scores, shaped[0], preferred_element_type=jnp.float32
            )
            * score_scale
        ).astype(jnp.bfloat16)
        grad_triple = jnp.stack([grad_query, grad_key, grad_value]).reshape(3, tokens, -1)
        in_grad = jnp.einsum(
            "td,jth->jdh",
            normed,
            own_part(grad_triple, head_cols, 2),
            preferred_element_type=jnp.float32,
        )
        project = in_full[layer_index]
        grad_normed_one = jnp.einsum(
            "jth,jdh->td", grad_triple, project, preferred_element_type=jnp.float32
        )
        norm_back_one = jax.vjp(norm_rows, stream_in, gains_now[0])[1](grad_normed_one)
        mats_grad = jnp.concatenate([in_grad, out_grad[None]], axis=0)
        mats_grad = mats_grad.reshape(4, experts, row_share, head_cols).transpose(1, 0, 2, 3)
        gain_grad = jnp.stack([norm_back_one[1], norm_back[1]]).reshape(2, experts, gain_share)
        smalls = jnp.concatenate(
            [router_grad, gain_grad.transpose(1, 0, 2).reshape(experts, -1)], axis=1
        )
        smalls = jnp.pad(smalls, ((0, 0), (0, -smalls.shape[1] % 2048)))
        grads_shared.append(
            jnp.concatenate(
                [mats_grad.reshape(experts, -1, 128), smalls.reshape(experts, -1, 128)], axis=1
            ).astype(jnp.bfloat16)
        )
        upstream = grad_middle + norm_back_one[0]
    total_rows = grads_shared[0].shape[1]
    mat_rows = 4 * row_share * head_cols // 128
    shared_all = sum_shares(jnp.concatenate(grads_shared, axis=1))
    for order in range(layers):
        shared = shared_all[order * total_rows : (order + 1) * total_rows]
        mats_own = shared[:mat_rows].reshape(4, row_share, head_cols)
        small_own = shared[mat_rows:].reshape(-1)
        grads_in.append(mats_own[:3])
        grads_out.append(mats_own[3].T)
        grads_router.append(small_own[:model_width, None])
        grads_gain.append(
            small_own[model_width : model_width + 2 * gain_share].reshape(2, gain_share)
        )
    win_grad_all = jnp.stack(grads_win[::-1])[:, None]
    wout_grad_all = jnp.stack(grads_wout[::-1])[:, None]
    return (
        stream,
        upstream,
        jnp.stack(grads_in[::-1]),
        jnp.stack(grads_out[::-1]),
        jnp.stack(grads_router[::-1]),
        jnp.stack(grads_gain[::-1]),
        win_grad_all,
        wout_grad_all,
    )


def solution(mesh):
    placed = (
        P("expert", None),
        P("expert", None),
        P(None, "expert", None),
        P(None, "expert"),
        P(None, None, "expert", "tensor"),
        P(None, "tensor", "expert"),
        P(None, None, "expert"),
        P(None, None, "expert"),
        P(None, "expert", None, "tensor"),
        P(None, "expert", "tensor", None),
    )
    return jax.shard_map(
        local,
        mesh=mesh,
        in_specs=placed,
        out_specs=(
            P("expert", None),
            P("expert", None),
            P(None, None, "expert", "tensor"),
            P(None, "tensor", "expert"),
            P(None, None, "expert"),
            P(None, None, "expert"),
            P(None, "expert", None, "tensor"),
            P(None, "expert", "tensor", None),
        ),
        check_vma=False,
    )
```

```python
import functools

import jax
import jax.numpy as jnp
from jax import lax
from jax.experimental import pallas as pl
from jax.experimental.pallas import tpu as pltpu
from jax.sharding import PartitionSpec as P

HEAD_DIM = 64
SEQ = 197


def gelu_exact(rows_in):
    return 0.5 * rows_in * (1.0 + lax.erf(rows_in * 0.7071067811865476))


def contract_rows(left_side, right_side):
    return lax.dot_general(
        left_side, right_side, (((0,), (0,)), ((), ())), preferred_element_type=jnp.float32
    )


def contract_last(left_side, right_side):
    return lax.dot_general(
        left_side, right_side, (((1,), (1,)), ((), ())), preferred_element_type=jnp.float32
    )


def gelu_parts(rows_in):
    half = 0.5 * (1.0 + lax.erf(rows_in * 0.7071067811865476))
    slope = half + rows_in * (jnp.exp(-0.5 * rows_in * rows_in) * 0.3989422804014327)
    return rows_in * half, slope


def meet_peers(me, peers):
    barrier = pltpu.get_barrier_semaphore()

    def greet(step, carry):
        pl.semaphore_signal(
            barrier,
            inc=1,
            device_id={"expert": lax.rem(me + step, peers)},
            device_id_type=pl.DeviceIdType.MESH,
        )
        return carry

    lax.fori_loop(1, peers, greet, 0)
    pl.semaphore_wait(barrier, peers - 1)


def send_chunk(source, landing, sends, arrivals, step, peer):
    return pltpu.make_async_remote_copy(
        src_ref=source,
        dst_ref=landing,
        send_sem=sends.at[step],
        recv_sem=arrivals.at[step],
        device_id={"expert": peer},
        device_id_type=pl.DeviceIdType.MESH,
    )


def exchange_chunks(peers, work, out_rows, landed, results, back, sems):
    out_send, out_recv, back_send, back_recv = sems
    me = lax.axis_index("expert")
    meet_peers(me, peers)

    def start_out(step, carry):
        peer = lax.rem(me + step, peers)
        send_chunk(out_rows.at[peer], landed.at[me], out_send, out_recv, step, peer).start()
        return carry

    lax.fori_loop(1, peers, start_out, 0)
    landed[me] = out_rows[me]

    def one_chunk(step, carry):
        peer = lax.rem(me + peers - step, peers)

        @pl.when(step > 0)
        def _():
            send_chunk(
                out_rows.at[peer], landed.at[peer], out_send, out_recv, step, peer
            ).wait_recv()

        work(step, peer)

        @pl.when(step > 0)
        def _():
            send_chunk(results.at[step], back.at[me], back_send, back_recv, step, peer).start()

        return carry

    lax.fori_loop(0, peers, one_chunk, 0)
    back[me] = results[0]

    def finish(step, carry):
        ahead = lax.rem(me + step, peers)
        send_chunk(out_rows.at[ahead], landed.at[me], out_send, out_recv, step, ahead).wait_send()
        last = send_chunk(results.at[step], back.at[ahead], back_send, back_recv, step, ahead)
        last.wait_send()
        last.wait_recv()
        return carry

    lax.fori_loop(1, peers, finish, 0)


def forward_kernel(
    peers, parts, rows_ref, win_ref, wout_ref, landed, back, results, total, *sems
):
    width = win_ref.shape[1] // parts

    def work(step, peer):
        chunk = landed[peer]
        for part in range(parts):
            cols = slice(part * width, (part + 1) * width)
            before = jnp.dot(chunk, win_ref[:, cols], preferred_element_type=jnp.float32)
            hidden = gelu_exact(before).astype(jnp.bfloat16)
            term = jnp.dot(hidden, wout_ref[cols, :], preferred_element_type=jnp.float32)
            if part == 0:
                total[...] = term
            elif part < parts - 1:
                total[...] += term
            else:
                results[step] = (total[...] + term).astype(jnp.bfloat16)

    exchange_chunks(peers, work, rows_ref, landed, results, back, sems)


def backward_kernel(
    peers,
    parts,
    rows_ref,
    arrived_ref,
    win_ref,
    wout_ref,
    back,
    win_grad,
    wout_grad,
    landed,
    results,
    total,
    hidden_all,
    before_all,
    *sems,
):
    width = win_ref.shape[1] // parts
    own = lax.axis_index("tensor") * width
    win_grad[...] = jnp.zeros_like(win_grad)
    wout_grad[...] = jnp.zeros_like(wout_grad)

    def work(step, peer):
        chunk = arrived_ref[peer]
        grad_chunk = landed[peer]
        for part in range(parts):
            cols = slice(part * width, (part + 1) * width)
            before = jnp.dot(chunk, win_ref[:, cols], preferred_element_type=jnp.float32)
            value, slope = gelu_parts(before)
            grad_hidden = contract_last(grad_chunk, wout_ref[cols, :])
            grad_before = (grad_hidden * slope).astype(jnp.bfloat16)
            hidden_all[:, cols] = value.astype(jnp.bfloat16)
            before_all[:, cols] = grad_before
            term = contract_last(grad_before, win_ref[:, cols])
            if part == 0:
                total[...] = term
            elif part < parts - 1:
                total[...] += term
            else:
                results[step] = (total[...] + term).astype(jnp.bfloat16)
        mine = pl.ds(pl.multiple_of(own, width), width)
        wout_grad[...] += contract_rows(hidden_all[:, mine], grad_chunk)
        win_grad[...] += contract_rows(chunk, before_all[:, mine])

    exchange_chunks(peers, work, rows_ref, landed, results, back, sems)


def sum_kernel(peers, rows_ref, sum_ref, landed, sends, arrivals):
    me = lax.axis_index("expert")
    meet_peers(me, peers)

    def start_out(step, carry):
        peer = lax.rem(me + step, peers)
        send_chunk(rows_ref.at[peer], landed.at[me], sends, arrivals, step, peer).start()
        return carry

    lax.fori_loop(1, peers, start_out, 0)
    landed[me] = rows_ref[me]

    def finish(step, carry):
        peer = lax.rem(me + peers - step, peers)
        one = send_chunk(rows_ref.at[peer], landed.at[peer], sends, arrivals, step, peer)
        one.wait_send()
        one.wait_recv()
        return carry

    lax.fori_loop(1, peers, finish, 0)
    sum_ref[...] = landed[0].astype(jnp.float32)

    def add_one(source, carry):
        sum_ref[...] += landed[source].astype(jnp.float32)
        return carry

    lax.fori_loop(1, peers, add_one, 0)


def sum_shares(rows):
    peers = rows.shape[0]
    return pl.pallas_call(
        functools.partial(sum_kernel, peers),
        out_shape=jax.ShapeDtypeStruct(rows.shape[1:], jnp.float32),
        in_specs=whole_in_vmem(1),
        out_specs=whole_in_vmem(1)[0],
        scratch_shapes=[pltpu.VMEM(rows.shape, rows.dtype)] + exchange_sems(peers)[:2],
        compiler_params=pltpu.CompilerParams(collective_id=2, has_side_effects=True),
    )(rows)


def whole_in_vmem(count):
    return [pl.BlockSpec(memory_space=pltpu.VMEM)] * count


def exchange_sems(peers):
    return [pltpu.SemaphoreType.DMA((peers,)) for _ in range(4)]


def experts_forward(rows, win, wout, parts):
    peers, capacity, width = rows.shape
    like = jax.ShapeDtypeStruct(rows.shape, jnp.bfloat16)
    return pl.pallas_call(
        functools.partial(forward_kernel, peers, parts),
        out_shape=(like, like),
        in_specs=whole_in_vmem(3),
        out_specs=tuple(whole_in_vmem(2)),
        scratch_shapes=[
            pltpu.VMEM(rows.shape, jnp.bfloat16),
            pltpu.VMEM((capacity, width), jnp.float32),
        ]
        + exchange_sems(peers),
        compiler_params=pltpu.CompilerParams(collective_id=0, has_side_effects=True),
    )(rows, win, wout)


def experts_backward(rows, arrived, win, wout, parts):
    peers, capacity, width = rows.shape
    inner = win.shape[1]
    return pl.pallas_call(
        functools.partial(backward_kernel, peers, parts),
        out_shape=(
            jax.ShapeDtypeStruct(rows.shape, jnp.bfloat16),
            jax.ShapeDtypeStruct((width, inner // parts), jnp.float32),
            jax.ShapeDtypeStruct((inner // parts, width), jnp.float32),
        ),
        in_specs=whole_in_vmem(4),
        out_specs=tuple(whole_in_vmem(3)),
        scratch_shapes=[
            pltpu.VMEM(rows.shape, jnp.bfloat16),
            pltpu.VMEM(rows.shape, jnp.bfloat16),
            pltpu.VMEM((capacity, width), jnp.float32),
            pltpu.VMEM((capacity, inner), jnp.bfloat16),
            pltpu.VMEM((capacity, inner), jnp.bfloat16),
        ]
        + exchange_sems(peers),
        compiler_params=pltpu.CompilerParams(collective_id=1, has_side_effects=True),
    )(rows, arrived, win, wout)


def norm_parts(rows_in):
    centred = rows_in - jnp.mean(rows_in, axis=-1, keepdims=True)
    inverse = lax.rsqrt(jnp.mean(centred * centred, axis=-1, keepdims=True) + 1e-06)
    return centred * inverse, inverse


def norm_back(unit, inverse, gain_row, grad_rows):
    scaled = grad_rows * gain_row
    inner = scaled - jnp.mean(scaled, axis=-1, keepdims=True)
    return inverse * (inner - unit * jnp.mean(scaled * unit, axis=-1, keepdims=True))


def two_heads(rows):
    low_half = lax.broadcasted_iota(jnp.int32, rows.shape, 1) < HEAD_DIM
    none = jnp.zeros_like(rows)
    return jnp.concatenate([jnp.where(low_half, rows, none), jnp.where(low_half, none, rows)], 0)


def join_heads(stacked):
    rows = stacked.shape[0] // 2
    low_half = lax.broadcasted_iota(jnp.int32, (rows, stacked.shape[1]), 1) < HEAD_DIM
    return jnp.where(low_half, stacked[:rows], stacked[rows:])


def pair_attention(query_two, key_pair):
    scores = contract_last(query_two, key_pair) * (HEAD_DIM ** (-0.5))
    real_key = lax.broadcasted_iota(jnp.int32, scores.shape, 1) < SEQ
    scores = jnp.where(real_key, scores, -jnp.inf)
    weights = jnp.exp(scores - jnp.max(scores, axis=-1, keepdims=True))
    return weights * (1.0 / jnp.sum(weights, axis=-1, keepdims=True))


def project_qkv(normed, mats_ref):
    return [
        jnp.dot(normed, mats_ref[part], preferred_element_type=jnp.float32).astype(jnp.bfloat16)
        for part in range(3)
    ]


def attend_kernel(
    experts, stream_ref, mats_ref, gains_ref, router_ref, middle_ref, normed_ref, probs_ref, mixed_ref
):
    rows = stream_ref[0]
    normed = (norm_parts(rows)[0] * gains_ref[0:1]).astype(jnp.bfloat16)
    query, keys, values = project_qkv(normed, mats_ref)
    for pair in range(query.shape[1] // (2 * HEAD_DIM)):
        cols = slice(pair * 2 * HEAD_DIM, (pair + 1) * 2 * HEAD_DIM)
        attention = pair_attention(two_heads(query[:, cols]), keys[:, cols]).astype(jnp.bfloat16)
        mixed = jnp.dot(attention, values[:, cols], preferred_element_type=jnp.float32)
        mixed_ref[0, :, cols] = join_heads(mixed).astype(jnp.bfloat16)
    middle = rows + contract_last(mixed_ref[0], mats_ref[3])
    middle_ref[0] = middle
    normed_two = (norm_parts(middle)[0] * gains_ref[1:2]).astype(jnp.bfloat16)
    normed_ref[0] = normed_two
    logits = jnp.dot(normed_two, router_ref[...], preferred_element_type=jnp.float32)
    real = lax.broadcasted_iota(jnp.int32, logits.shape, 1) < experts
    logits = jnp.where(real, logits, -jnp.inf)
    odds = jnp.exp(logits - jnp.max(logits, axis=-1, keepdims=True))
    probs_ref[0] = odds * (1.0 / jnp.sum(odds, axis=-1, keepdims=True))


def attend_back_kernel(
    own_ref,
    upstream_ref,
    grad_ref,
    grad_logits_ref,
    stream_ref,
    middle_ref,
    mixed_ref,
    mats_ref,
    gains_ref,
    router_ref,
    down_ref,
    mats_grad,
    router_grad,
    gains_grad,
    triple,
):
    @pl.when(pl.program_id(0) == 0)
    def _():
        mats_grad[...] = jnp.zeros_like(mats_grad)
        router_grad[...] = jnp.zeros_like(router_grad)
        gains_grad[...] = jnp.zeros_like(gains_grad)

    head_cols = mats_grad.shape[2]
    mine = pl.ds(pl.multiple_of(own_ref[0] * head_cols, head_cols), head_cols)
    gain_one, gain_two = gains_ref[0:1], gains_ref[1:2]
    unit_two, inverse_two = norm_parts(middle_ref[0])
    grad_logits = grad_logits_ref[0]
    router_grad[...] += contract_rows(
        grad_logits, (unit_two * gain_two).astype(jnp.bfloat16)
    )
    grad_normed = grad_ref[0] + contract_last(grad_logits, router_ref[...])
    gains_grad[1:2] += jnp.sum(grad_normed * unit_two, axis=0, keepdims=True)
    grad_middle = upstream_ref[0] + norm_back(unit_two, inverse_two, gain_two, grad_normed)
    grad_branch = grad_middle.astype(jnp.bfloat16)
    mats_grad[3] += contract_rows(grad_branch, mixed_ref[0, :, mine])
    grad_mixed = jnp.dot(
        grad_branch, mats_ref[3], preferred_element_type=jnp.float32
    ).astype(jnp.bfloat16)
    unit_one, inverse_one = norm_parts(stream_ref[0])
    normed = (unit_one * gain_one).astype(jnp.bfloat16)
    query, keys, values = project_qkv(normed, mats_ref)
    scale = HEAD_DIM ** (-0.5)
    for pair in range(query.shape[1] // (2 * HEAD_DIM)):
        cols = slice(pair * 2 * HEAD_DIM, (pair + 1) * 2 * HEAD_DIM)
        query_two = two_heads(query[:, cols])
        attention = pair_attention(query_two, keys[:, cols])
        grad_two = two_heads(grad_mixed[:, cols])
        triple[2, :, cols] = contract_rows(attention.astype(jnp.bfloat16), grad_two).astype(
            jnp.bfloat16
        )
        grad_attention = contract_last(grad_two, values[:, cols])
        grad_scores = (
            attention
            * (grad_attention - jnp.sum(attention * grad_attention, axis=-1, keepdims=True))
        ).astype(jnp.bfloat16)
        grad_query = jnp.dot(grad_scores, keys[:, cols], preferred_element_type=jnp.float32)
        triple[0, :, cols] = (join_heads(grad_query) * scale).astype(jnp.bfloat16)
        triple[1, :, cols] = (contract_rows(grad_scores, query_two) * scale).astype(jnp.bfloat16)
    grad_one = contract_last(triple[0], mats_ref[0])
    for part in range(3):
        if part:
            grad_one += contract_last(triple[part], mats_ref[part])
        mats_grad[part] += contract_rows(normed, triple[part, :, mine])
    gains_grad[0:1] += jnp.sum(grad_one * unit_one, axis=0, keepdims=True)
    down_ref[0] = grad_middle + norm_back(unit_one, inverse_one, gain_one, grad_one)


def image_spec(array):
    return pl.BlockSpec((1,) + array.shape[1:], lambda image: (image, 0, 0))


def fixed_spec(array):
    return pl.BlockSpec(array.shape, lambda image: (0,) * len(array.shape))


def attend(stream, mats, gains, router, experts):
    images, rows, width = stream.shape
    outs = (
        jax.ShapeDtypeStruct(stream.shape, jnp.float32),
        jax.ShapeDtypeStruct(stream.shape, jnp.bfloat16),
        jax.ShapeDtypeStruct((images, rows, router.shape[1]), jnp.float32),
        jax.ShapeDtypeStruct((images, rows, mats.shape[2]), jnp.bfloat16),
    )
    return pl.pallas_call(
        functools.partial(attend_kernel, experts),
        grid=(images,),
        out_shape=outs,
        in_specs=[image_spec(stream), fixed_spec(mats), fixed_spec(gains), fixed_spec(router)],
        out_specs=tuple(image_spec(one) for one in outs),
    )(stream, mats, gains, router)


def attend_back(upstream, grad_normed, grad_logits, stream, middle, mixed, mats, gains, router, head_cols):
    images, rows, width = stream.shape
    own = lax.axis_index("tensor").astype(jnp.int32).reshape(1)
    sums = (
        jax.ShapeDtypeStruct((4, width, head_cols), jnp.float32),
        jax.ShapeDtypeStruct((router.shape[1], width), jnp.float32),
        jax.ShapeDtypeStruct(gains.shape, jnp.float32),
    )
    per_image = [upstream, grad_normed, grad_logits, stream, middle, mixed]
    fixed = [mats, gains, router]
    return pl.pallas_call(
        attend_back_kernel,
        grid=(images,),
        out_shape=(jax.ShapeDtypeStruct(stream.shape, jnp.float32),) + sums,
        in_specs=[pl.BlockSpec(memory_space=pltpu.SMEM)]
        + [image_spec(one) for one in per_image]
        + [fixed_spec(one) for one in fixed],
        out_specs=(image_spec(stream),) + tuple(fixed_spec(one) for one in sums),
        scratch_shapes=[pltpu.VMEM((3, rows, mats.shape[2]), jnp.bfloat16)],
    )(own, *per_image, *fixed)


def slot_plan(chosen, rank_rows, experts, capacity, spacing):
    columns = lax.broadcasted_iota(jnp.int32, (1, experts), 1)
    first_hot = (chosen[:, 0:1] == columns).astype(jnp.bfloat16)
    second = (chosen[:, 1:2] == columns).astype(jnp.bfloat16)
    earlier = (rank_rows[None, :] < rank_rows[:, None]).astype(jnp.bfloat16)
    count_first = jnp.dot(earlier, first_hot, preferred_element_type=jnp.float32)
    count_second = jnp.dot(earlier, second, preferred_element_type=jnp.float32)
    first_f = first_hot.astype(jnp.float32)
    second_f = second.astype(jnp.float32)
    filled = jnp.sum(first_f, axis=0, keepdims=True)
    slot_first = jnp.sum(count_first * first_f, axis=1)
    slot_second = jnp.sum((filled + count_second) * second_f, axis=1)
    slot_nums = jnp.stack([slot_first, slot_second], axis=1).astype(jnp.int32)
    target = jnp.where(slot_nums < capacity, chosen * spacing + slot_nums, experts * spacing)
    return (target, first_f, second_f)


def local(
    inputs,
    cotangent,
    routes,
    priority,
    attend_in,
    attend_out,
    router,
    norm_gains,
    expert_in,
    expert_out,
):
    experts = lax.axis_size("expert")
    tokens = inputs.shape[0]
    model_width = inputs.shape[1]
    images = tokens // SEQ
    head_cols = attend_in.shape[3]
    layers = attend_in.shape[0]
    capacity = max(2, (10 * tokens + 4 * experts - 1) // (4 * experts))
    spacing = -(-capacity // 16) * 16
    slots_all = experts * spacing
    peers_tensor = lax.axis_size("tensor")
    row_share = attend_in.shape[2]
    gain_share = norm_gains.shape[2]
    image_rows = -(-SEQ // 16) * 16
    tokens_all = images * image_rows

    def spread(rows, fill):
        shaped = rows.reshape((images, SEQ) + rows.shape[1:])
        edges = ((0, 0), (0, image_rows - SEQ)) + ((0, 0),) * (rows.ndim - 1)
        return jnp.pad(shaped, edges, constant_values=fill)

    def gather_tensor(rows, axis):
        return lax.all_gather(rows.astype(jnp.bfloat16), "tensor", axis=axis, tiled=True)

    smalls = jnp.concatenate([router.reshape(-1), norm_gains.reshape(-1)])
    block = row_share * head_cols
    smalls = jnp.pad(smalls, (0, -smalls.shape[0] % block)).reshape(-1, row_share, head_cols)
    packed = jnp.concatenate(
        [
            jnp.concatenate([attend_in, attend_out.transpose(0, 2, 1)[:, None]], axis=1).reshape(
                -1, row_share, head_cols
            ),
            smalls,
        ]
    )
    whole = lax.all_gather(gather_tensor(packed, 2), "expert", axis=1, tiled=True)
    small_rows = whole[4 * layers :, :, :head_cols].reshape(-1, experts, block)
    small_rows = small_rows.transpose(1, 0, 2).reshape(experts, -1)
    router_all = small_rows[:, : layers * model_width].reshape(experts, layers, model_width)
    gains_all = small_rows[:, layers * model_width :][:, : layers * 2 * gain_share]
    gains_all = gains_all.reshape(experts, layers, 2, gain_share).transpose(1, 2, 0, 3)
    gains_all = gains_all.reshape(layers, 2, model_width).astype(jnp.float32)
    router_all = jnp.pad(router_all.transpose(1, 2, 0), ((0, 0), (0, 0), (0, -experts % 128)))
    win_full = [gather_tensor(expert_in[layer_index, 0], 1) for layer_index in range(layers)]
    wout_full = [gather_tensor(expert_out[layer_index, 0], 0) for layer_index in range(layers)]
    slot_ids = lax.broadcasted_iota(jnp.int32, (1, slots_all), 1)
    stream = spread(inputs, 0)
    stash_list = []
    for layer_index in range(layers):
        mats = whole[4 * layer_index : 4 * layer_index + 4]
        gains_now = gains_all[layer_index]
        router_now = router_all[layer_index]
        middle, normed_two, probs_all, mixed_heads = attend(
            stream, mats, gains_now, router_now, experts
        )
        probs_all = probs_all.reshape(tokens_all, -1)[:, :experts]
        chosen = spread(routes[layer_index], -1).reshape(tokens_all, 2)
        ranks = spread(priority[layer_index], tokens).reshape(tokens_all)
        target, first_f, second_f = slot_plan(chosen, ranks, experts, capacity, spacing)
        gate_values = jnp.stack(
            [jnp.sum(probs_all * first_f, axis=1), jnp.sum(probs_all * second_f, axis=1)], axis=1
        )
        pick_first = (target[:, 0:1] == slot_ids).astype(jnp.bfloat16)
        pick_second = (target[:, 1:2] == slot_ids).astype(jnp.bfloat16)
        pick_both = pick_first + pick_second
        dispatched = contract_rows(pick_both, normed_two.reshape(tokens_all, model_width))
        arrived, returned = experts_forward(
            dispatched.astype(jnp.bfloat16).reshape(experts, spacing, model_width),
            win_full[layer_index],
            wout_full[layer_index],
            peers_tensor,
        )
        returned = returned.reshape(slots_all, model_width)
        rows_first = jnp.dot(pick_first, returned, preferred_element_type=jnp.float32)
        rows_second = jnp.dot(pick_second, returned, preferred_element_type=jnp.float32)
        output = (
            middle.reshape(tokens_all, model_width)
            + gate_values[:, 0:1] * rows_first
            + gate_values[:, 1:2] * rows_second
        )
        stash_list.append(
            (
                stream,
                mats,
                gains_now,
                router_now,
                mixed_heads,
                middle,
                probs_all,
                gate_values,
                first_f,
                second_f,
                pick_first,
                pick_second,
                pick_both,
                arrived,
                rows_first,
                rows_second,
            )
        )
        stream = output.reshape(images, image_rows, model_width)
    upstream = spread(cotangent, 0).reshape(tokens_all, model_width)
    grads_in, grads_out, grads_router, grads_gain, grads_win, grads_wout = ([], [], [], [], [], [])
    grads_shared = []
    for layer_index in reversed(range(layers)):
        (
            stream_in,
            mats,
            gains_now,
            router_now,
            mixed_heads,
            middle,
            probs_all,
            gate_values,
            first_f,
            second_f,
            pick_first,
            pick_second,
            pick_both,
            arrived,
            rows_first,
            rows_second,
        ) = stash_list[layer_index]
        gate_first = jnp.sum(upstream * rows_first, axis=1)
        gate_second = jnp.sum(upstream * rows_second, axis=1)
        scaled_first = (gate_values[:, 0:1] * upstream).astype(jnp.bfloat16)
        scaled_second = (gate_values[:, 1:2] * upstream).astype(jnp.bfloat16)
        grad_slots = (
            contract_rows(pick_first, scaled_first) + contract_rows(pick_second, scaled_second)
        ).astype(jnp.bfloat16)
        grad_dispatched, win_grad, wout_grad = experts_backward(
            grad_slots.reshape(experts, spacing, model_width),
            arrived,
            win_full[layer_index],
            wout_full[layer_index],
            peers_tensor,
        )
        grads_win.append(win_grad)
        grads_wout.append(wout_grad)
        grad_dispatched = grad_dispatched.reshape(slots_all, model_width)
        grad_normed = jnp.dot(pick_both, grad_dispatched, preferred_element_type=jnp.float32)
        grad_probs = first_f * gate_first[:, None] + second_f * gate_second[:, None]
        grad_logits = (
            probs_all * (grad_probs - jnp.sum(probs_all * grad_probs, axis=1, keepdims=True))
        ).astype(jnp.bfloat16)
        grad_logits = jnp.pad(grad_logits, ((0, 0), (0, router_now.shape[1] - experts)))
        shape = stream_in.shape
        down, mats_grad, router_grad, gain_grad = attend_back(
            upstream.reshape(shape),
            grad_normed.reshape(shape),
            grad_logits.reshape(images, image_rows, -1),
            stream_in,
            middle,
            mixed_heads,
            mats,
            gains_now,
            router_now,
            head_cols,
        )
        mats_grad = mats_grad.reshape(4, experts, row_share, head_cols).transpose(1, 0, 2, 3)
        router_grad = router_grad[:experts]
        gain_grad = gain_grad.reshape(2, experts, gain_share)
        smalls = jnp.concatenate(
            [router_grad, gain_grad.transpose(1, 0, 2).reshape(experts, -1)], axis=1
        )
        smalls = jnp.pad(smalls, ((0, 0), (0, -smalls.shape[1] % 2048)))
        grads_shared.append(
            jnp.concatenate(
                [mats_grad.reshape(experts, -1, 128), smalls.reshape(experts, -1, 128)], axis=1
            ).astype(jnp.bfloat16)
        )
        upstream = down.reshape(tokens_all, model_width)
    total_rows = grads_shared[0].shape[1]
    mat_rows = 4 * row_share * head_cols // 128
    shared_all = sum_shares(jnp.concatenate(grads_shared, axis=1))
    for order in range(layers):
        shared = shared_all[order * total_rows : (order + 1) * total_rows]
        mats_own = shared[:mat_rows].reshape(4, row_share, head_cols)
        small_own = shared[mat_rows:].reshape(-1)
        grads_in.append(mats_own[:3])
        grads_out.append(mats_own[3].T)
        grads_router.append(small_own[:model_width, None])
        grads_gain.append(
            small_own[model_width : model_width + 2 * gain_share].reshape(2, gain_share)
        )
    win_grad_all = jnp.stack(grads_win[::-1])[:, None]
    wout_grad_all = jnp.stack(grads_wout[::-1])[:, None]
    return (
        stream[:, :SEQ].reshape(tokens, model_width),
        upstream.reshape(stream.shape)[:, :SEQ].reshape(tokens, model_width),
        jnp.stack(grads_in[::-1]),
        jnp.stack(grads_out[::-1]),
        jnp.stack(grads_router[::-1]),
        jnp.stack(grads_gain[::-1]),
        win_grad_all,
        wout_grad_all,
    )


def solution(mesh):
    placed = (
        P("expert", None),
        P("expert", None),
        P(None, "expert", None),
        P(None, "expert"),
        P(None, None, "expert", "tensor"),
        P(None, "tensor", "expert"),
        P(None, None, "expert"),
        P(None, None, "expert"),
        P(None, "expert", None, "tensor"),
        P(None, "expert", "tensor", None),
    )
    return jax.shard_map(
        local,
        mesh=mesh,
        in_specs=placed,
        out_specs=(
            P("expert", None),
            P("expert", None),
            P(None, None, "expert", "tensor"),
            P(None, "tensor", "expert"),
            P(None, None, "expert"),
            P(None, None, "expert"),
            P(None, "expert", None, "tensor"),
            P(None, "expert", "tensor", None),
        ),
        check_vma=False,
    )
```

```python
import functools

import jax
import jax.numpy as jnp
from jax import lax
from jax.experimental import pallas as pl
from jax.experimental.pallas import tpu as pltpu
from jax.sharding import PartitionSpec as P

HEAD_DIM = 64
SEQ = 197


def gelu_exact(rows_in):
    return 0.5 * rows_in * (1.0 + lax.erf(rows_in * 0.7071067811865476))


def contract_rows(left_side, right_side):
    return lax.dot_general(
        left_side, right_side, (((0,), (0,)), ((), ())), preferred_element_type=jnp.float32
    )


def contract_last(left_side, right_side):
    return lax.dot_general(
        left_side, right_side, (((1,), (1,)), ((), ())), preferred_element_type=jnp.float32
    )


def gelu_parts(rows_in):
    half = 0.5 * (1.0 + lax.erf(rows_in * 0.7071067811865476))
    slope = half + rows_in * (jnp.exp(-0.5 * rows_in * rows_in) * 0.3989422804014327)
    return rows_in * half, slope


def greet(barrier, axis, index):
    pl.semaphore_signal(
        barrier, inc=1, device_id={axis: index}, device_id_type=pl.DeviceIdType.MESH
    )


def greet_axis(barrier, axis, me, peers):
    def one(step, carry):
        greet(barrier, axis, lax.rem(me + step, peers))
        return carry

    lax.fori_loop(1, peers, one, 0)


def send(source, landing, send_sem, recv_sem, axis, index):
    return pltpu.make_async_remote_copy(
        src_ref=source,
        dst_ref=landing,
        send_sem=send_sem,
        recv_sem=recv_sem,
        device_id={axis: index},
        device_id_type=pl.DeviceIdType.MESH,
    )


def send_chunk(source, landing, sends, arrivals, step, peer):
    return send(source, landing, sends.at[step], arrivals.at[step], "expert", peer)


def meet_peers(me, peers):
    barrier = pltpu.get_barrier_semaphore()
    greet_axis(barrier, "expert", me, peers)
    pl.semaphore_wait(barrier, peers - 1)


def gather_kernel(
    experts,
    parts,
    small_ref,
    win_ref,
    wout_ref,
    whole,
    win_full,
    wout_full,
    side_send,
    side_recv,
    chip_send,
    chip_recv,
    twin_send,
    twin_recv,
    local_sem,
):
    me = lax.axis_index("expert")
    side = lax.axis_index("tensor")
    twin = me + 1 - 2 * lax.rem(me, 2)
    chips = experts // 2
    cols = small_ref.shape[2]
    width = win_ref.shape[1]
    barrier = pltpu.get_barrier_semaphore()
    greet_axis(barrier, "tensor", side, parts)
    greet(barrier, "expert", twin)
    for step in range(1, chips):
        greet(barrier, "expert", lax.rem(me + 2 * step, experts))
    pl.semaphore_wait(barrier, parts - 1 + chips)

    def places(index):
        lanes = pl.ds(pl.multiple_of(index * cols, cols), cols)
        hidden = pl.ds(pl.multiple_of(index * width, width), width)
        return (whole.at[:, me, :, lanes], win_full.at[:, hidden], wout_full.at[hidden, :])

    sources = (small_ref, win_ref, wout_ref)

    def side_copy(kind, step, owner, target):
        return send(
            sources[kind],
            places(owner)[kind],
            side_send.at[kind, step],
            side_recv.at[kind, step],
            "tensor",
            target,
        )

    for kind in range(3):
        for step in range(1, parts):
            side_copy(kind, step, side, lax.rem(side + step, parts)).start()
    for kind in range(3):
        pltpu.make_async_copy(sources[kind], places(side)[kind], local_sem.at[kind]).start()
    pltpu.make_async_copy(sources[0], places(side)[0], local_sem.at[0]).wait()
    for step in range(1, parts):
        side_copy(0, step, lax.rem(side + parts - step, parts), side).wait_recv()

    def chip_copy(step, owner, target):
        return send_chunk(whole.at[:, owner], whole.at[:, owner], chip_send, chip_recv, step, target)

    def twin_copy(step, owner):
        return send_chunk(whole.at[:, owner], whole.at[:, owner], twin_send, twin_recv, step, twin)

    for step in range(1, chips):
        chip_copy(step, me, lax.rem(me + 2 * step, experts)).start()
    twin_copy(0, me).start()
    for step in range(1, chips):
        owner = lax.rem(me + experts - 2 * step, experts)
        chip_copy(step, owner, owner).wait_recv()
        twin_copy(step, owner).start()
    for step in range(chips):
        twin_copy(step, lax.rem(twin + experts - 2 * step, experts)).wait_recv()
        twin_copy(step, lax.rem(me + experts - 2 * step, experts)).wait_send()
        if step:
            chip_copy(step, me, lax.rem(me + 2 * step, experts)).wait_send()
    for kind in range(3):
        for step in range(1, parts):
            one = side_copy(kind, step, lax.rem(side + parts - step, parts), side)
            one.wait_send()
            if kind:
                one.wait_recv()
    for kind in range(1, 3):
        pltpu.make_async_copy(sources[kind], places(side)[kind], local_sem.at[kind]).wait()


def gather_start(small, win, wout, experts, parts):
    count, rows, cols = small.shape
    depth, width = win.shape
    chips = experts // 2
    return pl.pallas_call(
        functools.partial(gather_kernel, experts, parts),
        out_shape=(
            jax.ShapeDtypeStruct((count, experts, rows, cols * parts), jnp.bfloat16),
            jax.ShapeDtypeStruct((depth, width * parts), jnp.bfloat16),
            jax.ShapeDtypeStruct((width * parts, depth), jnp.bfloat16),
        ),
        in_specs=whole_in_vmem(3),
        out_specs=tuple(whole_in_vmem(3)),
        scratch_shapes=[pltpu.SemaphoreType.DMA((3, parts))] * 2
        + [pltpu.SemaphoreType.DMA((chips,))] * 4
        + [pltpu.SemaphoreType.DMA((3,))],
        compiler_params=pltpu.CompilerParams(collective_id=3, has_side_effects=True),
    )(small, win, wout)


def exchange_chunks(peers, parts, work, out_rows, landed, results, back, sems, sum_up=None):
    out_send, out_recv, back_send, back_recv, side_send, side_recv = sems
    me = lax.axis_index("expert")
    side = lax.axis_index("tensor")
    share = back.shape[1] // parts
    barrier = pltpu.get_barrier_semaphore()
    greet_axis(barrier, "expert", me, peers)
    greet_axis(barrier, "tensor", side, parts)
    pl.semaphore_wait(barrier, peers + parts - 2)

    def share_of(index):
        return pl.ds(pl.multiple_of(index * share, 16), share)

    mine = share_of(side)

    def start_out(step, carry):
        peer = lax.rem(me + step, peers)
        send_chunk(out_rows.at[peer], landed.at[me], out_send, out_recv, step, peer).start()
        return carry

    lax.fori_loop(1, peers, start_out, 0)
    landed[me] = out_rows[me]

    def side_copy(shift, step, slab, owner, target):
        place = back.at[slab, share_of(owner)]
        return send(
            place, place, side_send.at[shift, step], side_recv.at[shift, step], "tensor", target
        )

    def pass_on(step):
        slab = lax.rem(me + step, peers)

        @pl.when(step > 0)
        def _():
            send_chunk(
                results.at[step], back.at[slab, mine], back_send, back_recv, step, slab
            ).wait_recv()

        for shift in range(1, parts):
            side_copy(shift, step, slab, side, lax.rem(side + shift, parts)).start()

    lag = 2

    def one_chunk(step, carry):
        peer = lax.rem(me + peers - step, peers)

        @pl.when(step > 0)
        def _():
            send_chunk(
                out_rows.at[peer], landed.at[peer], out_send, out_recv, step, peer
            ).wait_recv()

        work(step, peer, mine)

        @pl.when(step > 0)
        def _():
            send_chunk(
                results.at[step], back.at[me, mine], back_send, back_recv, step, peer
            ).start()

        @pl.when(step == 0)
        def _():
            back[me, mine] = results[0]

        @pl.when(step >= lag)
        def _():
            pass_on(step - lag)

        if sum_up is not None:
            sum_up(peer)
        return carry

    lax.fori_loop(0, peers, one_chunk, 0)

    def pass_last(step, carry):
        pass_on(step)
        return carry

    lax.fori_loop(peers - lag, peers, pass_last, 0)

    def finish(step, carry):
        ahead = lax.rem(me + step, peers)

        @pl.when(step > 0)
        def _():
            send_chunk(
                out_rows.at[ahead], landed.at[me], out_send, out_recv, step, ahead
            ).wait_send()
            send_chunk(
                results.at[step], back.at[me, mine], back_send, back_recv, step, ahead
            ).wait_send()

        for shift in range(1, parts):
            behind = lax.rem(side + parts - shift, parts)
            side_copy(shift, step, ahead, side, lax.rem(side + shift, parts)).wait_send()
            side_copy(shift, step, ahead, behind, behind).wait_recv()
        return carry

    lax.fori_loop(0, peers, finish, 0)


def forward_kernel(
    peers, parts, rows_ref, win_ref, wout_ref, landed, back, results, total, *sems
):
    width = win_ref.shape[1] // parts

    def work(step, peer, mine):
        chunk = landed[peer, mine]
        for part in range(parts):
            cols = slice(part * width, (part + 1) * width)
            before = jnp.dot(chunk, win_ref[:, cols], preferred_element_type=jnp.float32)
            hidden = gelu_exact(before).astype(jnp.bfloat16)
            term = jnp.dot(hidden, wout_ref[cols, :], preferred_element_type=jnp.float32)
            if part == 0:
                total[...] = term
            elif part < parts - 1:
                total[...] += term
            else:
                results[step] = (total[...] + term).astype(jnp.bfloat16)

    exchange_chunks(peers, parts, work, rows_ref, landed, results, back, sems)


def backward_kernel(
    peers,
    parts,
    rows_ref,
    arrived_ref,
    win_ref,
    wout_ref,
    back,
    win_grad,
    wout_grad,
    landed,
    results,
    total,
    *sems,
):
    width = win_ref.shape[1] // parts
    own = pl.ds(pl.multiple_of(lax.axis_index("tensor") * width, width), width)
    win_grad[...] = jnp.zeros_like(win_grad)
    wout_grad[...] = jnp.zeros_like(wout_grad)

    def hidden_pair(chunk, grad_chunk, cols):
        before = jnp.dot(chunk, win_ref[:, cols], preferred_element_type=jnp.float32)
        value, slope = gelu_parts(before)
        grad_before = contract_last(grad_chunk, wout_ref[cols, :]) * slope
        return value.astype(jnp.bfloat16), grad_before.astype(jnp.bfloat16)

    def work(step, peer, mine):
        chunk = arrived_ref[peer, mine]
        grad_chunk = landed[peer, mine]
        for part in range(parts):
            cols = slice(part * width, (part + 1) * width)
            grad_before = hidden_pair(chunk, grad_chunk, cols)[1]
            term = contract_last(grad_before, win_ref[:, cols])
            if part == 0:
                total[...] = term
            elif part < parts - 1:
                total[...] += term
            else:
                results[step] = (total[...] + term).astype(jnp.bfloat16)

    def sum_up(peer):
        chunk = arrived_ref[peer]
        grad_chunk = landed[peer]
        hidden, grad_before = hidden_pair(chunk, grad_chunk, own)
        wout_grad[...] += contract_rows(hidden, grad_chunk)
        win_grad[...] += contract_rows(chunk, grad_before)

    exchange_chunks(peers, parts, work, rows_ref, landed, results, back, sems, sum_up)


def whole_in_vmem(count):
    return [pl.BlockSpec(memory_space=pltpu.VMEM)] * count


def exchange_sems(peers, parts):
    return [pltpu.SemaphoreType.DMA((peers,))] * 4 + [pltpu.SemaphoreType.DMA((parts, peers))] * 2


def experts_forward(rows, win, wout, parts):
    peers, capacity, width = rows.shape
    like = jax.ShapeDtypeStruct(rows.shape, jnp.bfloat16)
    return pl.pallas_call(
        functools.partial(forward_kernel, peers, parts),
        out_shape=(like, like),
        in_specs=whole_in_vmem(3),
        out_specs=tuple(whole_in_vmem(2)),
        scratch_shapes=[
            pltpu.VMEM((peers, capacity // parts, width), jnp.bfloat16),
            pltpu.VMEM((capacity // parts, width), jnp.float32),
        ]
        + exchange_sems(peers, parts),
        compiler_params=pltpu.CompilerParams(collective_id=0, has_side_effects=True),
    )(rows, win, wout)


def experts_backward(rows, arrived, win, wout, parts):
    peers, capacity, width = rows.shape
    inner = win.shape[1]
    return pl.pallas_call(
        functools.partial(backward_kernel, peers, parts),
        out_shape=(
            jax.ShapeDtypeStruct(rows.shape, jnp.bfloat16),
            jax.ShapeDtypeStruct((width, inner // parts), jnp.float32),
            jax.ShapeDtypeStruct((inner // parts, width), jnp.float32),
        ),
        in_specs=whole_in_vmem(4),
        out_specs=tuple(whole_in_vmem(3)),
        scratch_shapes=[
            pltpu.VMEM(rows.shape, jnp.bfloat16),
            pltpu.VMEM((peers, capacity // parts, width), jnp.bfloat16),
            pltpu.VMEM((capacity // parts, width), jnp.float32),
        ]
        + exchange_sems(peers, parts),
        compiler_params=pltpu.CompilerParams(collective_id=1, has_side_effects=True),
    )(rows, arrived, win, wout)


def sum_kernel(peers, rows_ref, sum_ref, landed, sends, arrivals):
    me = lax.axis_index("expert")
    meet_peers(me, peers)

    def start_out(step, carry):
        peer = lax.rem(me + step, peers)
        send_chunk(rows_ref.at[peer], landed.at[me], sends, arrivals, step, peer).start()
        return carry

    lax.fori_loop(1, peers, start_out, 0)
    landed[me] = rows_ref[me]

    def finish(step, carry):
        peer = lax.rem(me + peers - step, peers)
        one = send_chunk(rows_ref.at[peer], landed.at[peer], sends, arrivals, step, peer)
        one.wait_send()
        one.wait_recv()
        return carry

    lax.fori_loop(1, peers, finish, 0)
    sum_ref[...] = landed[0].astype(jnp.float32)

    def add_one(source, carry):
        sum_ref[...] += landed[source].astype(jnp.float32)
        return carry

    lax.fori_loop(1, peers, add_one, 0)


def sum_shares(rows):
    peers = rows.shape[0]
    return pl.pallas_call(
        functools.partial(sum_kernel, peers),
        out_shape=jax.ShapeDtypeStruct(rows.shape[1:], jnp.float32),
        in_specs=whole_in_vmem(1),
        out_specs=whole_in_vmem(1)[0],
        scratch_shapes=[pltpu.VMEM(rows.shape, rows.dtype)] + [pltpu.SemaphoreType.DMA((peers,))] * 2,
        compiler_params=pltpu.CompilerParams(collective_id=2, has_side_effects=True),
    )(rows)


def norm_parts(rows_in):
    centred = rows_in - jnp.mean(rows_in, axis=-1, keepdims=True)
    inverse = lax.rsqrt(jnp.mean(centred * centred, axis=-1, keepdims=True) + 1e-06)
    return centred * inverse, inverse


def norm_back(unit, inverse, gain_row, grad_rows):
    scaled = grad_rows * gain_row
    inner = scaled - jnp.mean(scaled, axis=-1, keepdims=True)
    return inverse * (inner - unit * jnp.mean(scaled * unit, axis=-1, keepdims=True))


def two_heads(rows):
    low_half = lax.broadcasted_iota(jnp.int32, rows.shape, 1) < HEAD_DIM
    none = jnp.zeros_like(rows)
    return jnp.concatenate([jnp.where(low_half, rows, none), jnp.where(low_half, none, rows)], 0)


def join_heads(stacked):
    rows = stacked.shape[0] // 2
    low_half = lax.broadcasted_iota(jnp.int32, (rows, stacked.shape[1]), 1) < HEAD_DIM
    return jnp.where(low_half, stacked[:rows], stacked[rows:])


def pair_attention(query_two, key_pair):
    scores = contract_last(query_two, key_pair) * (HEAD_DIM ** (-0.5))
    real_key = lax.broadcasted_iota(jnp.int32, scores.shape, 1) < SEQ
    scores = jnp.where(real_key, scores, -jnp.inf)
    weights = jnp.exp(scores - jnp.max(scores, axis=-1, keepdims=True))
    return weights * (1.0 / jnp.sum(weights, axis=-1, keepdims=True))


def project_qkv(normed, mats_ref):
    return [
        jnp.dot(normed, mats_ref[part], preferred_element_type=jnp.float32).astype(jnp.bfloat16)
        for part in range(3)
    ]


def attend_kernel(
    experts, stream_ref, mats_ref, gains_ref, router_ref, middle_ref, normed_ref, probs_ref, mixed_ref
):
    rows = stream_ref[0]
    normed = (norm_parts(rows)[0] * gains_ref[0:1]).astype(jnp.bfloat16)
    query, keys, values = project_qkv(normed, mats_ref)
    for pair in range(query.shape[1] // (2 * HEAD_DIM)):
        cols = slice(pair * 2 * HEAD_DIM, (pair + 1) * 2 * HEAD_DIM)
        attention = pair_attention(two_heads(query[:, cols]), keys[:, cols]).astype(jnp.bfloat16)
        mixed = jnp.dot(attention, values[:, cols], preferred_element_type=jnp.float32)
        mixed_ref[0, :, cols] = join_heads(mixed).astype(jnp.bfloat16)
    middle = rows + contract_last(mixed_ref[0], mats_ref[3])
    middle_ref[0] = middle
    normed_two = (norm_parts(middle)[0] * gains_ref[1:2]).astype(jnp.bfloat16)
    normed_ref[0] = normed_two
    logits = jnp.dot(normed_two, router_ref[...], preferred_element_type=jnp.float32)
    real = lax.broadcasted_iota(jnp.int32, logits.shape, 1) < experts
    logits = jnp.where(real, logits, -jnp.inf)
    odds = jnp.exp(logits - jnp.max(logits, axis=-1, keepdims=True))
    probs_ref[0] = odds * (1.0 / jnp.sum(odds, axis=-1, keepdims=True))


def attend_back_kernel(
    own_ref,
    upstream_ref,
    grad_ref,
    grad_logits_ref,
    stream_ref,
    middle_ref,
    mixed_ref,
    mats_ref,
    gains_ref,
    router_ref,
    down_ref,
    mats_grad,
    router_grad,
    gains_grad,
    triple,
):
    @pl.when(pl.program_id(0) == 0)
    def _():
        mats_grad[...] = jnp.zeros_like(mats_grad)
        router_grad[...] = jnp.zeros_like(router_grad)
        gains_grad[...] = jnp.zeros_like(gains_grad)

    head_cols = mats_grad.shape[2]
    mine = pl.ds(pl.multiple_of(own_ref[0] * head_cols, head_cols), head_cols)
    gain_one, gain_two = gains_ref[0:1], gains_ref[1:2]
    unit_two, inverse_two = norm_parts(middle_ref[0])
    grad_logits = grad_logits_ref[0]
    router_grad[...] += contract_rows(
        grad_logits, (unit_two * gain_two).astype(jnp.bfloat16)
    )
    grad_normed = grad_ref[0] + contract_last(grad_logits, router_ref[...])
    gains_grad[1:2] += jnp.sum(grad_normed * unit_two, axis=0, keepdims=True)
    grad_middle = upstream_ref[0] + norm_back(unit_two, inverse_two, gain_two, grad_normed)
    grad_branch = grad_middle.astype(jnp.bfloat16)
    mats_grad[3] += contract_rows(grad_branch, mixed_ref[0, :, mine])
    grad_mixed = jnp.dot(
        grad_branch, mats_ref[3], preferred_element_type=jnp.float32
    ).astype(jnp.bfloat16)
    unit_one, inverse_one = norm_parts(stream_ref[0])
    normed = (unit_one * gain_one).astype(jnp.bfloat16)
    query, keys, values = project_qkv(normed, mats_ref)
    scale = HEAD_DIM ** (-0.5)
    for pair in range(query.shape[1] // (2 * HEAD_DIM)):
        cols = slice(pair * 2 * HEAD_DIM, (pair + 1) * 2 * HEAD_DIM)
        query_two = two_heads(query[:, cols])
        attention = pair_attention(query_two, keys[:, cols])
        grad_two = two_heads(grad_mixed[:, cols])
        triple[2, :, cols] = contract_rows(attention.astype(jnp.bfloat16), grad_two).astype(
            jnp.bfloat16
        )
        grad_attention = contract_last(grad_two, values[:, cols])
        grad_scores = (
            attention
            * (grad_attention - jnp.sum(attention * grad_attention, axis=-1, keepdims=True))
        ).astype(jnp.bfloat16)
        grad_query = jnp.dot(grad_scores, keys[:, cols], preferred_element_type=jnp.float32)
        triple[0, :, cols] = (join_heads(grad_query) * scale).astype(jnp.bfloat16)
        triple[1, :, cols] = (contract_rows(grad_scores, query_two) * scale).astype(jnp.bfloat16)
    grad_one = contract_last(triple[0], mats_ref[0])
    for part in range(3):
        if part:
            grad_one += contract_last(triple[part], mats_ref[part])
        mats_grad[part] += contract_rows(normed, triple[part, :, mine])
    gains_grad[0:1] += jnp.sum(grad_one * unit_one, axis=0, keepdims=True)
    down_ref[0] = grad_middle + norm_back(unit_one, inverse_one, gain_one, grad_one)


def image_spec(array):
    return pl.BlockSpec((1,) + array.shape[1:], lambda image: (image, 0, 0))


def fixed_spec(array):
    return pl.BlockSpec(array.shape, lambda image: (0,) * len(array.shape))


def attend(stream, mats, gains, router, experts):
    images, rows, width = stream.shape
    outs = (
        jax.ShapeDtypeStruct(stream.shape, jnp.float32),
        jax.ShapeDtypeStruct(stream.shape, jnp.bfloat16),
        jax.ShapeDtypeStruct((images, rows, router.shape[1]), jnp.float32),
        jax.ShapeDtypeStruct((images, rows, mats.shape[2]), jnp.bfloat16),
    )
    return pl.pallas_call(
        functools.partial(attend_kernel, experts),
        grid=(images,),
        out_shape=outs,
        in_specs=[image_spec(stream), fixed_spec(mats), fixed_spec(gains), fixed_spec(router)],
        out_specs=tuple(image_spec(one) for one in outs),
    )(stream, mats, gains, router)


def attend_back(upstream, grad_normed, grad_logits, stream, middle, mixed, mats, gains, router, head_cols):
    images, rows, width = stream.shape
    own = lax.axis_index("tensor").astype(jnp.int32).reshape(1)
    sums = (
        jax.ShapeDtypeStruct((4, width, head_cols), jnp.float32),
        jax.ShapeDtypeStruct((router.shape[1], width), jnp.float32),
        jax.ShapeDtypeStruct(gains.shape, jnp.float32),
    )
    per_image = [upstream, grad_normed, grad_logits, stream, middle, mixed]
    fixed = [mats, gains, router]
    return pl.pallas_call(
        attend_back_kernel,
        grid=(images,),
        out_shape=(jax.ShapeDtypeStruct(stream.shape, jnp.float32),) + sums,
        in_specs=[pl.BlockSpec(memory_space=pltpu.SMEM)]
        + [image_spec(one) for one in per_image]
        + [fixed_spec(one) for one in fixed],
        out_specs=(image_spec(stream),) + tuple(fixed_spec(one) for one in sums),
        scratch_shapes=[pltpu.VMEM((3, rows, mats.shape[2]), jnp.bfloat16)],
    )(own, *per_image, *fixed)


def slot_plan(chosen, rank_rows, experts, capacity, spacing):
    columns = lax.broadcasted_iota(jnp.int32, (1, experts), 1)
    first_hot = (chosen[:, 0:1] == columns).astype(jnp.bfloat16)
    second = (chosen[:, 1:2] == columns).astype(jnp.bfloat16)
    earlier = (rank_rows[None, :] < rank_rows[:, None]).astype(jnp.bfloat16)
    count_first = jnp.dot(earlier, first_hot, preferred_element_type=jnp.float32)
    count_second = jnp.dot(earlier, second, preferred_element_type=jnp.float32)
    first_f = first_hot.astype(jnp.float32)
    second_f = second.astype(jnp.float32)
    filled = jnp.sum(first_f, axis=0, keepdims=True)
    slot_first = jnp.sum(count_first * first_f, axis=1)
    slot_second = jnp.sum((filled + count_second) * second_f, axis=1)
    slot_nums = jnp.stack([slot_first, slot_second], axis=1).astype(jnp.int32)
    target = jnp.where(slot_nums < capacity, chosen * spacing + slot_nums, experts * spacing)
    return (target, first_f, second_f)


def local(
    inputs,
    cotangent,
    routes,
    priority,
    attend_in,
    attend_out,
    router,
    norm_gains,
    expert_in,
    expert_out,
):
    experts = lax.axis_size("expert")
    tokens = inputs.shape[0]
    model_width = inputs.shape[1]
    images = tokens // SEQ
    head_cols = attend_in.shape[3]
    layers = attend_in.shape[0]
    capacity = max(2, (10 * tokens + 4 * experts - 1) // (4 * experts))
    peers_tensor = lax.axis_size("tensor")
    spacing = -(-capacity // (16 * peers_tensor)) * 16 * peers_tensor
    slots_all = experts * spacing
    row_share = attend_in.shape[2]
    gain_share = norm_gains.shape[2]
    image_rows = -(-SEQ // 16) * 16
    tokens_all = images * image_rows

    def spread(rows, fill):
        shaped = rows.reshape((images, SEQ) + rows.shape[1:])
        edges = ((0, 0), (0, image_rows - SEQ)) + ((0, 0),) * (rows.ndim - 1)
        return jnp.pad(shaped, edges, constant_values=fill)

    def gather_tensor(rows, axis):
        return lax.all_gather(rows.astype(jnp.bfloat16), "tensor", axis=axis, tiled=True)

    smalls = jnp.concatenate([router.reshape(-1), norm_gains.reshape(-1)])
    block = row_share * head_cols
    smalls = jnp.pad(smalls, (0, -smalls.shape[0] % block)).reshape(-1, row_share, head_cols)
    packed = jnp.concatenate(
        [
            jnp.concatenate([attend_in, attend_out.transpose(0, 2, 1)[:, None]], axis=1).reshape(
                -1, row_share, head_cols
            ),
            smalls,
        ]
    )
    whole, win_first, wout_first = gather_start(
        packed.astype(jnp.bfloat16),
        expert_in[0, 0].astype(jnp.bfloat16),
        expert_out[0, 0].astype(jnp.bfloat16),
        experts,
        peers_tensor,
    )
    whole = whole.reshape(whole.shape[0], model_width, model_width)
    later_in, later_out, whole = lax.optimization_barrier(
        (expert_in[1:, 0], expert_out[1:, 0], whole)
    )
    small_rows = whole[4 * layers :, :, :head_cols].reshape(-1, experts, block)
    small_rows = small_rows.transpose(1, 0, 2).reshape(experts, -1)
    router_all = small_rows[:, : layers * model_width].reshape(experts, layers, model_width)
    gains_all = small_rows[:, layers * model_width :][:, : layers * 2 * gain_share]
    gains_all = gains_all.reshape(experts, layers, 2, gain_share).transpose(1, 2, 0, 3)
    gains_all = gains_all.reshape(layers, 2, model_width).astype(jnp.float32)
    router_all = jnp.pad(router_all.transpose(1, 2, 0), ((0, 0), (0, 0), (0, -experts % 128)))
    win_full, wout_full = [win_first], [wout_first]
    for layer_index in range(layers - 1):
        win_full.append(gather_tensor(later_in[layer_index], 1))
        wout_full.append(gather_tensor(later_out[layer_index], 0))
    slot_ids = lax.broadcasted_iota(jnp.int32, (1, slots_all), 1)
    stream = spread(inputs, 0)
    stash_list = []
    for layer_index in range(layers):
        mats = whole[4 * layer_index : 4 * layer_index + 4]
        gains_now = gains_all[layer_index]
        router_now = router_all[layer_index]
        middle, normed_two, probs_all, mixed_heads = attend(
            stream, mats, gains_now, router_now, experts
        )
        probs_all = probs_all.reshape(tokens_all, -1)[:, :experts]
        chosen = spread(routes[layer_index], -1).reshape(tokens_all, 2)
        ranks = spread(priority[layer_index], tokens).reshape(tokens_all)
        target, first_f, second_f = slot_plan(chosen, ranks, experts, capacity, spacing)
        gate_values = jnp.stack(
            [jnp.sum(probs_all * first_f, axis=1), jnp.sum(probs_all * second_f, axis=1)], axis=1
        )
        pick_first = (target[:, 0:1] == slot_ids).astype(jnp.bfloat16)
        pick_second = (target[:, 1:2] == slot_ids).astype(jnp.bfloat16)
        pick_both = pick_first + pick_second
        dispatched = contract_rows(pick_both, normed_two.reshape(tokens_all, model_width))
        arrived, returned = experts_forward(
            dispatched.astype(jnp.bfloat16).reshape(experts, spacing, model_width),
            win_full[layer_index],
            wout_full[layer_index],
            peers_tensor,
        )
        returned = returned.reshape(slots_all, model_width)
        rows_first = jnp.dot(pick_first, returned, preferred_element_type=jnp.float32)
        rows_second = jnp.dot(pick_second, returned, preferred_element_type=jnp.float32)
        output = (
            middle.reshape(tokens_all, model_width)
            + gate_values[:, 0:1] * rows_first
            + gate_values[:, 1:2] * rows_second
        )
        stash_list.append(
            (
                stream,
                mats,
                gains_now,
                router_now,
                mixed_heads,
                middle,
                probs_all,
                gate_values,
                first_f,
                second_f,
                pick_first,
                pick_second,
                pick_both,
                arrived,
                rows_first,
                rows_second,
            )
        )
        stream = output.reshape(images, image_rows, model_width)
    upstream = spread(cotangent, 0).reshape(tokens_all, model_width)
    grads_in, grads_out, grads_router, grads_gain, grads_win, grads_wout = ([], [], [], [], [], [])
    grads_shared = []
    for layer_index in reversed(range(layers)):
        (
            stream_in,
            mats,
            gains_now,
            router_now,
            mixed_heads,
            middle,
            probs_all,
            gate_values,
            first_f,
            second_f,
            pick_first,
            pick_second,
            pick_both,
            arrived,
            rows_first,
            rows_second,
        ) = stash_list[layer_index]
        gate_first = jnp.sum(upstream * rows_first, axis=1)
        gate_second = jnp.sum(upstream * rows_second, axis=1)
        scaled_first = (gate_values[:, 0:1] * upstream).astype(jnp.bfloat16)
        scaled_second = (gate_values[:, 1:2] * upstream).astype(jnp.bfloat16)
        grad_slots = (
            contract_rows(pick_first, scaled_first) + contract_rows(pick_second, scaled_second)
        ).astype(jnp.bfloat16)
        grad_dispatched, win_grad, wout_grad = experts_backward(
            grad_slots.reshape(experts, spacing, model_width),
            arrived,
            win_full[layer_index],
            wout_full[layer_index],
            peers_tensor,
        )
        grads_win.append(win_grad)
        grads_wout.append(wout_grad)
        grad_dispatched = grad_dispatched.reshape(slots_all, model_width)
        grad_normed = jnp.dot(pick_both, grad_dispatched, preferred_element_type=jnp.float32)
        grad_probs = first_f * gate_first[:, None] + second_f * gate_second[:, None]
        grad_logits = (
            probs_all * (grad_probs - jnp.sum(probs_all * grad_probs, axis=1, keepdims=True))
        ).astype(jnp.bfloat16)
        grad_logits = jnp.pad(grad_logits, ((0, 0), (0, router_now.shape[1] - experts)))
        shape = stream_in.shape
        down, mats_grad, router_grad, gain_grad = attend_back(
            upstream.reshape(shape),
            grad_normed.reshape(shape),
            grad_logits.reshape(images, image_rows, -1),
            stream_in,
            middle,
            mixed_heads,
            mats,
            gains_now,
            router_now,
            head_cols,
        )
        mats_grad = mats_grad.reshape(4, experts, row_share, head_cols).transpose(1, 0, 2, 3)
        router_grad = router_grad[:experts]
        gain_grad = gain_grad.reshape(2, experts, gain_share)
        smalls = jnp.concatenate(
            [router_grad, gain_grad.transpose(1, 0, 2).reshape(experts, -1)], axis=1
        )
        smalls = jnp.pad(smalls, ((0, 0), (0, -smalls.shape[1] % 2048)))
        grads_shared.append(
            jnp.concatenate(
                [mats_grad.reshape(experts, -1, 128), smalls.reshape(experts, -1, 128)], axis=1
            ).astype(jnp.bfloat16)
        )
        upstream = down.reshape(tokens_all, model_width)
    total_rows = grads_shared[0].shape[1]
    mat_rows = 4 * row_share * head_cols // 128
    shared_all = sum_shares(jnp.concatenate(grads_shared, axis=1))
    for order in range(layers):
        shared = shared_all[order * total_rows : (order + 1) * total_rows]
        mats_own = shared[:mat_rows].reshape(4, row_share, head_cols)
        small_own = shared[mat_rows:].reshape(-1)
        grads_in.append(mats_own[:3])
        grads_out.append(mats_own[3].T)
        grads_router.append(small_own[:model_width, None])
        grads_gain.append(
            small_own[model_width : model_width + 2 * gain_share].reshape(2, gain_share)
        )
    win_grad_all = jnp.stack(grads_win[::-1])[:, None]
    wout_grad_all = jnp.stack(grads_wout[::-1])[:, None]
    return (
        stream[:, :SEQ].reshape(tokens, model_width),
        upstream.reshape(stream.shape)[:, :SEQ].reshape(tokens, model_width),
        jnp.stack(grads_in[::-1]),
        jnp.stack(grads_out[::-1]),
        jnp.stack(grads_router[::-1]),
        jnp.stack(grads_gain[::-1]),
        win_grad_all,
        wout_grad_all,
    )


def solution(mesh):
    placed = (
        P("expert", None),
        P("expert", None),
        P(None, "expert", None),
        P(None, "expert"),
        P(None, None, "expert", "tensor"),
        P(None, "tensor", "expert"),
        P(None, None, "expert"),
        P(None, None, "expert"),
        P(None, "expert", None, "tensor"),
        P(None, "expert", "tensor", None),
    )
    return jax.shard_map(
        local,
        mesh=mesh,
        in_specs=placed,
        out_specs=(
            P("expert", None),
            P("expert", None),
            P(None, None, "expert", "tensor"),
            P(None, "tensor", "expert"),
            P(None, None, "expert"),
            P(None, None, "expert"),
            P(None, "expert", None, "tensor"),
            P(None, "expert", "tensor", None),
        ),
        check_vma=False,
    )
```

```python
import functools

import jax
import jax.numpy as jnp
from jax import lax
from jax.experimental import pallas as pl
from jax.experimental.pallas import tpu as pltpu
from jax.sharding import PartitionSpec as P

HEAD_DIM = 64
SEQ = 197


def gelu_exact(rows_in):
    return 0.5 * rows_in * (1.0 + lax.erf(rows_in * 0.7071067811865476))


def contract_rows(left_side, right_side):
    return lax.dot_general(
        left_side, right_side, (((0,), (0,)), ((), ())), preferred_element_type=jnp.float32
    )


def contract_last(left_side, right_side):
    return lax.dot_general(
        left_side, right_side, (((1,), (1,)), ((), ())), preferred_element_type=jnp.float32
    )


def gelu_parts(rows_in):
    half = 0.5 * (1.0 + lax.erf(rows_in * 0.7071067811865476))
    slope = half + rows_in * (jnp.exp(-0.5 * rows_in * rows_in) * 0.3989422804014327)
    return rows_in * half, slope


def greet(barrier, axis, index):
    pl.semaphore_signal(
        barrier, inc=1, device_id={axis: index}, device_id_type=pl.DeviceIdType.MESH
    )


def greet_axis(barrier, axis, me, peers):
    def one(step, carry):
        greet(barrier, axis, lax.rem(me + step, peers))
        return carry

    lax.fori_loop(1, peers, one, 0)


def send(source, landing, send_sem, recv_sem, axis, index):
    return pltpu.make_async_remote_copy(
        src_ref=source,
        dst_ref=landing,
        send_sem=send_sem,
        recv_sem=recv_sem,
        device_id={axis: index},
        device_id_type=pl.DeviceIdType.MESH,
    )


def send_chunk(source, landing, sends, arrivals, step, peer):
    return send(source, landing, sends.at[step], arrivals.at[step], "expert", peer)


def meet_peers(me, peers):
    barrier = pltpu.get_barrier_semaphore()
    greet_axis(barrier, "expert", me, peers)
    pl.semaphore_wait(barrier, peers - 1)


class Ring:
    def __init__(self, parts, place, own, sends, arrivals, both=True):
        self.parts, self.place, self.own = parts, place, own
        self.sends, self.arrivals = sends, arrivals
        self.side = lax.axis_index("tensor")
        self.hops = []
        for distance in range(1, parts // 2 + 1):
            if 2 * distance < parts:
                self.hops += [(distance, 1, None), (distance, -1, None)]
            elif both:
                self.hops += [(distance, 1, 0), (distance, -1, 1)]
            else:
                self.hops += [(distance, 1, None)]

    def wrap(self, index):
        return lax.rem(self.side + self.parts + index, self.parts)

    def outgoing(self, number):
        distance, way, half = self.hops[number]
        landing = self.place(self.wrap(-way * (distance - 1)), half)
        source = landing if distance > 1 else self.own(half)
        return send(
            source,
            landing,
            self.sends(number),
            self.arrivals(number),
            "tensor",
            self.wrap(way),
        )

    def incoming(self, number):
        distance, way, half = self.hops[number]
        landing = self.place(self.wrap(-way * distance), half)
        return send(
            landing,
            landing,
            self.sends(number),
            self.arrivals(number),
            "tensor",
            self.wrap(way),
        )

    def stage(self, wanted):
        for number, (distance, way, _) in enumerate(self.hops):
            if distance == wanted:
                for earlier, (before, same, _) in enumerate(self.hops):
                    if before == distance - 1 and same == way:
                        self.incoming(earlier).wait_recv()
                self.outgoing(number).start()

    def finish(self):
        kept = {(distance, way) for distance, way, _ in self.hops}
        for number, (distance, way, _) in enumerate(self.hops):
            self.outgoing(number).wait_send()
            if (distance + 1, way) not in kept:
                self.incoming(number).wait_recv()


def weight_rings(parts, sources, targets, sends, arrivals):
    def ring_of(kind):
        source, target = sources[kind], targets[kind]
        length = source.shape[1 - kind]

        def cut(ref, start, half):
            size = length if half is None else length // 2
            start = start + (0 if half is None else half * size)
            span = pl.ds(pl.multiple_of(start, size), size)
            return ref.at[:, span] if kind == 0 else ref.at[span, :]

        return Ring(
            parts,
            lambda owner, half: cut(target, owner * length, half),
            lambda half: cut(source, 0, half),
            lambda number: sends.at[kind, number],
            lambda number: arrivals.at[kind, number],
        )

    return [ring_of(kind) for kind in range(2)]


def own_weights(sources, targets, local_sem):
    side = lax.axis_index("tensor")
    copies = []
    for kind in range(2):
        length = sources[kind].shape[1 - kind]
        span = pl.ds(pl.multiple_of(side * length, length), length)
        target = targets[kind].at[:, span] if kind == 0 else targets[kind].at[span, :]
        copies.append(pltpu.make_async_copy(sources[kind], target, local_sem.at[kind]))
    return copies


def gather_kernel(
    experts,
    parts,
    small_ref,
    win_ref,
    wout_ref,
    whole,
    win_full,
    wout_full,
    side_send,
    side_recv,
    ring_send,
    ring_recv,
    chip_send,
    chip_recv,
    twin_send,
    twin_recv,
    local_sem,
):
    me = lax.axis_index("expert")
    side = lax.axis_index("tensor")
    twin = me + 1 - 2 * lax.rem(me, 2)
    chips = experts // 2
    cols = small_ref.shape[2]
    barrier = pltpu.get_barrier_semaphore()
    greet_axis(barrier, "tensor", side, parts)
    greet(barrier, "expert", twin)
    for step in range(1, chips):
        greet(barrier, "expert", lax.rem(me + 2 * step, experts))
    pl.semaphore_wait(barrier, parts - 1 + chips)

    def place(index):
        return whole.at[:, me, :, pl.ds(pl.multiple_of(index * cols, cols), cols)]

    def side_copy(step, owner, target):
        return send(
            small_ref, place(owner), side_send.at[step], side_recv.at[step], "tensor", target
        )

    for step in range(1, parts):
        side_copy(step, side, lax.rem(side + step, parts)).start()
    rings = weight_rings(parts, (win_ref, wout_ref), (win_full, wout_full), ring_send, ring_recv)
    for ring in rings:
        ring.stage(1)
    copies = own_weights((win_ref, wout_ref), (win_full, wout_full), local_sem)
    copies.append(pltpu.make_async_copy(small_ref, place(side), local_sem.at[2]))
    for copy in copies:
        copy.start()
    copies[2].wait()
    for step in range(1, parts):
        side_copy(step, lax.rem(side + parts - step, parts), side).wait_recv()

    def chip_copy(step, owner, target):
        return send_chunk(whole.at[:, owner], whole.at[:, owner], chip_send, chip_recv, step, target)

    def twin_copy(step, owner):
        return send_chunk(whole.at[:, owner], whole.at[:, owner], twin_send, twin_recv, step, twin)

    for step in range(1, chips):
        chip_copy(step, me, lax.rem(me + 2 * step, experts)).start()
    twin_copy(0, me).start()
    for distance in range(2, parts // 2 + 1):
        for ring in rings:
            ring.stage(distance)
    for step in range(1, chips):
        owner = lax.rem(me + experts - 2 * step, experts)
        chip_copy(step, owner, owner).wait_recv()
        twin_copy(step, owner).start()
    for step in range(chips):
        twin_copy(step, lax.rem(twin + experts - 2 * step, experts)).wait_recv()
        twin_copy(step, lax.rem(me + experts - 2 * step, experts)).wait_send()
        if step:
            chip_copy(step, me, lax.rem(me + 2 * step, experts)).wait_send()
    for step in range(1, parts):
        side_copy(step, side, lax.rem(side + step, parts)).wait_send()
    for ring in rings:
        ring.finish()
    for copy in copies[:2]:
        copy.wait()


def gather_start(small, win, wout, experts, parts):
    count, rows, cols = small.shape
    depth, width = win.shape
    chips = experts // 2
    return pl.pallas_call(
        functools.partial(gather_kernel, experts, parts),
        out_shape=(
            jax.ShapeDtypeStruct((count, experts, rows, cols * parts), jnp.bfloat16),
            jax.ShapeDtypeStruct((depth, width * parts), jnp.bfloat16),
            jax.ShapeDtypeStruct((width * parts, depth), jnp.bfloat16),
        ),
        in_specs=whole_in_vmem(3),
        out_specs=tuple(whole_in_vmem(3)),
        scratch_shapes=[pltpu.SemaphoreType.DMA((parts,))] * 2
        + [pltpu.SemaphoreType.DMA((2, parts))] * 2
        + [pltpu.SemaphoreType.DMA((chips,))] * 4
        + [pltpu.SemaphoreType.DMA((3,))],
        compiler_params=pltpu.CompilerParams(collective_id=3, has_side_effects=True),
    )(small, win, wout)


def exchange_chunks(
    peers, parts, work, out_rows, landed, results, back, sems, sum_up=None, rings=()
):
    out_send, out_recv, back_send, back_recv, side_send, side_recv = sems
    me = lax.axis_index("expert")
    side = lax.axis_index("tensor")
    share = back.shape[1] // parts
    barrier = pltpu.get_barrier_semaphore()
    greet_axis(barrier, "expert", me, peers)
    greet_axis(barrier, "tensor", side, parts)
    pl.semaphore_wait(barrier, peers + parts - 2)

    def share_of(index):
        return pl.ds(pl.multiple_of(index * share, 16), share)

    mine = share_of(side)

    def start_out(step, carry):
        peer = lax.rem(me + step, peers)
        send_chunk(out_rows.at[peer], landed.at[me], out_send, out_recv, step, peer).start()
        return carry

    lax.fori_loop(1, peers, start_out, 0)
    for ring in rings:
        ring.stage(1)
    landed[me] = out_rows[me]

    first = -(-share // 32) * 16
    distances = range(1, parts // 2 + 1)

    def chunk_ring(step):
        slab = lax.rem(me + step, peers)

        def place(owner, half):
            start = owner * share + (first if half == 1 else 0)
            size = share if half is None else (share - first if half else first)
            return back.at[slab, pl.ds(pl.multiple_of(start, 16), size)]

        return Ring(
            parts,
            place,
            lambda half: place(side, half),
            lambda number: side_send.at[number, step],
            lambda number: side_recv.at[number, step],
            both=first < share,
        )

    def pass_on(step, distance):
        if distance == 1:
            slab = lax.rem(me + step, peers)

            @pl.when(step > 0)
            def _():
                send_chunk(
                    results.at[step], back.at[slab, mine], back_send, back_recv, step, slab
                ).wait_recv()

        chunk_ring(step).stage(distance)

    lag = 2

    def one_chunk(step, carry):
        peer = lax.rem(me + peers - step, peers)

        @pl.when(step > 0)
        def _():
            send_chunk(
                out_rows.at[peer], landed.at[peer], out_send, out_recv, step, peer
            ).wait_recv()

        work(step, peer, mine)

        @pl.when(step > 0)
        def _():
            send_chunk(
                results.at[step], back.at[me, mine], back_send, back_recv, step, peer
            ).start()

        @pl.when(step == 0)
        def _():
            back[me, mine] = results[0]

        for distance in distances:

            @pl.when(step >= lag * distance)
            def _(distance=distance):
                pass_on(step - lag * distance, distance)

        if rings:

            @pl.when(step == peers // 2)
            def _():
                for distance in distances[1:]:
                    for ring in rings:
                        ring.stage(distance)

        if sum_up is not None:
            sum_up(peer)
        return carry

    lax.fori_loop(0, peers, one_chunk, 0)

    for distance in distances:

        def pass_last(step, carry, distance=distance):
            pass_on(step, distance)
            return carry

        lax.fori_loop(max(0, peers - lag * distance), peers, pass_last, 0)

    def finish(step, carry):
        ahead = lax.rem(me + step, peers)

        @pl.when(step > 0)
        def _():
            send_chunk(
                out_rows.at[ahead], landed.at[me], out_send, out_recv, step, ahead
            ).wait_send()
            send_chunk(
                results.at[step], back.at[me, mine], back_send, back_recv, step, ahead
            ).wait_send()

        chunk_ring(step).finish()
        return carry

    lax.fori_loop(0, peers, finish, 0)
    for ring in rings:
        ring.finish()


def forward_kernel(peers, parts, follow, *refs):
    rows_ref, win_ref, wout_ref = refs[:3]
    sources = refs[3 : 3 + follow]
    landed, back = refs[3 + follow : 5 + follow]
    targets = refs[5 + follow : 5 + 2 * follow]
    results, total, *sems = refs[5 + 2 * follow :]
    rings, copies = (), ()
    if follow:
        rings = weight_rings(parts, sources, targets, sems[6], sems[7])
        copies = own_weights(sources, targets, sems[8])
        for copy in copies:
            copy.start()
    width = win_ref.shape[1] // parts

    def work(step, peer, mine):
        chunk = landed[peer, mine]
        for part in range(parts):
            cols = slice(part * width, (part + 1) * width)
            before = jnp.dot(chunk, win_ref[:, cols], preferred_element_type=jnp.float32)
            hidden = gelu_exact(before).astype(jnp.bfloat16)
            term = jnp.dot(hidden, wout_ref[cols, :], preferred_element_type=jnp.float32)
            if part == 0:
                total[...] = term
            elif part < parts - 1:
                total[...] += term
            else:
                results[step] = (total[...] + term).astype(jnp.bfloat16)

    exchange_chunks(
        peers, parts, work, rows_ref, landed, results, back, sems[:6], rings=rings
    )
    for copy in copies:
        copy.wait()


def backward_kernel(
    peers,
    parts,
    rows_ref,
    arrived_ref,
    win_ref,
    wout_ref,
    back,
    win_grad,
    wout_grad,
    landed,
    results,
    total,
    *sems,
):
    width = win_ref.shape[1] // parts
    own = pl.ds(pl.multiple_of(lax.axis_index("tensor") * width, width), width)
    win_grad[...] = jnp.zeros_like(win_grad)
    wout_grad[...] = jnp.zeros_like(wout_grad)

    def hidden_pair(chunk, grad_chunk, cols):
        before = jnp.dot(chunk, win_ref[:, cols], preferred_element_type=jnp.float32)
        value, slope = gelu_parts(before)
        grad_before = contract_last(grad_chunk, wout_ref[cols, :]) * slope
        return value.astype(jnp.bfloat16), grad_before.astype(jnp.bfloat16)

    def work(step, peer, mine):
        chunk = arrived_ref[peer, mine]
        grad_chunk = landed[peer, mine]
        for part in range(parts):
            cols = slice(part * width, (part + 1) * width)
            grad_before = hidden_pair(chunk, grad_chunk, cols)[1]
            term = contract_last(grad_before, win_ref[:, cols])
            if part == 0:
                total[...] = term
            elif part < parts - 1:
                total[...] += term
            else:
                results[step] = (total[...] + term).astype(jnp.bfloat16)

    def sum_up(peer):
        chunk = arrived_ref[peer]
        grad_chunk = landed[peer]
        hidden, grad_before = hidden_pair(chunk, grad_chunk, own)
        wout_grad[...] += contract_rows(hidden, grad_chunk)
        win_grad[...] += contract_rows(chunk, grad_before)

    exchange_chunks(peers, parts, work, rows_ref, landed, results, back, sems, sum_up)


def whole_in_vmem(count):
    return [pl.BlockSpec(memory_space=pltpu.VMEM)] * count


def exchange_sems(peers, parts):
    return [pltpu.SemaphoreType.DMA((peers,))] * 4 + [pltpu.SemaphoreType.DMA((parts, peers))] * 2


def experts_forward(rows, win, wout, parts, following=()):
    peers, capacity, width = rows.shape
    like = jax.ShapeDtypeStruct(rows.shape, jnp.bfloat16)
    follow = len(following)
    wholes = (win, wout)[:follow]
    return pl.pallas_call(
        functools.partial(forward_kernel, peers, parts, follow),
        out_shape=(like, like) + tuple(jax.ShapeDtypeStruct(w.shape, w.dtype) for w in wholes),
        in_specs=whole_in_vmem(3 + follow),
        out_specs=tuple(whole_in_vmem(2 + follow)),
        scratch_shapes=[
            pltpu.VMEM((peers, capacity // parts, width), jnp.bfloat16),
            pltpu.VMEM((capacity // parts, width), jnp.float32),
        ]
        + exchange_sems(peers, parts)
        + [pltpu.SemaphoreType.DMA((2, parts))] * follow
        + [pltpu.SemaphoreType.DMA((2,))] * (follow // 2),
        compiler_params=pltpu.CompilerParams(
            collective_id=4 if follow else 0, has_side_effects=True
        ),
    )(rows, win, wout, *following)


def experts_backward(rows, arrived, win, wout, parts):
    peers, capacity, width = rows.shape
    inner = win.shape[1]
    return pl.pallas_call(
        functools.partial(backward_kernel, peers, parts),
        out_shape=(
            jax.ShapeDtypeStruct(rows.shape, jnp.bfloat16),
            jax.ShapeDtypeStruct((width, inner // parts), jnp.float32),
            jax.ShapeDtypeStruct((inner // parts, width), jnp.float32),
        ),
        in_specs=whole_in_vmem(4),
        out_specs=tuple(whole_in_vmem(3)),
        scratch_shapes=[
            pltpu.VMEM(rows.shape, jnp.bfloat16),
            pltpu.VMEM((peers, capacity // parts, width), jnp.bfloat16),
            pltpu.VMEM((capacity // parts, width), jnp.float32),
        ]
        + exchange_sems(peers, parts),
        compiler_params=pltpu.CompilerParams(collective_id=1, has_side_effects=True),
    )(rows, arrived, win, wout)


def sum_kernel(peers, rows_ref, sum_ref, landed, sends, arrivals):
    me = lax.axis_index("expert")
    meet_peers(me, peers)

    def start_out(step, carry):
        peer = lax.rem(me + step, peers)
        send_chunk(rows_ref.at[peer], landed.at[me], sends, arrivals, step, peer).start()
        return carry

    lax.fori_loop(1, peers, start_out, 0)
    landed[me] = rows_ref[me]

    def finish(step, carry):
        peer = lax.rem(me + peers - step, peers)
        one = send_chunk(rows_ref.at[peer], landed.at[peer], sends, arrivals, step, peer)
        one.wait_send()
        one.wait_recv()
        return carry

    lax.fori_loop(1, peers, finish, 0)
    sum_ref[...] = landed[0].astype(jnp.float32)

    def add_one(source, carry):
        sum_ref[...] += landed[source].astype(jnp.float32)
        return carry

    lax.fori_loop(1, peers, add_one, 0)


def sum_shares(rows):
    peers = rows.shape[0]
    return pl.pallas_call(
        functools.partial(sum_kernel, peers),
        out_shape=jax.ShapeDtypeStruct(rows.shape[1:], jnp.float32),
        in_specs=whole_in_vmem(1),
        out_specs=whole_in_vmem(1)[0],
        scratch_shapes=[pltpu.VMEM(rows.shape, rows.dtype)] + [pltpu.SemaphoreType.DMA((peers,))] * 2,
        compiler_params=pltpu.CompilerParams(collective_id=2, has_side_effects=True),
    )(rows)


def norm_parts(rows_in):
    centred = rows_in - jnp.mean(rows_in, axis=-1, keepdims=True)
    inverse = lax.rsqrt(jnp.mean(centred * centred, axis=-1, keepdims=True) + 1e-06)
    return centred * inverse, inverse


def norm_back(unit, inverse, gain_row, grad_rows):
    scaled = grad_rows * gain_row
    inner = scaled - jnp.mean(scaled, axis=-1, keepdims=True)
    return inverse * (inner - unit * jnp.mean(scaled * unit, axis=-1, keepdims=True))


def two_heads(rows):
    low_half = lax.broadcasted_iota(jnp.int32, rows.shape, 1) < HEAD_DIM
    none = jnp.zeros_like(rows)
    return jnp.concatenate([jnp.where(low_half, rows, none), jnp.where(low_half, none, rows)], 0)


def join_heads(stacked):
    rows = stacked.shape[0] // 2
    low_half = lax.broadcasted_iota(jnp.int32, (rows, stacked.shape[1]), 1) < HEAD_DIM
    return jnp.where(low_half, stacked[:rows], stacked[rows:])


def pair_attention(query_two, key_pair):
    scores = contract_last(query_two, key_pair) * (HEAD_DIM ** (-0.5))
    real_key = lax.broadcasted_iota(jnp.int32, scores.shape, 1) < SEQ
    scores = jnp.where(real_key, scores, -jnp.inf)
    weights = jnp.exp(scores - jnp.max(scores, axis=-1, keepdims=True))
    return weights * (1.0 / jnp.sum(weights, axis=-1, keepdims=True))


def project_qkv(normed, mats_ref):
    return [
        jnp.dot(normed, mats_ref[part], preferred_element_type=jnp.float32).astype(jnp.bfloat16)
        for part in range(3)
    ]


def attend_kernel(
    experts, stream_ref, mats_ref, gains_ref, router_ref, middle_ref, normed_ref, probs_ref, mixed_ref
):
    rows = stream_ref[0]
    normed = (norm_parts(rows)[0] * gains_ref[0:1]).astype(jnp.bfloat16)
    query, keys, values = project_qkv(normed, mats_ref)
    for pair in range(query.shape[1] // (2 * HEAD_DIM)):
        cols = slice(pair * 2 * HEAD_DIM, (pair + 1) * 2 * HEAD_DIM)
        attention = pair_attention(two_heads(query[:, cols]), keys[:, cols]).astype(jnp.bfloat16)
        mixed = jnp.dot(attention, values[:, cols], preferred_element_type=jnp.float32)
        mixed_ref[0, :, cols] = join_heads(mixed).astype(jnp.bfloat16)
    middle = rows + contract_last(mixed_ref[0], mats_ref[3])
    middle_ref[0] = middle
    normed_two = (norm_parts(middle)[0] * gains_ref[1:2]).astype(jnp.bfloat16)
    normed_ref[0] = normed_two
    logits = jnp.dot(normed_two, router_ref[...], preferred_element_type=jnp.float32)
    real = lax.broadcasted_iota(jnp.int32, logits.shape, 1) < experts
    logits = jnp.where(real, logits, -jnp.inf)
    odds = jnp.exp(logits - jnp.max(logits, axis=-1, keepdims=True))
    probs_ref[0] = odds * (1.0 / jnp.sum(odds, axis=-1, keepdims=True))


def attend_back_kernel(
    own_ref,
    upstream_ref,
    grad_ref,
    grad_logits_ref,
    stream_ref,
    middle_ref,
    mixed_ref,
    mats_ref,
    gains_ref,
    router_ref,
    down_ref,
    mats_grad,
    router_grad,
    gains_grad,
    triple,
):
    @pl.when(pl.program_id(0) == 0)
    def _():
        mats_grad[...] = jnp.zeros_like(mats_grad)
        router_grad[...] = jnp.zeros_like(router_grad)
        gains_grad[...] = jnp.zeros_like(gains_grad)

    head_cols = mats_grad.shape[2]
    mine = pl.ds(pl.multiple_of(own_ref[0] * head_cols, head_cols), head_cols)
    gain_one, gain_two = gains_ref[0:1], gains_ref[1:2]
    unit_two, inverse_two = norm_parts(middle_ref[0])
    grad_logits = grad_logits_ref[0]
    router_grad[...] += contract_rows(
        grad_logits, (unit_two * gain_two).astype(jnp.bfloat16)
    )
    grad_normed = grad_ref[0] + contract_last(grad_logits, router_ref[...])
    gains_grad[1:2] += jnp.sum(grad_normed * unit_two, axis=0, keepdims=True)
    grad_middle = upstream_ref[0] + norm_back(unit_two, inverse_two, gain_two, grad_normed)
    grad_branch = grad_middle.astype(jnp.bfloat16)
    mats_grad[3] += contract_rows(grad_branch, mixed_ref[0, :, mine])
    grad_mixed = jnp.dot(
        grad_branch, mats_ref[3], preferred_element_type=jnp.float32
    ).astype(jnp.bfloat16)
    unit_one, inverse_one = norm_parts(stream_ref[0])
    normed = (unit_one * gain_one).astype(jnp.bfloat16)
    query, keys, values = project_qkv(normed, mats_ref)
    scale = HEAD_DIM ** (-0.5)
    for pair in range(query.shape[1] // (2 * HEAD_DIM)):
        cols = slice(pair * 2 * HEAD_DIM, (pair + 1) * 2 * HEAD_DIM)
        query_two = two_heads(query[:, cols])
        attention = pair_attention(query_two, keys[:, cols])
        grad_two = two_heads(grad_mixed[:, cols])
        triple[2, :, cols] = contract_rows(attention.astype(jnp.bfloat16), grad_two).astype(
            jnp.bfloat16
        )
        grad_attention = contract_last(grad_two, values[:, cols])
        grad_scores = (
            attention
            * (grad_attention - jnp.sum(attention * grad_attention, axis=-1, keepdims=True))
        ).astype(jnp.bfloat16)
        grad_query = jnp.dot(grad_scores, keys[:, cols], preferred_element_type=jnp.float32)
        triple[0, :, cols] = (join_heads(grad_query) * scale).astype(jnp.bfloat16)
        triple[1, :, cols] = (contract_rows(grad_scores, query_two) * scale).astype(jnp.bfloat16)
    grad_one = contract_last(triple[0], mats_ref[0])
    for part in range(3):
        if part:
            grad_one += contract_last(triple[part], mats_ref[part])
        mats_grad[part] += contract_rows(normed, triple[part, :, mine])
    gains_grad[0:1] += jnp.sum(grad_one * unit_one, axis=0, keepdims=True)
    down_ref[0] = grad_middle + norm_back(unit_one, inverse_one, gain_one, grad_one)


def image_spec(array):
    return pl.BlockSpec((1,) + array.shape[1:], lambda image: (image, 0, 0))


def fixed_spec(array):
    return pl.BlockSpec(array.shape, lambda image: (0,) * len(array.shape))


def attend(stream, mats, gains, router, experts):
    images, rows, width = stream.shape
    outs = (
        jax.ShapeDtypeStruct(stream.shape, jnp.float32),
        jax.ShapeDtypeStruct(stream.shape, jnp.bfloat16),
        jax.ShapeDtypeStruct((images, rows, router.shape[1]), jnp.float32),
        jax.ShapeDtypeStruct((images, rows, mats.shape[2]), jnp.bfloat16),
    )
    return pl.pallas_call(
        functools.partial(attend_kernel, experts),
        grid=(images,),
        out_shape=outs,
        in_specs=[image_spec(stream), fixed_spec(mats), fixed_spec(gains), fixed_spec(router)],
        out_specs=tuple(image_spec(one) for one in outs),
    )(stream, mats, gains, router)


def attend_back(upstream, grad_normed, grad_logits, stream, middle, mixed, mats, gains, router, head_cols):
    images, rows, width = stream.shape
    own = lax.axis_index("tensor").astype(jnp.int32).reshape(1)
    sums = (
        jax.ShapeDtypeStruct((4, width, head_cols), jnp.float32),
        jax.ShapeDtypeStruct((router.shape[1], width), jnp.float32),
        jax.ShapeDtypeStruct(gains.shape, jnp.float32),
    )
    per_image = [upstream, grad_normed, grad_logits, stream, middle, mixed]
    fixed = [mats, gains, router]
    return pl.pallas_call(
        attend_back_kernel,
        grid=(images,),
        out_shape=(jax.ShapeDtypeStruct(stream.shape, jnp.float32),) + sums,
        in_specs=[pl.BlockSpec(memory_space=pltpu.SMEM)]
        + [image_spec(one) for one in per_image]
        + [fixed_spec(one) for one in fixed],
        out_specs=(image_spec(stream),) + tuple(fixed_spec(one) for one in sums),
        scratch_shapes=[pltpu.VMEM((3, rows, mats.shape[2]), jnp.bfloat16)],
    )(own, *per_image, *fixed)


def slot_plan(chosen, rank_rows, experts, capacity, spacing):
    columns = lax.broadcasted_iota(jnp.int32, (1, experts), 1)
    first_hot = (chosen[:, 0:1] == columns).astype(jnp.bfloat16)
    second = (chosen[:, 1:2] == columns).astype(jnp.bfloat16)
    earlier = (rank_rows[None, :] < rank_rows[:, None]).astype(jnp.bfloat16)
    count_first = jnp.dot(earlier, first_hot, preferred_element_type=jnp.float32)
    count_second = jnp.dot(earlier, second, preferred_element_type=jnp.float32)
    first_f = first_hot.astype(jnp.float32)
    second_f = second.astype(jnp.float32)
    filled = jnp.sum(first_f, axis=0, keepdims=True)
    slot_first = jnp.sum(count_first * first_f, axis=1)
    slot_second = jnp.sum((filled + count_second) * second_f, axis=1)
    slot_nums = jnp.stack([slot_first, slot_second], axis=1).astype(jnp.int32)
    target = jnp.where(slot_nums < capacity, chosen * spacing + slot_nums, experts * spacing)
    return (target, first_f, second_f)


def local(
    inputs,
    cotangent,
    routes,
    priority,
    attend_in,
    attend_out,
    router,
    norm_gains,
    expert_in,
    expert_out,
):
    experts = lax.axis_size("expert")
    tokens = inputs.shape[0]
    model_width = inputs.shape[1]
    images = tokens // SEQ
    head_cols = attend_in.shape[3]
    layers = attend_in.shape[0]
    capacity = max(2, (10 * tokens + 4 * experts - 1) // (4 * experts))
    peers_tensor = lax.axis_size("tensor")
    spacing = -(-capacity // (16 * peers_tensor)) * 16 * peers_tensor
    slots_all = experts * spacing
    row_share = attend_in.shape[2]
    gain_share = norm_gains.shape[2]
    image_rows = -(-SEQ // 16) * 16
    tokens_all = images * image_rows

    def spread(rows, fill):
        shaped = rows.reshape((images, SEQ) + rows.shape[1:])
        edges = ((0, 0), (0, image_rows - SEQ)) + ((0, 0),) * (rows.ndim - 1)
        return jnp.pad(shaped, edges, constant_values=fill)

    def gather_tensor(rows, axis):
        return lax.all_gather(rows.astype(jnp.bfloat16), "tensor", axis=axis, tiled=True)

    smalls = jnp.concatenate([router.reshape(-1), norm_gains.reshape(-1)])
    block = row_share * head_cols
    smalls = jnp.pad(smalls, (0, -smalls.shape[0] % block)).reshape(-1, row_share, head_cols)
    packed = jnp.concatenate(
        [
            jnp.concatenate([attend_in, attend_out.transpose(0, 2, 1)[:, None]], axis=1).reshape(
                -1, row_share, head_cols
            ),
            smalls,
        ]
    )
    whole, win_first, wout_first = gather_start(
        packed.astype(jnp.bfloat16),
        expert_in[0, 0].astype(jnp.bfloat16),
        expert_out[0, 0].astype(jnp.bfloat16),
        experts,
        peers_tensor,
    )
    whole = whole.reshape(whole.shape[0], model_width, model_width)
    small_rows = whole[4 * layers :, :, :head_cols].reshape(-1, experts, block)
    small_rows = small_rows.transpose(1, 0, 2).reshape(experts, -1)
    router_all = small_rows[:, : layers * model_width].reshape(experts, layers, model_width)
    gains_all = small_rows[:, layers * model_width :][:, : layers * 2 * gain_share]
    gains_all = gains_all.reshape(experts, layers, 2, gain_share).transpose(1, 2, 0, 3)
    gains_all = gains_all.reshape(layers, 2, model_width).astype(jnp.float32)
    router_all = jnp.pad(router_all.transpose(1, 2, 0), ((0, 0), (0, 0), (0, -experts % 128)))
    win_full, wout_full = [win_first], [wout_first]
    slot_ids = lax.broadcasted_iota(jnp.int32, (1, slots_all), 1)
    stream = spread(inputs, 0)
    stash_list = []
    for layer_index in range(layers):
        mats = whole[4 * layer_index : 4 * layer_index + 4]
        gains_now = gains_all[layer_index]
        router_now = router_all[layer_index]
        middle, normed_two, probs_all, mixed_heads = attend(
            stream, mats, gains_now, router_now, experts
        )
        probs_all = probs_all.reshape(tokens_all, -1)[:, :experts]
        chosen = spread(routes[layer_index], -1).reshape(tokens_all, 2)
        ranks = spread(priority[layer_index], tokens).reshape(tokens_all)
        target, first_f, second_f = slot_plan(chosen, ranks, experts, capacity, spacing)
        gate_values = jnp.stack(
            [jnp.sum(probs_all * first_f, axis=1), jnp.sum(probs_all * second_f, axis=1)], axis=1
        )
        pick_first = (target[:, 0:1] == slot_ids).astype(jnp.bfloat16)
        pick_second = (target[:, 1:2] == slot_ids).astype(jnp.bfloat16)
        pick_both = pick_first + pick_second
        dispatched = contract_rows(pick_both, normed_two.reshape(tokens_all, model_width))
        following = ()
        if layer_index + 1 < layers:
            following = (
                expert_in[layer_index + 1, 0].astype(jnp.bfloat16),
                expert_out[layer_index + 1, 0].astype(jnp.bfloat16),
            )
        arrived, returned, *gathered = experts_forward(
            dispatched.astype(jnp.bfloat16).reshape(experts, spacing, model_width),
            win_full[layer_index],
            wout_full[layer_index],
            peers_tensor,
            following,
        )
        if gathered:
            win_full.append(gathered[0])
            wout_full.append(gathered[1])
        returned = returned.reshape(slots_all, model_width)
        rows_first = jnp.dot(pick_first, returned, preferred_element_type=jnp.float32)
        rows_second = jnp.dot(pick_second, returned, preferred_element_type=jnp.float32)
        output = (
            middle.reshape(tokens_all, model_width)
            + gate_values[:, 0:1] * rows_first
            + gate_values[:, 1:2] * rows_second
        )
        stash_list.append(
            (
                stream,
                mats,
                gains_now,
                router_now,
                mixed_heads,
                middle,
                probs_all,
                gate_values,
                first_f,
                second_f,
                pick_first,
                pick_second,
                pick_both,
                arrived,
                rows_first,
                rows_second,
            )
        )
        stream = output.reshape(images, image_rows, model_width)
    upstream = spread(cotangent, 0).reshape(tokens_all, model_width)
    grads_in, grads_out, grads_router, grads_gain, grads_win, grads_wout = ([], [], [], [], [], [])
    grads_shared = []
    for layer_index in reversed(range(layers)):
        (
            stream_in,
            mats,
            gains_now,
            router_now,
            mixed_heads,
            middle,
            probs_all,
            gate_values,
            first_f,
            second_f,
            pick_first,
            pick_second,
            pick_both,
            arrived,
            rows_first,
            rows_second,
        ) = stash_list[layer_index]
        gate_first = jnp.sum(upstream * rows_first, axis=1)
        gate_second = jnp.sum(upstream * rows_second, axis=1)
        scaled_first = (gate_values[:, 0:1] * upstream).astype(jnp.bfloat16)
        scaled_second = (gate_values[:, 1:2] * upstream).astype(jnp.bfloat16)
        grad_slots = (
            contract_rows(pick_first, scaled_first) + contract_rows(pick_second, scaled_second)
        ).astype(jnp.bfloat16)
        grad_dispatched, win_grad, wout_grad = experts_backward(
            grad_slots.reshape(experts, spacing, model_width),
            arrived,
            win_full[layer_index],
            wout_full[layer_index],
            peers_tensor,
        )
        grads_win.append(win_grad)
        grads_wout.append(wout_grad)
        grad_dispatched = grad_dispatched.reshape(slots_all, model_width)
        grad_normed = jnp.dot(pick_both, grad_dispatched, preferred_element_type=jnp.float32)
        grad_probs = first_f * gate_first[:, None] + second_f * gate_second[:, None]
        grad_logits = (
            probs_all * (grad_probs - jnp.sum(probs_all * grad_probs, axis=1, keepdims=True))
        ).astype(jnp.bfloat16)
        grad_logits = jnp.pad(grad_logits, ((0, 0), (0, router_now.shape[1] - experts)))
        shape = stream_in.shape
        down, mats_grad, router_grad, gain_grad = attend_back(
            upstream.reshape(shape),
            grad_normed.reshape(shape),
            grad_logits.reshape(images, image_rows, -1),
            stream_in,
            middle,
            mixed_heads,
            mats,
            gains_now,
            router_now,
            head_cols,
        )
        mats_grad = mats_grad.reshape(4, experts, row_share, head_cols).transpose(1, 0, 2, 3)
        router_grad = router_grad[:experts]
        gain_grad = gain_grad.reshape(2, experts, gain_share)
        smalls = jnp.concatenate(
            [router_grad, gain_grad.transpose(1, 0, 2).reshape(experts, -1)], axis=1
        )
        smalls = jnp.pad(smalls, ((0, 0), (0, -smalls.shape[1] % 2048)))
        grads_shared.append(
            jnp.concatenate(
                [mats_grad.reshape(experts, -1, 128), smalls.reshape(experts, -1, 128)], axis=1
            ).astype(jnp.bfloat16)
        )
        upstream = down.reshape(tokens_all, model_width)
    total_rows = grads_shared[0].shape[1]
    mat_rows = 4 * row_share * head_cols // 128
    shared_all = sum_shares(jnp.concatenate(grads_shared, axis=1))
    for order in range(layers):
        shared = shared_all[order * total_rows : (order + 1) * total_rows]
        mats_own = shared[:mat_rows].reshape(4, row_share, head_cols)
        small_own = shared[mat_rows:].reshape(-1)
        grads_in.append(mats_own[:3])
        grads_out.append(mats_own[3].T)
        grads_router.append(small_own[:model_width, None])
        grads_gain.append(
            small_own[model_width : model_width + 2 * gain_share].reshape(2, gain_share)
        )
    win_grad_all = jnp.stack(grads_win[::-1])[:, None]
    wout_grad_all = jnp.stack(grads_wout[::-1])[:, None]
    return (
        stream[:, :SEQ].reshape(tokens, model_width),
        upstream.reshape(stream.shape)[:, :SEQ].reshape(tokens, model_width),
        jnp.stack(grads_in[::-1]),
        jnp.stack(grads_out[::-1]),
        jnp.stack(grads_router[::-1]),
        jnp.stack(grads_gain[::-1]),
        win_grad_all,
        wout_grad_all,
    )


def solution(mesh):
    placed = (
        P("expert", None),
        P("expert", None),
        P(None, "expert", None),
        P(None, "expert"),
        P(None, None, "expert", "tensor"),
        P(None, "tensor", "expert"),
        P(None, None, "expert"),
        P(None, None, "expert"),
        P(None, "expert", None, "tensor"),
        P(None, "expert", "tensor", None),
    )
    return jax.shard_map(
        local,
        mesh=mesh,
        in_specs=placed,
        out_specs=(
            P("expert", None),
            P("expert", None),
            P(None, None, "expert", "tensor"),
            P(None, "tensor", "expert"),
            P(None, None, "expert"),
            P(None, None, "expert"),
            P(None, "expert", None, "tensor"),
            P(None, "expert", "tensor", None),
        ),
        check_vma=False,
    )
```

```python
import functools

import jax
import jax.numpy as jnp
from jax import lax
from jax.experimental import pallas as pl
from jax.experimental.pallas import tpu as pltpu
from jax.sharding import PartitionSpec as P

HEAD_DIM = 64
SEQ = 197


def gelu_exact(rows_in):
    return 0.5 * rows_in * (1.0 + lax.erf(rows_in * 0.7071067811865476))


def contract_rows(left_side, right_side):
    return lax.dot_general(
        left_side, right_side, (((0,), (0,)), ((), ())), preferred_element_type=jnp.float32
    )


def contract_last(left_side, right_side):
    return lax.dot_general(
        left_side, right_side, (((1,), (1,)), ((), ())), preferred_element_type=jnp.float32
    )


def gelu_parts(rows_in):
    half = 0.5 * (1.0 + lax.erf(rows_in * 0.7071067811865476))
    slope = half + rows_in * (jnp.exp(-0.5 * rows_in * rows_in) * 0.3989422804014327)
    return rows_in * half, slope


def greet(barrier, axis, index):
    pl.semaphore_signal(
        barrier, inc=1, device_id={axis: index}, device_id_type=pl.DeviceIdType.MESH
    )


def greet_axis(barrier, axis, me, peers):
    def one(step, carry):
        greet(barrier, axis, lax.rem(me + step, peers))
        return carry

    lax.fori_loop(1, peers, one, 0)


def send(source, landing, send_sem, recv_sem, axis, index):
    return pltpu.make_async_remote_copy(
        src_ref=source,
        dst_ref=landing,
        send_sem=send_sem,
        recv_sem=recv_sem,
        device_id={axis: index},
        device_id_type=pl.DeviceIdType.MESH,
    )


def send_chunk(source, landing, sends, arrivals, step, peer):
    return send(source, landing, sends.at[step], arrivals.at[step], "expert", peer)


def meet_peers(me, peers):
    barrier = pltpu.get_barrier_semaphore()
    greet_axis(barrier, "expert", me, peers)
    pl.semaphore_wait(barrier, peers - 1)


class Ring:
    def __init__(self, parts, place, own, sends, arrivals, both=True):
        self.parts, self.place, self.own = parts, place, own
        self.sends, self.arrivals = sends, arrivals
        self.side = lax.axis_index("tensor")
        self.hops = []
        for distance in range(1, parts // 2 + 1):
            if 2 * distance < parts:
                self.hops += [(distance, 1, None), (distance, -1, None)]
            elif both:
                self.hops += [(distance, 1, 0), (distance, -1, 1)]
            else:
                self.hops += [(distance, 1, None)]

    def wrap(self, index):
        return lax.rem(self.side + self.parts + index, self.parts)

    def outgoing(self, number):
        distance, way, half = self.hops[number]
        landing = self.place(self.wrap(-way * (distance - 1)), half)
        source = landing if distance > 1 else self.own(half)
        return send(
            source,
            landing,
            self.sends(number),
            self.arrivals(number),
            "tensor",
            self.wrap(way),
        )

    def incoming(self, number):
        distance, way, half = self.hops[number]
        landing = self.place(self.wrap(-way * distance), half)
        return send(
            landing,
            landing,
            self.sends(number),
            self.arrivals(number),
            "tensor",
            self.wrap(way),
        )

    def stage(self, wanted):
        for number, (distance, way, _) in enumerate(self.hops):
            if distance == wanted:
                for earlier, (before, same, _) in enumerate(self.hops):
                    if before == distance - 1 and same == way:
                        self.incoming(earlier).wait_recv()
                self.outgoing(number).start()

    def finish(self):
        kept = {(distance, way) for distance, way, _ in self.hops}
        for number, (distance, way, _) in enumerate(self.hops):
            self.outgoing(number).wait_send()
            if (distance + 1, way) not in kept:
                self.incoming(number).wait_recv()


def weight_ring(parts, kind, source, target, sends, arrivals):
    length = source.shape[1 - kind]

    def cut(ref, start, half):
        size = length if half is None else length // 2
        start = start + (0 if half is None else half * size)
        span = pl.ds(pl.multiple_of(start, size), size)
        return ref.at[:, span] if kind == 0 else ref.at[span, :]

    return Ring(
        parts,
        lambda owner, half: cut(target, owner * length, half),
        lambda half: cut(source, 0, half),
        lambda number: sends.at[number],
        lambda number: arrivals.at[number],
    )


def own_weight(kind, source, target, local_sem):
    length = source.shape[1 - kind]
    span = pl.ds(pl.multiple_of(lax.axis_index("tensor") * length, length), length)
    place = target.at[:, span] if kind == 0 else target.at[span, :]
    return pltpu.make_async_copy(source, place, local_sem)


def gather_kernel(
    experts,
    parts,
    small_ref,
    win_ref,
    whole,
    win_full,
    side_send,
    side_recv,
    ring_send,
    ring_recv,
    chip_send,
    chip_recv,
    twin_send,
    twin_recv,
    local_sem,
):
    me = lax.axis_index("expert")
    side = lax.axis_index("tensor")
    twin = me + 1 - 2 * lax.rem(me, 2)
    chips = experts // 2
    cols = small_ref.shape[2]
    barrier = pltpu.get_barrier_semaphore()
    greet_axis(barrier, "tensor", side, parts)
    greet(barrier, "expert", twin)
    for step in range(1, chips):
        greet(barrier, "expert", lax.rem(me + 2 * step, experts))
    pl.semaphore_wait(barrier, parts - 1 + chips)

    def place(index):
        return whole.at[:, me, :, pl.ds(pl.multiple_of(index * cols, cols), cols)]

    def side_copy(step, owner, target):
        return send(
            small_ref, place(owner), side_send.at[step], side_recv.at[step], "tensor", target
        )

    for step in range(1, parts):
        side_copy(step, side, lax.rem(side + step, parts)).start()
    ring = weight_ring(parts, 0, win_ref, win_full, ring_send, ring_recv)
    ring.stage(1)
    own_win = own_weight(0, win_ref, win_full, local_sem.at[0])
    own_small = pltpu.make_async_copy(small_ref, place(side), local_sem.at[1])
    own_win.start()
    own_small.start()
    own_small.wait()
    for step in range(1, parts):
        side_copy(step, lax.rem(side + parts - step, parts), side).wait_recv()

    def chip_copy(step, owner, target):
        return send_chunk(whole.at[:, owner], whole.at[:, owner], chip_send, chip_recv, step, target)

    def twin_copy(step, owner):
        return send_chunk(whole.at[:, owner], whole.at[:, owner], twin_send, twin_recv, step, twin)

    for step in range(1, chips):
        chip_copy(step, me, lax.rem(me + 2 * step, experts)).start()
    twin_copy(0, me).start()
    for distance in range(2, parts // 2 + 1):
        ring.stage(distance)
    for step in range(1, chips):
        owner = lax.rem(me + experts - 2 * step, experts)
        chip_copy(step, owner, owner).wait_recv()
        twin_copy(step, owner).start()
    for step in range(chips):
        twin_copy(step, lax.rem(twin + experts - 2 * step, experts)).wait_recv()
        twin_copy(step, lax.rem(me + experts - 2 * step, experts)).wait_send()
        if step:
            chip_copy(step, me, lax.rem(me + 2 * step, experts)).wait_send()
    for step in range(1, parts):
        side_copy(step, side, lax.rem(side + step, parts)).wait_send()
    ring.finish()
    own_win.wait()


def gather_start(small, win, experts, parts):
    count, rows, cols = small.shape
    depth, width = win.shape
    chips = experts // 2
    return pl.pallas_call(
        functools.partial(gather_kernel, experts, parts),
        out_shape=(
            jax.ShapeDtypeStruct((count, experts, rows, cols * parts), jnp.bfloat16),
            jax.ShapeDtypeStruct((depth, width * parts), jnp.bfloat16),
        ),
        in_specs=whole_in_vmem(2),
        out_specs=tuple(whole_in_vmem(2)),
        scratch_shapes=[pltpu.SemaphoreType.DMA((parts,))] * 4
        + [pltpu.SemaphoreType.DMA((chips,))] * 4
        + [pltpu.SemaphoreType.DMA((2,))],
        compiler_params=pltpu.CompilerParams(collective_id=3, has_side_effects=True),
    )(small, win)


def exchange_chunks(peers, work, out_rows, landed, results, back, sems, parts=1, rings=()):
    out_send, out_recv, back_send, back_recv = sems
    me = lax.axis_index("expert")
    barrier = pltpu.get_barrier_semaphore()
    greet_axis(barrier, "expert", me, peers)
    if rings:
        greet_axis(barrier, "tensor", lax.axis_index("tensor"), parts)
    pl.semaphore_wait(barrier, peers - 1 + (parts - 1 if rings else 0))
    for ring in rings:
        ring.stage(1)

    def start_out(step, carry):
        peer = lax.rem(me + step, peers)
        send_chunk(out_rows.at[peer], landed.at[me], out_send, out_recv, step, peer).start()
        return carry

    lax.fori_loop(1, peers, start_out, 0)
    landed[me] = out_rows[me]
    for distance in range(2, parts // 2 + 1):
        for ring in rings[:1]:
            ring.stage(distance)
    for ring in rings[:1]:
        ring.finish()

    def one_chunk(step, carry):
        peer = lax.rem(me + peers - step, peers)
        if len(rings) > 1:

            @pl.when(step == peers // 4)
            def _():
                for distance in range(2, parts // 2 + 1):
                    for ring in rings[1:]:
                        ring.stage(distance)

        @pl.when(step > 0)
        def _():
            send_chunk(
                out_rows.at[peer], landed.at[peer], out_send, out_recv, step, peer
            ).wait_recv()

        work(step, peer)

        @pl.when(step > 0)
        def _():
            send_chunk(results.at[step], back.at[me], back_send, back_recv, step, peer).start()

        return carry

    lax.fori_loop(0, peers, one_chunk, 0)
    back[me] = results[0]

    def finish(step, carry):
        ahead = lax.rem(me + step, peers)
        send_chunk(out_rows.at[ahead], landed.at[me], out_send, out_recv, step, ahead).wait_send()
        last = send_chunk(results.at[step], back.at[ahead], back_send, back_recv, step, ahead)
        last.wait_send()
        last.wait_recv()
        return carry

    lax.fori_loop(1, peers, finish, 0)
    for ring in rings[1:]:
        ring.finish()


def forward_kernel(peers, parts, follow, *refs):
    rows_ref, win_ref = refs[:2]
    sources = refs[2 : 3 + follow]
    landed, back = refs[3 + follow : 5 + follow]
    targets = refs[5 + follow : 6 + 2 * follow]
    results, total, *sems = refs[6 + 2 * follow :]
    wout_ref = targets[0]
    kinds = (1, 0)[: 1 + follow]
    local_sem = sems[-1]
    rings, copies = [], []
    for order, kind in enumerate(kinds):
        pair = (sources[order], targets[order])
        rings.append(weight_ring(parts, kind, *pair, sems[4 + 2 * order], sems[5 + 2 * order]))
        copies.append(own_weight(kind, *pair, local_sem.at[order]))
    for copy in copies:
        copy.start()
    copies[0].wait()
    width = win_ref.shape[1] // parts

    def work(step, peer):
        chunk = landed[peer]
        for part in range(parts):
            cols = slice(part * width, (part + 1) * width)
            before = jnp.dot(chunk, win_ref[:, cols], preferred_element_type=jnp.float32)
            hidden = gelu_exact(before).astype(jnp.bfloat16)
            term = jnp.dot(hidden, wout_ref[cols, :], preferred_element_type=jnp.float32)
            if part == 0:
                total[...] = term
            elif part < parts - 1:
                total[...] += term
            else:
                results[step] = (total[...] + term).astype(jnp.bfloat16)

    exchange_chunks(
        peers, work, rows_ref, landed, results, back, sems[:4], parts=parts, rings=rings
    )
    for copy in copies[1:]:
        copy.wait()


def backward_kernel(
    peers,
    parts,
    rows_ref,
    arrived_ref,
    win_ref,
    wout_ref,
    back,
    win_grad,
    wout_grad,
    landed,
    results,
    total,
    hidden_all,
    before_all,
    *sems,
):
    width = win_ref.shape[1] // parts
    own = lax.axis_index("tensor") * width
    win_grad[...] = jnp.zeros_like(win_grad)
    wout_grad[...] = jnp.zeros_like(wout_grad)

    def work(step, peer):
        chunk = arrived_ref[peer]
        grad_chunk = landed[peer]
        for part in range(parts):
            cols = slice(part * width, (part + 1) * width)
            before = jnp.dot(chunk, win_ref[:, cols], preferred_element_type=jnp.float32)
            value, slope = gelu_parts(before)
            grad_hidden = contract_last(grad_chunk, wout_ref[cols, :])
            grad_before = (grad_hidden * slope).astype(jnp.bfloat16)
            hidden_all[:, cols] = value.astype(jnp.bfloat16)
            before_all[:, cols] = grad_before
            term = contract_last(grad_before, win_ref[:, cols])
            if part == 0:
                total[...] = term
            elif part < parts - 1:
                total[...] += term
            else:
                results[step] = (total[...] + term).astype(jnp.bfloat16)
        mine = pl.ds(pl.multiple_of(own, width), width)
        wout_grad[...] += contract_rows(hidden_all[:, mine], grad_chunk)
        win_grad[...] += contract_rows(chunk, before_all[:, mine])

    exchange_chunks(peers, work, rows_ref, landed, results, back, sems)


def sum_kernel(peers, rows_ref, sum_ref, landed, sends, arrivals):
    me = lax.axis_index("expert")
    meet_peers(me, peers)

    def start_out(step, carry):
        peer = lax.rem(me + step, peers)
        send_chunk(rows_ref.at[peer], landed.at[me], sends, arrivals, step, peer).start()
        return carry

    lax.fori_loop(1, peers, start_out, 0)
    landed[me] = rows_ref[me]

    def finish(step, carry):
        peer = lax.rem(me + peers - step, peers)
        one = send_chunk(rows_ref.at[peer], landed.at[peer], sends, arrivals, step, peer)
        one.wait_send()
        one.wait_recv()
        return carry

    lax.fori_loop(1, peers, finish, 0)
    sum_ref[...] = landed[0].astype(jnp.float32)

    def add_one(source, carry):
        sum_ref[...] += landed[source].astype(jnp.float32)
        return carry

    lax.fori_loop(1, peers, add_one, 0)


def sum_shares(rows):
    peers = rows.shape[0]
    return pl.pallas_call(
        functools.partial(sum_kernel, peers),
        out_shape=jax.ShapeDtypeStruct(rows.shape[1:], jnp.float32),
        in_specs=whole_in_vmem(1),
        out_specs=whole_in_vmem(1)[0],
        scratch_shapes=[pltpu.VMEM(rows.shape, rows.dtype)] + [pltpu.SemaphoreType.DMA((peers,))] * 2,
        compiler_params=pltpu.CompilerParams(collective_id=2, has_side_effects=True),
    )(rows)


def whole_in_vmem(count):
    return [pl.BlockSpec(memory_space=pltpu.VMEM)] * count


def exchange_sems(peers):
    return [pltpu.SemaphoreType.DMA((peers,)) for _ in range(4)]


def experts_forward(rows, win, wout_part, parts, following=()):
    peers, capacity, width = rows.shape
    like = jax.ShapeDtypeStruct(rows.shape, jnp.bfloat16)
    follow = len(following)
    wholes = (jax.ShapeDtypeStruct(win.shape[::-1], win.dtype),)
    wholes += (jax.ShapeDtypeStruct(win.shape, win.dtype),) * follow
    return pl.pallas_call(
        functools.partial(forward_kernel, peers, parts, follow),
        out_shape=(like, like) + wholes,
        in_specs=whole_in_vmem(3 + follow),
        out_specs=tuple(whole_in_vmem(3 + follow)),
        scratch_shapes=[
            pltpu.VMEM(rows.shape, jnp.bfloat16),
            pltpu.VMEM((capacity, width), jnp.float32),
        ]
        + exchange_sems(peers)
        + [pltpu.SemaphoreType.DMA((parts,))] * (2 + 2 * follow)
        + [pltpu.SemaphoreType.DMA((2,))],
        compiler_params=pltpu.CompilerParams(
            collective_id=4 if follow else 0, has_side_effects=True
        ),
    )(rows, win, wout_part, *following)


def experts_backward(rows, arrived, win, wout, parts):
    peers, capacity, width = rows.shape
    inner = win.shape[1]
    return pl.pallas_call(
        functools.partial(backward_kernel, peers, parts),
        out_shape=(
            jax.ShapeDtypeStruct(rows.shape, jnp.bfloat16),
            jax.ShapeDtypeStruct((width, inner // parts), jnp.float32),
            jax.ShapeDtypeStruct((inner // parts, width), jnp.float32),
        ),
        in_specs=whole_in_vmem(4),
        out_specs=tuple(whole_in_vmem(3)),
        scratch_shapes=[
            pltpu.VMEM(rows.shape, jnp.bfloat16),
            pltpu.VMEM(rows.shape, jnp.bfloat16),
            pltpu.VMEM((capacity, width), jnp.float32),
            pltpu.VMEM((capacity, inner), jnp.bfloat16),
            pltpu.VMEM((capacity, inner), jnp.bfloat16),
        ]
        + exchange_sems(peers),
        compiler_params=pltpu.CompilerParams(collective_id=1, has_side_effects=True),
    )(rows, arrived, win, wout)


def norm_parts(rows_in):
    centred = rows_in - jnp.mean(rows_in, axis=-1, keepdims=True)
    inverse = lax.rsqrt(jnp.mean(centred * centred, axis=-1, keepdims=True) + 1e-06)
    return centred * inverse, inverse


def norm_back(unit, inverse, gain_row, grad_rows):
    scaled = grad_rows * gain_row
    inner = scaled - jnp.mean(scaled, axis=-1, keepdims=True)
    return inverse * (inner - unit * jnp.mean(scaled * unit, axis=-1, keepdims=True))


def two_heads(rows):
    low_half = lax.broadcasted_iota(jnp.int32, rows.shape, 1) < HEAD_DIM
    none = jnp.zeros_like(rows)
    return jnp.concatenate([jnp.where(low_half, rows, none), jnp.where(low_half, none, rows)], 0)


def join_heads(stacked):
    rows = stacked.shape[0] // 2
    low_half = lax.broadcasted_iota(jnp.int32, (rows, stacked.shape[1]), 1) < HEAD_DIM
    return jnp.where(low_half, stacked[:rows], stacked[rows:])


def pair_attention(query_two, key_pair):
    scores = contract_last(query_two, key_pair) * (HEAD_DIM ** (-0.5))
    real_key = lax.broadcasted_iota(jnp.int32, scores.shape, 1) < SEQ
    scores = jnp.where(real_key, scores, -jnp.inf)
    weights = jnp.exp(scores - jnp.max(scores, axis=-1, keepdims=True))
    return weights * (1.0 / jnp.sum(weights, axis=-1, keepdims=True))


def project_qkv(normed, mats_ref):
    return [
        jnp.dot(normed, mats_ref[part], preferred_element_type=jnp.float32).astype(jnp.bfloat16)
        for part in range(3)
    ]


def attend_kernel(
    experts, stream_ref, mats_ref, gains_ref, router_ref, middle_ref, normed_ref, probs_ref, mixed_ref
):
    rows = stream_ref[0]
    normed = (norm_parts(rows)[0] * gains_ref[0:1]).astype(jnp.bfloat16)
    query, keys, values = project_qkv(normed, mats_ref)
    for pair in range(query.shape[1] // (2 * HEAD_DIM)):
        cols = slice(pair * 2 * HEAD_DIM, (pair + 1) * 2 * HEAD_DIM)
        attention = pair_attention(two_heads(query[:, cols]), keys[:, cols]).astype(jnp.bfloat16)
        mixed = jnp.dot(attention, values[:, cols], preferred_element_type=jnp.float32)
        mixed_ref[0, :, cols] = join_heads(mixed).astype(jnp.bfloat16)
    middle = rows + contract_last(mixed_ref[0], mats_ref[3])
    middle_ref[0] = middle
    normed_two = (norm_parts(middle)[0] * gains_ref[1:2]).astype(jnp.bfloat16)
    normed_ref[0] = normed_two
    logits = jnp.dot(normed_two, router_ref[...], preferred_element_type=jnp.float32)
    real = lax.broadcasted_iota(jnp.int32, logits.shape, 1) < experts
    logits = jnp.where(real, logits, -jnp.inf)
    odds = jnp.exp(logits - jnp.max(logits, axis=-1, keepdims=True))
    probs_ref[0] = odds * (1.0 / jnp.sum(odds, axis=-1, keepdims=True))


def attend_back_kernel(
    own_ref,
    upstream_ref,
    grad_ref,
    grad_logits_ref,
    stream_ref,
    middle_ref,
    mixed_ref,
    mats_ref,
    gains_ref,
    router_ref,
    down_ref,
    mats_grad,
    router_grad,
    gains_grad,
    triple,
):
    @pl.when(pl.program_id(0) == 0)
    def _():
        mats_grad[...] = jnp.zeros_like(mats_grad)
        router_grad[...] = jnp.zeros_like(router_grad)
        gains_grad[...] = jnp.zeros_like(gains_grad)

    head_cols = mats_grad.shape[2]
    mine = pl.ds(pl.multiple_of(own_ref[0] * head_cols, head_cols), head_cols)
    gain_one, gain_two = gains_ref[0:1], gains_ref[1:2]
    unit_two, inverse_two = norm_parts(middle_ref[0])
    grad_logits = grad_logits_ref[0]
    router_grad[...] += contract_rows(
        grad_logits, (unit_two * gain_two).astype(jnp.bfloat16)
    )
    grad_normed = grad_ref[0] + contract_last(grad_logits, router_ref[...])
    gains_grad[1:2] += jnp.sum(grad_normed * unit_two, axis=0, keepdims=True)
    grad_middle = upstream_ref[0] + norm_back(unit_two, inverse_two, gain_two, grad_normed)
    grad_branch = grad_middle.astype(jnp.bfloat16)
    mats_grad[3] += contract_rows(grad_branch, mixed_ref[0, :, mine])
    grad_mixed = jnp.dot(
        grad_branch, mats_ref[3], preferred_element_type=jnp.float32
    ).astype(jnp.bfloat16)
    unit_one, inverse_one = norm_parts(stream_ref[0])
    normed = (unit_one * gain_one).astype(jnp.bfloat16)
    query, keys, values = project_qkv(normed, mats_ref)
    scale = HEAD_DIM ** (-0.5)
    for pair in range(query.shape[1] // (2 * HEAD_DIM)):
        cols = slice(pair * 2 * HEAD_DIM, (pair + 1) * 2 * HEAD_DIM)
        query_two = two_heads(query[:, cols])
        attention = pair_attention(query_two, keys[:, cols])
        grad_two = two_heads(grad_mixed[:, cols])
        triple[2, :, cols] = contract_rows(attention.astype(jnp.bfloat16), grad_two).astype(
            jnp.bfloat16
        )
        grad_attention = contract_last(grad_two, values[:, cols])
        grad_scores = (
            attention
            * (grad_attention - jnp.sum(attention * grad_attention, axis=-1, keepdims=True))
        ).astype(jnp.bfloat16)
        grad_query = jnp.dot(grad_scores, keys[:, cols], preferred_element_type=jnp.float32)
        triple[0, :, cols] = (join_heads(grad_query) * scale).astype(jnp.bfloat16)
        triple[1, :, cols] = (contract_rows(grad_scores, query_two) * scale).astype(jnp.bfloat16)
    grad_one = contract_last(triple[0], mats_ref[0])
    for part in range(3):
        if part:
            grad_one += contract_last(triple[part], mats_ref[part])
        mats_grad[part] += contract_rows(normed, triple[part, :, mine])
    gains_grad[0:1] += jnp.sum(grad_one * unit_one, axis=0, keepdims=True)
    down_ref[0] = grad_middle + norm_back(unit_one, inverse_one, gain_one, grad_one)


def image_spec(array):
    return pl.BlockSpec((1,) + array.shape[1:], lambda image: (image, 0, 0))


def fixed_spec(array):
    return pl.BlockSpec(array.shape, lambda image: (0,) * len(array.shape))


def attend(stream, mats, gains, router, experts):
    images, rows, width = stream.shape
    outs = (
        jax.ShapeDtypeStruct(stream.shape, jnp.float32),
        jax.ShapeDtypeStruct(stream.shape, jnp.bfloat16),
        jax.ShapeDtypeStruct((images, rows, router.shape[1]), jnp.float32),
        jax.ShapeDtypeStruct((images, rows, mats.shape[2]), jnp.bfloat16),
    )
    return pl.pallas_call(
        functools.partial(attend_kernel, experts),
        grid=(images,),
        out_shape=outs,
        in_specs=[image_spec(stream), fixed_spec(mats), fixed_spec(gains), fixed_spec(router)],
        out_specs=tuple(image_spec(one) for one in outs),
    )(stream, mats, gains, router)


def attend_back(upstream, grad_normed, grad_logits, stream, middle, mixed, mats, gains, router, head_cols):
    images, rows, width = stream.shape
    own = lax.axis_index("tensor").astype(jnp.int32).reshape(1)
    sums = (
        jax.ShapeDtypeStruct((4, width, head_cols), jnp.float32),
        jax.ShapeDtypeStruct((router.shape[1], width), jnp.float32),
        jax.ShapeDtypeStruct(gains.shape, jnp.float32),
    )
    per_image = [upstream, grad_normed, grad_logits, stream, middle, mixed]
    fixed = [mats, gains, router]
    return pl.pallas_call(
        attend_back_kernel,
        grid=(images,),
        out_shape=(jax.ShapeDtypeStruct(stream.shape, jnp.float32),) + sums,
        in_specs=[pl.BlockSpec(memory_space=pltpu.SMEM)]
        + [image_spec(one) for one in per_image]
        + [fixed_spec(one) for one in fixed],
        out_specs=(image_spec(stream),) + tuple(fixed_spec(one) for one in sums),
        scratch_shapes=[pltpu.VMEM((3, rows, mats.shape[2]), jnp.bfloat16)],
    )(own, *per_image, *fixed)


def slot_plan(chosen, rank_rows, experts, capacity, spacing):
    columns = lax.broadcasted_iota(jnp.int32, (1, experts), 1)
    first_hot = (chosen[:, 0:1] == columns).astype(jnp.bfloat16)
    second = (chosen[:, 1:2] == columns).astype(jnp.bfloat16)
    earlier = (rank_rows[None, :] < rank_rows[:, None]).astype(jnp.bfloat16)
    count_first = jnp.dot(earlier, first_hot, preferred_element_type=jnp.float32)
    count_second = jnp.dot(earlier, second, preferred_element_type=jnp.float32)
    first_f = first_hot.astype(jnp.float32)
    second_f = second.astype(jnp.float32)
    filled = jnp.sum(first_f, axis=0, keepdims=True)
    slot_first = jnp.sum(count_first * first_f, axis=1)
    slot_second = jnp.sum((filled + count_second) * second_f, axis=1)
    slot_nums = jnp.stack([slot_first, slot_second], axis=1).astype(jnp.int32)
    target = jnp.where(slot_nums < capacity, chosen * spacing + slot_nums, experts * spacing)
    return (target, first_f, second_f)


def local(
    inputs,
    cotangent,
    routes,
    priority,
    attend_in,
    attend_out,
    router,
    norm_gains,
    expert_in,
    expert_out,
):
    experts = lax.axis_size("expert")
    tokens = inputs.shape[0]
    model_width = inputs.shape[1]
    images = tokens // SEQ
    head_cols = attend_in.shape[3]
    layers = attend_in.shape[0]
    capacity = max(2, (10 * tokens + 4 * experts - 1) // (4 * experts))
    peers_tensor = lax.axis_size("tensor")
    spacing = -(-capacity // 16) * 16
    slots_all = experts * spacing
    row_share = attend_in.shape[2]
    gain_share = norm_gains.shape[2]
    image_rows = -(-SEQ // 16) * 16
    tokens_all = images * image_rows

    def spread(rows, fill):
        shaped = rows.reshape((images, SEQ) + rows.shape[1:])
        edges = ((0, 0), (0, image_rows - SEQ)) + ((0, 0),) * (rows.ndim - 1)
        return jnp.pad(shaped, edges, constant_values=fill)

    smalls = jnp.concatenate([router.reshape(-1), norm_gains.reshape(-1)])
    block = row_share * head_cols
    smalls = jnp.pad(smalls, (0, -smalls.shape[0] % block)).reshape(-1, row_share, head_cols)
    packed = jnp.concatenate(
        [
            jnp.concatenate([attend_in, attend_out.transpose(0, 2, 1)[:, None]], axis=1).reshape(
                -1, row_share, head_cols
            ),
            smalls,
        ]
    )
    whole, win_first = gather_start(
        packed.astype(jnp.bfloat16),
        expert_in[0, 0].astype(jnp.bfloat16),
        experts,
        peers_tensor,
    )
    whole = whole.reshape(whole.shape[0], model_width, model_width)
    small_rows = whole[4 * layers :, :, :head_cols].reshape(-1, experts, block)
    small_rows = small_rows.transpose(1, 0, 2).reshape(experts, -1)
    router_all = small_rows[:, : layers * model_width].reshape(experts, layers, model_width)
    gains_all = small_rows[:, layers * model_width :][:, : layers * 2 * gain_share]
    gains_all = gains_all.reshape(experts, layers, 2, gain_share).transpose(1, 2, 0, 3)
    gains_all = gains_all.reshape(layers, 2, model_width).astype(jnp.float32)
    router_all = jnp.pad(router_all.transpose(1, 2, 0), ((0, 0), (0, 0), (0, -experts % 128)))
    win_full, wout_full = [win_first], []
    slot_ids = lax.broadcasted_iota(jnp.int32, (1, slots_all), 1)
    stream = spread(inputs, 0)
    stash_list = []
    for layer_index in range(layers):
        mats = whole[4 * layer_index : 4 * layer_index + 4]
        gains_now = gains_all[layer_index]
        router_now = router_all[layer_index]
        middle, normed_two, probs_all, mixed_heads = attend(
            stream, mats, gains_now, router_now, experts
        )
        probs_all = probs_all.reshape(tokens_all, -1)[:, :experts]
        chosen = spread(routes[layer_index], -1).reshape(tokens_all, 2)
        ranks = spread(priority[layer_index], tokens).reshape(tokens_all)
        target, first_f, second_f = slot_plan(chosen, ranks, experts, capacity, spacing)
        gate_values = jnp.stack(
            [jnp.sum(probs_all * first_f, axis=1), jnp.sum(probs_all * second_f, axis=1)], axis=1
        )
        pick_first = (target[:, 0:1] == slot_ids).astype(jnp.bfloat16)
        pick_second = (target[:, 1:2] == slot_ids).astype(jnp.bfloat16)
        pick_both = pick_first + pick_second
        dispatched = contract_rows(pick_both, normed_two.reshape(tokens_all, model_width))
        following = ()
        if layer_index + 1 < layers:
            following = (expert_in[layer_index + 1, 0].astype(jnp.bfloat16),)
        arrived, returned, wout_now, *gathered = experts_forward(
            dispatched.astype(jnp.bfloat16).reshape(experts, spacing, model_width),
            win_full[layer_index],
            expert_out[layer_index, 0].astype(jnp.bfloat16),
            peers_tensor,
            following,
        )
        win_full.extend(gathered)
        wout_full.append(wout_now)
        returned = returned.reshape(slots_all, model_width)
        rows_first = jnp.dot(pick_first, returned, preferred_element_type=jnp.float32)
        rows_second = jnp.dot(pick_second, returned, preferred_element_type=jnp.float32)
        output = (
            middle.reshape(tokens_all, model_width)
            + gate_values[:, 0:1] * rows_first
            + gate_values[:, 1:2] * rows_second
        )
        stash_list.append(
            (
                stream,
                mats,
                gains_now,
                router_now,
                mixed_heads,
                middle,
                probs_all,
                gate_values,
                first_f,
                second_f,
                pick_first,
                pick_second,
                pick_both,
                arrived,
                rows_first,
                rows_second,
            )
        )
        stream = output.reshape(images, image_rows, model_width)
    upstream = spread(cotangent, 0).reshape(tokens_all, model_width)
    grads_in, grads_out, grads_router, grads_gain, grads_win, grads_wout = ([], [], [], [], [], [])
    grads_shared = []
    for layer_index in reversed(range(layers)):
        (
            stream_in,
            mats,
            gains_now,
            router_now,
            mixed_heads,
            middle,
            probs_all,
            gate_values,
            first_f,
            second_f,
            pick_first,
            pick_second,
            pick_both,
            arrived,
            rows_first,
            rows_second,
        ) = stash_list[layer_index]
        gate_first = jnp.sum(upstream * rows_first, axis=1)
        gate_second = jnp.sum(upstream * rows_second, axis=1)
        scaled_first = (gate_values[:, 0:1] * upstream).astype(jnp.bfloat16)
        scaled_second = (gate_values[:, 1:2] * upstream).astype(jnp.bfloat16)
        grad_slots = (
            contract_rows(pick_first, scaled_first) + contract_rows(pick_second, scaled_second)
        ).astype(jnp.bfloat16)
        grad_dispatched, win_grad, wout_grad = experts_backward(
            grad_slots.reshape(experts, spacing, model_width),
            arrived,
            win_full[layer_index],
            wout_full[layer_index],
            peers_tensor,
        )
        grads_win.append(win_grad)
        grads_wout.append(wout_grad)
        grad_dispatched = grad_dispatched.reshape(slots_all, model_width)
        grad_normed = jnp.dot(pick_both, grad_dispatched, preferred_element_type=jnp.float32)
        grad_probs = first_f * gate_first[:, None] + second_f * gate_second[:, None]
        grad_logits = (
            probs_all * (grad_probs - jnp.sum(probs_all * grad_probs, axis=1, keepdims=True))
        ).astype(jnp.bfloat16)
        grad_logits = jnp.pad(grad_logits, ((0, 0), (0, router_now.shape[1] - experts)))
        shape = stream_in.shape
        down, mats_grad, router_grad, gain_grad = attend_back(
            upstream.reshape(shape),
            grad_normed.reshape(shape),
            grad_logits.reshape(images, image_rows, -1),
            stream_in,
            middle,
            mixed_heads,
            mats,
            gains_now,
            router_now,
            head_cols,
        )
        mats_grad = mats_grad.reshape(4, experts, row_share, head_cols).transpose(1, 0, 2, 3)
        router_grad = router_grad[:experts]
        gain_grad = gain_grad.reshape(2, experts, gain_share)
        smalls = jnp.concatenate(
            [router_grad, gain_grad.transpose(1, 0, 2).reshape(experts, -1)], axis=1
        )
        smalls = jnp.pad(smalls, ((0, 0), (0, -smalls.shape[1] % 2048)))
        grads_shared.append(
            jnp.concatenate(
                [mats_grad.reshape(experts, -1, 128), smalls.reshape(experts, -1, 128)], axis=1
            ).astype(jnp.bfloat16)
        )
        upstream = down.reshape(tokens_all, model_width)
    total_rows = grads_shared[0].shape[1]
    mat_rows = 4 * row_share * head_cols // 128
    shared_all = sum_shares(jnp.concatenate(grads_shared, axis=1))
    for order in range(layers):
        shared = shared_all[order * total_rows : (order + 1) * total_rows]
        mats_own = shared[:mat_rows].reshape(4, row_share, head_cols)
        small_own = shared[mat_rows:].reshape(-1)
        grads_in.append(mats_own[:3])
        grads_out.append(mats_own[3].T)
        grads_router.append(small_own[:model_width, None])
        grads_gain.append(
            small_own[model_width : model_width + 2 * gain_share].reshape(2, gain_share)
        )
    win_grad_all = jnp.stack(grads_win[::-1])[:, None]
    wout_grad_all = jnp.stack(grads_wout[::-1])[:, None]
    return (
        stream[:, :SEQ].reshape(tokens, model_width),
        upstream.reshape(stream.shape)[:, :SEQ].reshape(tokens, model_width),
        jnp.stack(grads_in[::-1]),
        jnp.stack(grads_out[::-1]),
        jnp.stack(grads_router[::-1]),
        jnp.stack(grads_gain[::-1]),
        win_grad_all,
        wout_grad_all,
    )


def solution(mesh):
    placed = (
        P("expert", None),
        P("expert", None),
        P(None, "expert", None),
        P(None, "expert"),
        P(None, None, "expert", "tensor"),
        P(None, "tensor", "expert"),
        P(None, None, "expert"),
        P(None, None, "expert"),
        P(None, "expert", None, "tensor"),
        P(None, "expert", "tensor", None),
    )
    return jax.shard_map(
        local,
        mesh=mesh,
        in_specs=placed,
        out_specs=(
            P("expert", None),
            P("expert", None),
            P(None, None, "expert", "tensor"),
            P(None, "tensor", "expert"),
            P(None, None, "expert"),
            P(None, None, "expert"),
            P(None, "expert", None, "tensor"),
            P(None, "expert", "tensor", None),
        ),
        check_vma=False,
    )
```

```python
import functools

import jax
import jax.numpy as jnp
from jax import lax
from jax.experimental import pallas as pl
from jax.experimental.pallas import tpu as pltpu
from jax.sharding import PartitionSpec as P

HEAD_DIM = 64
SEQ = 197


def gelu_exact(rows_in):
    return 0.5 * rows_in * (1.0 + lax.erf(rows_in * 0.7071067811865476))


def contract_rows(left_side, right_side):
    return lax.dot_general(
        left_side, right_side, (((0,), (0,)), ((), ())), preferred_element_type=jnp.float32
    )


def contract_last(left_side, right_side):
    return lax.dot_general(
        left_side, right_side, (((1,), (1,)), ((), ())), preferred_element_type=jnp.float32
    )


def gelu_parts(rows_in):
    half = 0.5 * (1.0 + lax.erf(rows_in * 0.7071067811865476))
    slope = half + rows_in * (jnp.exp(-0.5 * rows_in * rows_in) * 0.3989422804014327)
    return rows_in * half, slope


def greet(barrier, axis, index):
    pl.semaphore_signal(
        barrier, inc=1, device_id={axis: index}, device_id_type=pl.DeviceIdType.MESH
    )


def greet_axis(barrier, axis, me, peers):
    def one(step, carry):
        greet(barrier, axis, lax.rem(me + step, peers))
        return carry

    lax.fori_loop(1, peers, one, 0)


def send(source, landing, send_sem, recv_sem, axis, index):
    return pltpu.make_async_remote_copy(
        src_ref=source,
        dst_ref=landing,
        send_sem=send_sem,
        recv_sem=recv_sem,
        device_id={axis: index},
        device_id_type=pl.DeviceIdType.MESH,
    )


def send_chunk(source, landing, sends, arrivals, step, peer):
    return send(source, landing, sends.at[step], arrivals.at[step], "expert", peer)


def meet_peers(me, peers):
    barrier = pltpu.get_barrier_semaphore()
    greet_axis(barrier, "expert", me, peers)
    pl.semaphore_wait(barrier, peers - 1)


class Ring:
    def __init__(self, parts, place, own, sends, arrivals, both=True):
        self.parts, self.place, self.own = parts, place, own
        self.sends, self.arrivals = sends, arrivals
        self.side = lax.axis_index("tensor")
        self.hops = []
        for distance in range(1, parts // 2 + 1):
            if 2 * distance < parts:
                self.hops += [(distance, 1, None), (distance, -1, None)]
            elif both:
                self.hops += [(distance, 1, 0), (distance, -1, 1)]
            else:
                self.hops += [(distance, 1, None)]

    def wrap(self, index):
        return lax.rem(self.side + self.parts + index, self.parts)

    def outgoing(self, number):
        distance, way, half = self.hops[number]
        landing = self.place(self.wrap(-way * (distance - 1)), half)
        source = landing if distance > 1 else self.own(half)
        return send(
            source,
            landing,
            self.sends(number),
            self.arrivals(number),
            "tensor",
            self.wrap(way),
        )

    def incoming(self, number):
        distance, way, half = self.hops[number]
        landing = self.place(self.wrap(-way * distance), half)
        return send(
            landing,
            landing,
            self.sends(number),
            self.arrivals(number),
            "tensor",
            self.wrap(way),
        )

    def stage(self, wanted):
        for number, (distance, way, _) in enumerate(self.hops):
            if distance == wanted:
                for earlier, (before, same, _) in enumerate(self.hops):
                    if before == distance - 1 and same == way:
                        self.incoming(earlier).wait_recv()
                self.outgoing(number).start()

    def finish(self):
        kept = {(distance, way) for distance, way, _ in self.hops}
        for number, (distance, way, _) in enumerate(self.hops):
            self.outgoing(number).wait_send()
            if (distance + 1, way) not in kept:
                self.incoming(number).wait_recv()


def weight_ring(parts, kind, source, target, sends, arrivals):
    length = source.shape[1 - kind]

    def cut(ref, start, half):
        size = length if half is None else length // 2
        start = start + (0 if half is None else half * size)
        span = pl.ds(pl.multiple_of(start, size), size)
        return ref.at[:, span] if kind == 0 else ref.at[span, :]

    return Ring(
        parts,
        lambda owner, half: cut(target, owner * length, half),
        lambda half: cut(source, 0, half),
        lambda number: sends.at[number],
        lambda number: arrivals.at[number],
    )


def own_weight(kind, source, target, local_sem):
    length = source.shape[1 - kind]
    span = pl.ds(pl.multiple_of(lax.axis_index("tensor") * length, length), length)
    place = target.at[:, span] if kind == 0 else target.at[span, :]
    return pltpu.make_async_copy(source, place, local_sem)


def gather_kernel(
    experts,
    parts,
    small_ref,
    win_ref,
    whole,
    win_full,
    side_send,
    side_recv,
    ring_send,
    ring_recv,
    chip_send,
    chip_recv,
    twin_send,
    twin_recv,
    local_sem,
):
    me = lax.axis_index("expert")
    side = lax.axis_index("tensor")
    twin = me + 1 - 2 * lax.rem(me, 2)
    chips = experts // 2
    cols = small_ref.shape[2]
    barrier = pltpu.get_barrier_semaphore()
    greet_axis(barrier, "tensor", side, parts)
    greet(barrier, "expert", twin)
    for step in range(1, chips):
        greet(barrier, "expert", lax.rem(me + 2 * step, experts))
    pl.semaphore_wait(barrier, parts - 1 + chips)

    def place(index):
        return whole.at[:, me, :, pl.ds(pl.multiple_of(index * cols, cols), cols)]

    def side_copy(step, owner, target):
        return send(
            small_ref, place(owner), side_send.at[step], side_recv.at[step], "tensor", target
        )

    for step in range(1, parts):
        side_copy(step, side, lax.rem(side + step, parts)).start()
    ring = weight_ring(parts, 0, win_ref, win_full, ring_send, ring_recv)
    ring.stage(1)
    own_win = own_weight(0, win_ref, win_full, local_sem.at[0])
    own_small = pltpu.make_async_copy(small_ref, place(side), local_sem.at[1])
    own_win.start()
    own_small.start()
    own_small.wait()
    for step in range(1, parts):
        side_copy(step, lax.rem(side + parts - step, parts), side).wait_recv()

    def chip_copy(step, owner, target):
        return send_chunk(whole.at[:, owner], whole.at[:, owner], chip_send, chip_recv, step, target)

    def twin_copy(step, owner):
        return send_chunk(whole.at[:, owner], whole.at[:, owner], twin_send, twin_recv, step, twin)

    for step in range(1, chips):
        chip_copy(step, me, lax.rem(me + 2 * step, experts)).start()
    twin_copy(0, me).start()
    for distance in range(2, parts // 2 + 1):
        ring.stage(distance)
    for step in range(1, chips):
        owner = lax.rem(me + experts - 2 * step, experts)
        chip_copy(step, owner, owner).wait_recv()
        twin_copy(step, owner).start()
    for step in range(chips):
        twin_copy(step, lax.rem(twin + experts - 2 * step, experts)).wait_recv()
        twin_copy(step, lax.rem(me + experts - 2 * step, experts)).wait_send()
        if step:
            chip_copy(step, me, lax.rem(me + 2 * step, experts)).wait_send()
    for step in range(1, parts):
        side_copy(step, side, lax.rem(side + step, parts)).wait_send()
    ring.finish()
    own_win.wait()


def gather_start(small, win, experts, parts):
    count, rows, cols = small.shape
    depth, width = win.shape
    chips = experts // 2
    return pl.pallas_call(
        functools.partial(gather_kernel, experts, parts),
        out_shape=(
            jax.ShapeDtypeStruct((count, experts, rows, cols * parts), jnp.bfloat16),
            jax.ShapeDtypeStruct((depth, width * parts), jnp.bfloat16),
        ),
        in_specs=whole_in_vmem(2),
        out_specs=tuple(whole_in_vmem(2)),
        scratch_shapes=[pltpu.SemaphoreType.DMA((parts,))] * 4
        + [pltpu.SemaphoreType.DMA((chips,))] * 4
        + [pltpu.SemaphoreType.DMA((2,))],
        compiler_params=pltpu.CompilerParams(collective_id=3, has_side_effects=True),
    )(small, win)


def exchange_chunks(
    peers, make_rows, work, take_rows, out_rows, landed, results, back, sems, parts=1, rings=()
):
    out_send, out_recv, back_send, back_recv = sems
    me = lax.axis_index("expert")
    barrier = pltpu.get_barrier_semaphore()
    greet_axis(barrier, "expert", me, peers)
    if rings:
        greet_axis(barrier, "tensor", lax.axis_index("tensor"), parts)
    pl.semaphore_wait(barrier, peers - 1 + (parts - 1 if rings else 0))
    for ring in rings[:1]:
        ring.stage(1)

    def start_out(step):
        peer = lax.rem(me + step, peers)
        send_chunk(out_rows.at[peer], landed.at[me], out_send, out_recv, step, peer).start()

    def make_out(step, carry):
        peer = lax.rem(me + step, peers)
        out_rows[peer] = make_rows(peer)

        @pl.when(step > 1)
        def _():
            start_out(step - 1)

        return carry

    lax.fori_loop(1, peers, make_out, 0)
    landed[me] = make_rows(me)
    start_out(peers - 1)
    for distance in range(2, parts // 2 + 1):
        for ring in rings[:1]:
            ring.stage(distance)
    for ring in rings[:1]:
        ring.finish()
    for ring in rings[1:]:
        ring.stage(1)

    def one_chunk(step, carry):
        peer = lax.rem(me + peers - step, peers)

        @pl.when(step > 0)
        def _():
            send_chunk(
                out_rows.at[peer], landed.at[peer], out_send, out_recv, step, peer
            ).wait_recv()

        work(step, peer)

        @pl.when(step > 0)
        def _():
            send_chunk(results.at[step], back.at[me], back_send, back_recv, step, peer).start()

        return carry

    lax.fori_loop(0, peers, one_chunk, 0)
    for distance in range(2, parts // 2 + 1):
        for ring in rings[1:]:
            ring.stage(distance)
    back[me] = results[0]
    take_rows(me)

    def finish(step, carry):
        ahead = lax.rem(me + step, peers)
        last = send_chunk(results.at[step], back.at[ahead], back_send, back_recv, step, ahead)
        last.wait_recv()
        take_rows(ahead)
        send_chunk(out_rows.at[ahead], landed.at[me], out_send, out_recv, step, ahead).wait_send()
        last.wait_send()
        return carry

    lax.fori_loop(1, peers, finish, 0)
    for ring in rings[1:]:
        ring.finish()


def slot_hits(slots, start, shape, axis):
    return slots == start + lax.broadcasted_iota(jnp.int32, shape, axis)


def one_hot(hits):
    return jnp.where(hits, 1.0, 0.0).astype(jnp.bfloat16)


def forward_kernel(peers, parts, follow, *refs):
    rows_ref, across_ref, down_ref, win_ref = refs[:4]
    sources = refs[4 : 5 + follow]
    landed, first, second = refs[5 + follow : 8 + follow]
    targets = refs[8 + follow : 9 + 2 * follow]
    out_rows, back, results, total, *sems = refs[9 + 2 * follow :]
    wout_ref = targets[0]
    spacing = landed.shape[1]
    tokens = rows_ref.shape[0]
    kinds = (1, 0)[: 1 + follow]
    local_sem = sems[-1]
    rings, copies = [], []
    for order, kind in enumerate(kinds):
        pair = (sources[order], targets[order])
        rings.append(weight_ring(parts, kind, *pair, sems[4 + 2 * order], sems[5 + 2 * order]))
        copies.append(own_weight(kind, *pair, local_sem.at[order]))
    for copy in copies:
        copy.start()
    copies[0].wait()
    width = win_ref.shape[1] // parts
    first[...] = jnp.zeros_like(first)
    second[...] = jnp.zeros_like(second)

    def make_rows(peer):
        shape = (spacing, tokens)
        hits = [slot_hits(across_ref[k : k + 1], peer * spacing, shape, 0) for k in range(2)]
        return jnp.dot(
            one_hot(hits[0] | hits[1]), rows_ref[...], preferred_element_type=jnp.float32
        ).astype(jnp.bfloat16)

    def work(step, peer):
        chunk = landed[peer]
        for part in range(parts):
            cols = slice(part * width, (part + 1) * width)
            before = jnp.dot(chunk, win_ref[:, cols], preferred_element_type=jnp.float32)
            hidden = gelu_exact(before).astype(jnp.bfloat16)
            term = jnp.dot(hidden, wout_ref[cols, :], preferred_element_type=jnp.float32)
            if part == 0:
                total[...] = term
            elif part < parts - 1:
                total[...] += term
            else:
                results[step] = (total[...] + term).astype(jnp.bfloat16)

    def take_rows(slab):
        rows_back = back[slab]
        for k, kept in enumerate((first, second)):
            hits = slot_hits(down_ref[:, k : k + 1], slab * spacing, (tokens, spacing), 1)
            kept[...] += jnp.dot(
                one_hot(hits), rows_back, preferred_element_type=jnp.float32
            ).astype(jnp.bfloat16)

    exchange_chunks(
        peers,
        make_rows,
        work,
        take_rows,
        out_rows,
        landed,
        results,
        back,
        sems[:4],
        parts=parts,
        rings=rings,
    )
    for copy in copies[1:]:
        copy.wait()


def backward_kernel(
    peers,
    parts,
    first_ref,
    second_ref,
    across_ref,
    down_ref,
    arrived_ref,
    win_ref,
    wout_ref,
    token_grad,
    win_grad,
    wout_grad,
    out_rows,
    landed,
    back,
    results,
    total,
    hidden_all,
    before_all,
    *sems,
):
    width = win_ref.shape[1] // parts
    spacing = landed.shape[1]
    tokens = first_ref.shape[0]
    own = lax.axis_index("tensor") * width
    win_grad[...] = jnp.zeros_like(win_grad)
    wout_grad[...] = jnp.zeros_like(wout_grad)
    token_grad[...] = jnp.zeros_like(token_grad)

    def make_rows(peer):
        made = 0.0
        for k, rows_ref in enumerate((first_ref, second_ref)):
            hits = slot_hits(across_ref[k : k + 1], peer * spacing, (spacing, tokens), 0)
            made += jnp.dot(one_hot(hits), rows_ref[...], preferred_element_type=jnp.float32)
        return made.astype(jnp.bfloat16)

    def work(step, peer):
        chunk = arrived_ref[peer]
        grad_chunk = landed[peer]
        for part in range(parts):
            cols = slice(part * width, (part + 1) * width)
            before = jnp.dot(chunk, win_ref[:, cols], preferred_element_type=jnp.float32)
            value, slope = gelu_parts(before)
            grad_hidden = contract_last(grad_chunk, wout_ref[cols, :])
            grad_before = (grad_hidden * slope).astype(jnp.bfloat16)
            hidden_all[:, cols] = value.astype(jnp.bfloat16)
            before_all[:, cols] = grad_before
            term = contract_last(grad_before, win_ref[:, cols])
            if part == 0:
                total[...] = term
            elif part < parts - 1:
                total[...] += term
            else:
                results[step] = (total[...] + term).astype(jnp.bfloat16)
        mine = pl.ds(pl.multiple_of(own, width), width)
        wout_grad[...] += contract_rows(hidden_all[:, mine], grad_chunk)
        win_grad[...] += contract_rows(chunk, before_all[:, mine])

    def take_rows(slab):
        shape = (tokens, spacing)
        hits = [slot_hits(down_ref[:, k : k + 1], slab * spacing, shape, 1) for k in range(2)]
        token_grad[...] += jnp.dot(
            one_hot(hits[0] | hits[1]), back[slab], preferred_element_type=jnp.float32
        )

    exchange_chunks(peers, make_rows, work, take_rows, out_rows, landed, results, back, sems)


def sum_kernel(peers, rows_ref, sum_ref, landed, sends, arrivals):
    me = lax.axis_index("expert")
    meet_peers(me, peers)

    def start_out(step, carry):
        peer = lax.rem(me + step, peers)
        send_chunk(rows_ref.at[peer], landed.at[me], sends, arrivals, step, peer).start()
        return carry

    lax.fori_loop(1, peers, start_out, 0)
    landed[me] = rows_ref[me]

    def finish(step, carry):
        peer = lax.rem(me + peers - step, peers)
        one = send_chunk(rows_ref.at[peer], landed.at[peer], sends, arrivals, step, peer)
        one.wait_send()
        one.wait_recv()
        return carry

    lax.fori_loop(1, peers, finish, 0)
    sum_ref[...] = landed[0].astype(jnp.float32)

    def add_one(source, carry):
        sum_ref[...] += landed[source].astype(jnp.float32)
        return carry

    lax.fori_loop(1, peers, add_one, 0)


def sum_shares(rows):
    peers = rows.shape[0]
    return pl.pallas_call(
        functools.partial(sum_kernel, peers),
        out_shape=jax.ShapeDtypeStruct(rows.shape[1:], jnp.float32),
        in_specs=whole_in_vmem(1),
        out_specs=whole_in_vmem(1)[0],
        scratch_shapes=[pltpu.VMEM(rows.shape, rows.dtype)] + [pltpu.SemaphoreType.DMA((peers,))] * 2,
        compiler_params=pltpu.CompilerParams(collective_id=2, has_side_effects=True),
    )(rows)


def whole_in_vmem(count):
    return [pl.BlockSpec(memory_space=pltpu.VMEM)] * count


def exchange_sems(peers):
    return [pltpu.SemaphoreType.DMA((peers,)) for _ in range(4)]


def experts_forward(rows, slots, peers, spacing, win, wout_part, parts, following=()):
    tokens, width = rows.shape
    chunks = (peers, spacing, width)
    follow = len(following)
    wholes = (jax.ShapeDtypeStruct(win.shape[::-1], win.dtype),)
    wholes += (jax.ShapeDtypeStruct(win.shape, win.dtype),) * follow
    outs = tuple(
        jax.ShapeDtypeStruct(shape, jnp.bfloat16) for shape in (chunks, rows.shape, rows.shape)
    )
    return pl.pallas_call(
        functools.partial(forward_kernel, peers, parts, follow),
        out_shape=outs + wholes,
        in_specs=whole_in_vmem(5 + follow),
        out_specs=tuple(whole_in_vmem(4 + follow)),
        scratch_shapes=[pltpu.VMEM(chunks, jnp.bfloat16)] * 3
        + [pltpu.VMEM((spacing, width), jnp.float32)]
        + exchange_sems(peers)
        + [pltpu.SemaphoreType.DMA((parts,))] * (2 + 2 * follow)
        + [pltpu.SemaphoreType.DMA((2,))],
        compiler_params=pltpu.CompilerParams(
            collective_id=4 if follow else 0, has_side_effects=True
        ),
    )(rows, slots.T, slots, win, wout_part, *following)


def experts_backward(first, second, slots, arrived, win, wout, parts):
    peers, spacing, width = arrived.shape
    inner = win.shape[1]
    return pl.pallas_call(
        functools.partial(backward_kernel, peers, parts),
        out_shape=(
            jax.ShapeDtypeStruct(first.shape, jnp.float32),
            jax.ShapeDtypeStruct((width, inner // parts), jnp.float32),
            jax.ShapeDtypeStruct((inner // parts, width), jnp.float32),
        ),
        in_specs=whole_in_vmem(7),
        out_specs=tuple(whole_in_vmem(3)),
        scratch_shapes=[pltpu.VMEM(arrived.shape, jnp.bfloat16)] * 4
        + [pltpu.VMEM((spacing, width), jnp.float32)]
        + [pltpu.VMEM((spacing, inner), jnp.bfloat16)] * 2
        + exchange_sems(peers),
        compiler_params=pltpu.CompilerParams(collective_id=1, has_side_effects=True),
    )(first, second, slots.T, slots, arrived, win, wout)


def norm_parts(rows_in):
    centred = rows_in - jnp.mean(rows_in, axis=-1, keepdims=True)
    inverse = lax.rsqrt(jnp.mean(centred * centred, axis=-1, keepdims=True) + 1e-06)
    return centred * inverse, inverse


def norm_back(unit, inverse, gain_row, grad_rows):
    scaled = grad_rows * gain_row
    inner = scaled - jnp.mean(scaled, axis=-1, keepdims=True)
    return inverse * (inner - unit * jnp.mean(scaled * unit, axis=-1, keepdims=True))


def two_heads(rows):
    low_half = lax.broadcasted_iota(jnp.int32, rows.shape, 1) < HEAD_DIM
    none = jnp.zeros_like(rows)
    return jnp.concatenate([jnp.where(low_half, rows, none), jnp.where(low_half, none, rows)], 0)


def join_heads(stacked):
    rows = stacked.shape[0] // 2
    low_half = lax.broadcasted_iota(jnp.int32, (rows, stacked.shape[1]), 1) < HEAD_DIM
    return jnp.where(low_half, stacked[:rows], stacked[rows:])


def pair_attention(query_two, key_pair):
    scores = contract_last(query_two, key_pair) * (HEAD_DIM ** (-0.5))
    real_key = lax.broadcasted_iota(jnp.int32, scores.shape, 1) < SEQ
    scores = jnp.where(real_key, scores, -jnp.inf)
    weights = jnp.exp(scores - jnp.max(scores, axis=-1, keepdims=True))
    return weights * (1.0 / jnp.sum(weights, axis=-1, keepdims=True))


def project_qkv(normed, mats_ref):
    return [
        jnp.dot(normed, mats_ref[part], preferred_element_type=jnp.float32).astype(jnp.bfloat16)
        for part in range(3)
    ]


def attend_kernel(
    experts, stream_ref, mats_ref, gains_ref, router_ref, middle_ref, normed_ref, probs_ref, mixed_ref
):
    rows = stream_ref[0]
    normed = (norm_parts(rows)[0] * gains_ref[0:1]).astype(jnp.bfloat16)
    query, keys, values = project_qkv(normed, mats_ref)
    for pair in range(query.shape[1] // (2 * HEAD_DIM)):
        cols = slice(pair * 2 * HEAD_DIM, (pair + 1) * 2 * HEAD_DIM)
        attention = pair_attention(two_heads(query[:, cols]), keys[:, cols]).astype(jnp.bfloat16)
        mixed = jnp.dot(attention, values[:, cols], preferred_element_type=jnp.float32)
        mixed_ref[0, :, cols] = join_heads(mixed).astype(jnp.bfloat16)
    middle = rows + contract_last(mixed_ref[0], mats_ref[3])
    middle_ref[0] = middle
    normed_two = (norm_parts(middle)[0] * gains_ref[1:2]).astype(jnp.bfloat16)
    normed_ref[0] = normed_two
    logits = jnp.dot(normed_two, router_ref[...], preferred_element_type=jnp.float32)
    real = lax.broadcasted_iota(jnp.int32, logits.shape, 1) < experts
    logits = jnp.where(real, logits, -jnp.inf)
    odds = jnp.exp(logits - jnp.max(logits, axis=-1, keepdims=True))
    probs_ref[0] = odds * (1.0 / jnp.sum(odds, axis=-1, keepdims=True))


def attend_back_kernel(
    own_ref,
    upstream_ref,
    grad_ref,
    grad_logits_ref,
    stream_ref,
    middle_ref,
    mixed_ref,
    mats_ref,
    gains_ref,
    router_ref,
    down_ref,
    mats_grad,
    router_grad,
    gains_grad,
    triple,
):
    @pl.when(pl.program_id(0) == 0)
    def _():
        mats_grad[...] = jnp.zeros_like(mats_grad)
        router_grad[...] = jnp.zeros_like(router_grad)
        gains_grad[...] = jnp.zeros_like(gains_grad)

    head_cols = mats_grad.shape[2]
    mine = pl.ds(pl.multiple_of(own_ref[0] * head_cols, head_cols), head_cols)
    gain_one, gain_two = gains_ref[0:1], gains_ref[1:2]
    unit_two, inverse_two = norm_parts(middle_ref[0])
    grad_logits = grad_logits_ref[0]
    router_grad[...] += contract_rows(
        grad_logits, (unit_two * gain_two).astype(jnp.bfloat16)
    )
    grad_normed = grad_ref[0] + contract_last(grad_logits, router_ref[...])
    gains_grad[1:2] += jnp.sum(grad_normed * unit_two, axis=0, keepdims=True)
    grad_middle = upstream_ref[0] + norm_back(unit_two, inverse_two, gain_two, grad_normed)
    grad_branch = grad_middle.astype(jnp.bfloat16)
    mats_grad[3] += contract_rows(grad_branch, mixed_ref[0, :, mine])
    grad_mixed = jnp.dot(
        grad_branch, mats_ref[3], preferred_element_type=jnp.float32
    ).astype(jnp.bfloat16)
    unit_one, inverse_one = norm_parts(stream_ref[0])
    normed = (unit_one * gain_one).astype(jnp.bfloat16)
    query, keys, values = project_qkv(normed, mats_ref)
    scale = HEAD_DIM ** (-0.5)
    for pair in range(query.shape[1] // (2 * HEAD_DIM)):
        cols = slice(pair * 2 * HEAD_DIM, (pair + 1) * 2 * HEAD_DIM)
        query_two = two_heads(query[:, cols])
        attention = pair_attention(query_two, keys[:, cols])
        grad_two = two_heads(grad_mixed[:, cols])
        triple[2, :, cols] = contract_rows(attention.astype(jnp.bfloat16), grad_two).astype(
            jnp.bfloat16
        )
        grad_attention = contract_last(grad_two, values[:, cols])
        grad_scores = (
            attention
            * (grad_attention - jnp.sum(attention * grad_attention, axis=-1, keepdims=True))
        ).astype(jnp.bfloat16)
        grad_query = jnp.dot(grad_scores, keys[:, cols], preferred_element_type=jnp.float32)
        triple[0, :, cols] = (join_heads(grad_query) * scale).astype(jnp.bfloat16)
        triple[1, :, cols] = (contract_rows(grad_scores, query_two) * scale).astype(jnp.bfloat16)
    grad_one = contract_last(triple[0], mats_ref[0])
    for part in range(3):
        if part:
            grad_one += contract_last(triple[part], mats_ref[part])
        mats_grad[part] += contract_rows(normed, triple[part, :, mine])
    gains_grad[0:1] += jnp.sum(grad_one * unit_one, axis=0, keepdims=True)
    down_ref[0] = grad_middle + norm_back(unit_one, inverse_one, gain_one, grad_one)


def image_spec(array):
    return pl.BlockSpec((1,) + array.shape[1:], lambda image: (image, 0, 0))


def fixed_spec(array):
    return pl.BlockSpec(array.shape, lambda image: (0,) * len(array.shape))


def attend(stream, mats, gains, router, experts):
    images, rows, width = stream.shape
    outs = (
        jax.ShapeDtypeStruct(stream.shape, jnp.float32),
        jax.ShapeDtypeStruct(stream.shape, jnp.bfloat16),
        jax.ShapeDtypeStruct((images, rows, router.shape[1]), jnp.float32),
        jax.ShapeDtypeStruct((images, rows, mats.shape[2]), jnp.bfloat16),
    )
    return pl.pallas_call(
        functools.partial(attend_kernel, experts),
        grid=(images,),
        out_shape=outs,
        in_specs=[image_spec(stream), fixed_spec(mats), fixed_spec(gains), fixed_spec(router)],
        out_specs=tuple(image_spec(one) for one in outs),
    )(stream, mats, gains, router)


def attend_back(upstream, grad_normed, grad_logits, stream, middle, mixed, mats, gains, router, head_cols):
    images, rows, width = stream.shape
    own = lax.axis_index("tensor").astype(jnp.int32).reshape(1)
    sums = (
        jax.ShapeDtypeStruct((4, width, head_cols), jnp.float32),
        jax.ShapeDtypeStruct((router.shape[1], width), jnp.float32),
        jax.ShapeDtypeStruct(gains.shape, jnp.float32),
    )
    per_image = [upstream, grad_normed, grad_logits, stream, middle, mixed]
    fixed = [mats, gains, router]
    return pl.pallas_call(
        attend_back_kernel,
        grid=(images,),
        out_shape=(jax.ShapeDtypeStruct(stream.shape, jnp.float32),) + sums,
        in_specs=[pl.BlockSpec(memory_space=pltpu.SMEM)]
        + [image_spec(one) for one in per_image]
        + [fixed_spec(one) for one in fixed],
        out_specs=(image_spec(stream),) + tuple(fixed_spec(one) for one in sums),
        scratch_shapes=[pltpu.VMEM((3, rows, mats.shape[2]), jnp.bfloat16)],
    )(own, *per_image, *fixed)


def slot_plan(chosen, rank_rows, experts, capacity, spacing):
    columns = lax.broadcasted_iota(jnp.int32, (1, experts), 1)
    first_hot = (chosen[:, 0:1] == columns).astype(jnp.bfloat16)
    second = (chosen[:, 1:2] == columns).astype(jnp.bfloat16)
    earlier = (rank_rows[None, :] < rank_rows[:, None]).astype(jnp.bfloat16)
    count_first = jnp.dot(earlier, first_hot, preferred_element_type=jnp.float32)
    count_second = jnp.dot(earlier, second, preferred_element_type=jnp.float32)
    first_f = first_hot.astype(jnp.float32)
    second_f = second.astype(jnp.float32)
    filled = jnp.sum(first_f, axis=0, keepdims=True)
    slot_first = jnp.sum(count_first * first_f, axis=1)
    slot_second = jnp.sum((filled + count_second) * second_f, axis=1)
    slot_nums = jnp.stack([slot_first, slot_second], axis=1).astype(jnp.int32)
    target = jnp.where(slot_nums < capacity, chosen * spacing + slot_nums, experts * spacing)
    return (target, first_f, second_f)


def local(
    inputs,
    cotangent,
    routes,
    priority,
    attend_in,
    attend_out,
    router,
    norm_gains,
    expert_in,
    expert_out,
):
    experts = lax.axis_size("expert")
    tokens = inputs.shape[0]
    model_width = inputs.shape[1]
    images = tokens // SEQ
    head_cols = attend_in.shape[3]
    layers = attend_in.shape[0]
    capacity = max(2, (10 * tokens + 4 * experts - 1) // (4 * experts))
    peers_tensor = lax.axis_size("tensor")
    spacing = -(-capacity // 16) * 16
    row_share = attend_in.shape[2]
    gain_share = norm_gains.shape[2]
    image_rows = -(-SEQ // 16) * 16
    tokens_all = images * image_rows

    def spread(rows, fill):
        shaped = rows.reshape((images, SEQ) + rows.shape[1:])
        edges = ((0, 0), (0, image_rows - SEQ)) + ((0, 0),) * (rows.ndim - 1)
        return jnp.pad(shaped, edges, constant_values=fill)

    smalls = jnp.concatenate([router.reshape(-1), norm_gains.reshape(-1)])
    block = row_share * head_cols
    smalls = jnp.pad(smalls, (0, -smalls.shape[0] % block)).reshape(-1, row_share, head_cols)
    packed = jnp.concatenate(
        [
            jnp.concatenate([attend_in, attend_out.transpose(0, 2, 1)[:, None]], axis=1).reshape(
                -1, row_share, head_cols
            ),
            smalls,
        ]
    )
    whole, win_first = gather_start(
        packed.astype(jnp.bfloat16),
        expert_in[0, 0].astype(jnp.bfloat16),
        experts,
        peers_tensor,
    )
    whole = whole.reshape(whole.shape[0], model_width, model_width)
    small_rows = whole[4 * layers :, :, :head_cols].reshape(-1, experts, block)
    small_rows = small_rows.transpose(1, 0, 2).reshape(experts, -1)
    router_all = small_rows[:, : layers * model_width].reshape(experts, layers, model_width)
    gains_all = small_rows[:, layers * model_width :][:, : layers * 2 * gain_share]
    gains_all = gains_all.reshape(experts, layers, 2, gain_share).transpose(1, 2, 0, 3)
    gains_all = gains_all.reshape(layers, 2, model_width).astype(jnp.float32)
    router_all = jnp.pad(router_all.transpose(1, 2, 0), ((0, 0), (0, 0), (0, -experts % 128)))
    win_full, wout_full = [win_first], []
    stream = spread(inputs, 0)
    stash_list = []
    for layer_index in range(layers):
        mats = whole[4 * layer_index : 4 * layer_index + 4]
        gains_now = gains_all[layer_index]
        router_now = router_all[layer_index]
        middle, normed_two, probs_all, mixed_heads = attend(
            stream, mats, gains_now, router_now, experts
        )
        probs_all = probs_all.reshape(tokens_all, -1)[:, :experts]
        chosen = spread(routes[layer_index], -1).reshape(tokens_all, 2)
        ranks = spread(priority[layer_index], tokens).reshape(tokens_all)
        target, first_f, second_f = slot_plan(chosen, ranks, experts, capacity, spacing)
        gate_values = jnp.stack(
            [jnp.sum(probs_all * first_f, axis=1), jnp.sum(probs_all * second_f, axis=1)], axis=1
        )
        following = ()
        if layer_index + 1 < layers:
            following = (expert_in[layer_index + 1, 0].astype(jnp.bfloat16),)
        arrived, rows_first, rows_second, wout_now, *gathered = experts_forward(
            normed_two.reshape(tokens_all, model_width),
            target,
            experts,
            spacing,
            win_full[layer_index],
            expert_out[layer_index, 0].astype(jnp.bfloat16),
            peers_tensor,
            following,
        )
        win_full.extend(gathered)
        wout_full.append(wout_now)
        rows_first = rows_first.astype(jnp.float32)
        rows_second = rows_second.astype(jnp.float32)
        output = (
            middle.reshape(tokens_all, model_width)
            + gate_values[:, 0:1] * rows_first
            + gate_values[:, 1:2] * rows_second
        )
        stash_list.append(
            (
                stream,
                mats,
                gains_now,
                router_now,
                mixed_heads,
                middle,
                probs_all,
                gate_values,
                first_f,
                second_f,
                target,
                arrived,
                rows_first,
                rows_second,
            )
        )
        stream = output.reshape(images, image_rows, model_width)
    upstream = spread(cotangent, 0).reshape(tokens_all, model_width)
    grads_in, grads_out, grads_router, grads_gain, grads_win, grads_wout = ([], [], [], [], [], [])
    grads_shared = []
    for layer_index in reversed(range(layers)):
        (
            stream_in,
            mats,
            gains_now,
            router_now,
            mixed_heads,
            middle,
            probs_all,
            gate_values,
            first_f,
            second_f,
            target,
            arrived,
            rows_first,
            rows_second,
        ) = stash_list[layer_index]
        gate_first = jnp.sum(upstream * rows_first, axis=1)
        gate_second = jnp.sum(upstream * rows_second, axis=1)
        scaled_first = (gate_values[:, 0:1] * upstream).astype(jnp.bfloat16)
        scaled_second = (gate_values[:, 1:2] * upstream).astype(jnp.bfloat16)
        grad_normed, win_grad, wout_grad = experts_backward(
            scaled_first,
            scaled_second,
            target,
            arrived,
            win_full[layer_index],
            wout_full[layer_index],
            peers_tensor,
        )
        grads_win.append(win_grad)
        grads_wout.append(wout_grad)
        grad_probs = first_f * gate_first[:, None] + second_f * gate_second[:, None]
        grad_logits = (
            probs_all * (grad_probs - jnp.sum(probs_all * grad_probs, axis=1, keepdims=True))
        ).astype(jnp.bfloat16)
        grad_logits = jnp.pad(grad_logits, ((0, 0), (0, router_now.shape[1] - experts)))
        shape = stream_in.shape
        down, mats_grad, router_grad, gain_grad = attend_back(
            upstream.reshape(shape),
            grad_normed.reshape(shape),
            grad_logits.reshape(images, image_rows, -1),
            stream_in,
            middle,
            mixed_heads,
            mats,
            gains_now,
            router_now,
            head_cols,
        )
        mats_grad = mats_grad.reshape(4, experts, row_share, head_cols).transpose(1, 0, 2, 3)
        router_grad = router_grad[:experts]
        gain_grad = gain_grad.reshape(2, experts, gain_share)
        smalls = jnp.concatenate(
            [router_grad, gain_grad.transpose(1, 0, 2).reshape(experts, -1)], axis=1
        )
        smalls = jnp.pad(smalls, ((0, 0), (0, -smalls.shape[1] % 2048)))
        grads_shared.append(
            jnp.concatenate(
                [mats_grad.reshape(experts, -1, 128), smalls.reshape(experts, -1, 128)], axis=1
            ).astype(jnp.bfloat16)
        )
        upstream = down.reshape(tokens_all, model_width)
    total_rows = grads_shared[0].shape[1]
    mat_rows = 4 * row_share * head_cols // 128
    shared_all = sum_shares(jnp.concatenate(grads_shared, axis=1))
    for order in range(layers):
        shared = shared_all[order * total_rows : (order + 1) * total_rows]
        mats_own = shared[:mat_rows].reshape(4, row_share, head_cols)
        small_own = shared[mat_rows:].reshape(-1)
        grads_in.append(mats_own[:3])
        grads_out.append(mats_own[3].T)
        grads_router.append(small_own[:model_width, None])
        grads_gain.append(
            small_own[model_width : model_width + 2 * gain_share].reshape(2, gain_share)
        )
    win_grad_all = jnp.stack(grads_win[::-1])[:, None]
    wout_grad_all = jnp.stack(grads_wout[::-1])[:, None]
    return (
        stream[:, :SEQ].reshape(tokens, model_width),
        upstream.reshape(stream.shape)[:, :SEQ].reshape(tokens, model_width),
        jnp.stack(grads_in[::-1]),
        jnp.stack(grads_out[::-1]),
        jnp.stack(grads_router[::-1]),
        jnp.stack(grads_gain[::-1]),
        win_grad_all,
        wout_grad_all,
    )


def solution(mesh):
    placed = (
        P("expert", None),
        P("expert", None),
        P(None, "expert", None),
        P(None, "expert"),
        P(None, None, "expert", "tensor"),
        P(None, "tensor", "expert"),
        P(None, None, "expert"),
        P(None, None, "expert"),
        P(None, "expert", None, "tensor"),
        P(None, "expert", "tensor", None),
    )
    return jax.shard_map(
        local,
        mesh=mesh,
        in_specs=placed,
        out_specs=(
            P("expert", None),
            P("expert", None),
            P(None, None, "expert", "tensor"),
            P(None, "tensor", "expert"),
            P(None, None, "expert"),
            P(None, None, "expert"),
            P(None, "expert", None, "tensor"),
            P(None, "expert", "tensor", None),
        ),
        check_vma=False,
    )
```

```python
import functools

import jax
import jax.numpy as jnp
from jax import lax
from jax.experimental import pallas as pl
from jax.experimental.pallas import tpu as pltpu
from jax.sharding import PartitionSpec as P

HEAD_DIM = 64
SEQ = 197


def gelu_exact(rows_in):
    return 0.5 * rows_in * (1.0 + lax.erf(rows_in * 0.7071067811865476))


def contract_rows(left_side, right_side):
    return lax.dot_general(
        left_side, right_side, (((0,), (0,)), ((), ())), preferred_element_type=jnp.float32
    )


def contract_last(left_side, right_side):
    return lax.dot_general(
        left_side, right_side, (((1,), (1,)), ((), ())), preferred_element_type=jnp.float32
    )


def gelu_parts(rows_in):
    half = 0.5 * (1.0 + lax.erf(rows_in * 0.7071067811865476))
    slope = half + rows_in * (jnp.exp(-0.5 * rows_in * rows_in) * 0.3989422804014327)
    return rows_in * half, slope


def greet(barrier, axis, index):
    pl.semaphore_signal(
        barrier, inc=1, device_id={axis: index}, device_id_type=pl.DeviceIdType.MESH
    )


def greet_axis(barrier, axis, me, peers):
    def one(step, carry):
        greet(barrier, axis, lax.rem(me + step, peers))
        return carry

    lax.fori_loop(1, peers, one, 0)


def send(source, landing, send_sem, recv_sem, axis, index):
    return pltpu.make_async_remote_copy(
        src_ref=source,
        dst_ref=landing,
        send_sem=send_sem,
        recv_sem=recv_sem,
        device_id={axis: index},
        device_id_type=pl.DeviceIdType.MESH,
    )


def send_chunk(source, landing, sends, arrivals, step, peer):
    return send(source, landing, sends.at[step], arrivals.at[step], "expert", peer)


def meet_peers(me, peers):
    barrier = pltpu.get_barrier_semaphore()
    greet_axis(barrier, "expert", me, peers)
    pl.semaphore_wait(barrier, peers - 1)


class Ring:
    def __init__(self, parts, place, own, sends, arrivals, both=True):
        self.parts, self.place, self.own = parts, place, own
        self.sends, self.arrivals = sends, arrivals
        self.side = lax.axis_index("tensor")
        self.hops = []
        for distance in range(1, parts // 2 + 1):
            if 2 * distance < parts:
                self.hops += [(distance, 1, None), (distance, -1, None)]
            elif both:
                self.hops += [(distance, 1, 0), (distance, -1, 1)]
            else:
                self.hops += [(distance, 1, None)]

    def wrap(self, index):
        return lax.rem(self.side + self.parts + index, self.parts)

    def outgoing(self, number):
        distance, way, half = self.hops[number]
        landing = self.place(self.wrap(-way * (distance - 1)), half)
        source = landing if distance > 1 else self.own(half)
        return send(
            source,
            landing,
            self.sends(number),
            self.arrivals(number),
            "tensor",
            self.wrap(way),
        )

    def incoming(self, number):
        distance, way, half = self.hops[number]
        landing = self.place(self.wrap(-way * distance), half)
        return send(
            landing,
            landing,
            self.sends(number),
            self.arrivals(number),
            "tensor",
            self.wrap(way),
        )

    def stage(self, wanted):
        for number, (distance, way, _) in enumerate(self.hops):
            if distance == wanted:
                for earlier, (before, same, _) in enumerate(self.hops):
                    if before == distance - 1 and same == way:
                        self.incoming(earlier).wait_recv()
                self.outgoing(number).start()

    def finish(self):
        kept = {(distance, way) for distance, way, _ in self.hops}
        for number, (distance, way, _) in enumerate(self.hops):
            self.outgoing(number).wait_send()
            if (distance + 1, way) not in kept:
                self.incoming(number).wait_recv()


def weight_ring(parts, kind, source, target, sends, arrivals):
    length = source.shape[1 - kind]

    def cut(ref, start, half):
        size = length if half is None else length // 2
        start = start + (0 if half is None else half * size)
        span = pl.ds(pl.multiple_of(start, size), size)
        return ref.at[:, span] if kind == 0 else ref.at[span, :]

    return Ring(
        parts,
        lambda owner, half: cut(target, owner * length, half),
        lambda half: cut(source, 0, half),
        lambda number: sends.at[number],
        lambda number: arrivals.at[number],
    )


def own_weight(kind, source, target, local_sem):
    length = source.shape[1 - kind]
    span = pl.ds(pl.multiple_of(lax.axis_index("tensor") * length, length), length)
    place = target.at[:, span] if kind == 0 else target.at[span, :]
    return pltpu.make_async_copy(source, place, local_sem)


def gather_kernel(
    experts,
    parts,
    small_ref,
    win_ref,
    whole,
    win_full,
    side_send,
    side_recv,
    ring_send,
    ring_recv,
    chip_send,
    chip_recv,
    twin_send,
    twin_recv,
    local_sem,
):
    me = lax.axis_index("expert")
    side = lax.axis_index("tensor")
    twin = me + 1 - 2 * lax.rem(me, 2)
    chips = experts // 2
    cols = small_ref.shape[2]
    barrier = pltpu.get_barrier_semaphore()
    greet_axis(barrier, "tensor", side, parts)
    greet(barrier, "expert", twin)
    for step in range(1, chips):
        greet(barrier, "expert", lax.rem(me + 2 * step, experts))
    pl.semaphore_wait(barrier, parts - 1 + chips)

    def place(index):
        return whole.at[:, me, :, pl.ds(pl.multiple_of(index * cols, cols), cols)]

    def side_copy(step, owner, target):
        return send(
            small_ref, place(owner), side_send.at[step], side_recv.at[step], "tensor", target
        )

    for step in range(1, parts):
        side_copy(step, side, lax.rem(side + step, parts)).start()
    ring = weight_ring(parts, 0, win_ref, win_full, ring_send, ring_recv)
    ring.stage(1)
    own_win = own_weight(0, win_ref, win_full, local_sem.at[0])
    own_small = pltpu.make_async_copy(small_ref, place(side), local_sem.at[1])
    own_win.start()
    own_small.start()
    own_small.wait()
    for step in range(1, parts):
        side_copy(step, lax.rem(side + parts - step, parts), side).wait_recv()

    def chip_copy(step, owner, target):
        return send_chunk(whole.at[:, owner], whole.at[:, owner], chip_send, chip_recv, step, target)

    def twin_copy(step, owner):
        return send_chunk(whole.at[:, owner], whole.at[:, owner], twin_send, twin_recv, step, twin)

    for step in range(1, chips):
        chip_copy(step, me, lax.rem(me + 2 * step, experts)).start()
    twin_copy(0, me).start()
    for distance in range(2, parts // 2 + 1):
        ring.stage(distance)
    for step in range(1, chips):
        owner = lax.rem(me + experts - 2 * step, experts)
        chip_copy(step, owner, owner).wait_recv()
        twin_copy(step, owner).start()
    for step in range(chips):
        twin_copy(step, lax.rem(twin + experts - 2 * step, experts)).wait_recv()
        twin_copy(step, lax.rem(me + experts - 2 * step, experts)).wait_send()
        if step:
            chip_copy(step, me, lax.rem(me + 2 * step, experts)).wait_send()
    for step in range(1, parts):
        side_copy(step, side, lax.rem(side + step, parts)).wait_send()
    ring.finish()
    own_win.wait()


def gather_start(small, win, experts, parts):
    count, rows, cols = small.shape
    depth, width = win.shape
    chips = experts // 2
    return pl.pallas_call(
        functools.partial(gather_kernel, experts, parts),
        out_shape=(
            jax.ShapeDtypeStruct((count, experts, rows, cols * parts), jnp.bfloat16),
            jax.ShapeDtypeStruct((depth, width * parts), jnp.bfloat16),
        ),
        in_specs=whole_in_vmem(2),
        out_specs=tuple(whole_in_vmem(2)),
        scratch_shapes=[pltpu.SemaphoreType.DMA((parts,))] * 4
        + [pltpu.SemaphoreType.DMA((chips,))] * 4
        + [pltpu.SemaphoreType.DMA((2,))],
        compiler_params=pltpu.CompilerParams(collective_id=3, has_side_effects=True),
    )(small, win)


def exchange_chunks(
    peers,
    make_rows,
    work,
    take_rows,
    out_rows,
    landed,
    results,
    back,
    sems,
    parts=1,
    rings=(),
    early=None,
):
    out_send, out_recv, back_send, back_recv = sems
    me = lax.axis_index("expert")
    barrier = pltpu.get_barrier_semaphore()
    greet_axis(barrier, "expert", me, peers)
    if rings:
        greet_axis(barrier, "tensor", lax.axis_index("tensor"), parts)
    pl.semaphore_wait(barrier, peers - 1 + (parts - 1 if rings else 0))
    for ring in rings[:1]:
        ring.stage(1)

    def start_out(step):
        peer = lax.rem(me + step, peers)
        send_chunk(out_rows.at[peer], landed.at[me], out_send, out_recv, step, peer).start()

    def make_out(step, carry):
        peer = lax.rem(me + step, peers)
        out_rows[peer] = make_rows(peer)

        @pl.when(step > 1)
        def _():
            start_out(step - 1)

        return carry

    lax.fori_loop(1, peers, make_out, 0)
    landed[me] = make_rows(me)
    start_out(peers - 1)

    def await_chunk(step):
        peer = lax.rem(me + peers - step, peers)

        @pl.when(step > 0)
        def _():
            send_chunk(
                out_rows.at[peer], landed.at[peer], out_send, out_recv, step, peer
            ).wait_recv()

        return peer

    if early is not None:

        def early_chunk(step, carry):
            for distance in range(2, parts // 2 + 1):

                @pl.when(step == (5 * peers) // 8 + distance - 2)
                def _(distance=distance):
                    for ring in rings[:1]:
                        ring.stage(distance)

            early(step, await_chunk(step))
            return carry

        lax.fori_loop(0, peers, early_chunk, 0)
    for ring in rings[:1]:
        ring.finish()
    for ring in rings[1:]:
        ring.stage(1)

    def one_chunk(step, carry):
        if early is None:
            peer = await_chunk(step)
        else:
            peer = lax.rem(me + peers - step, peers)
        work(step, peer)

        @pl.when(step > 0)
        def _():
            send_chunk(results.at[step], back.at[me], back_send, back_recv, step, peer).start()

        return carry

    lax.fori_loop(0, peers, one_chunk, 0)
    for distance in range(2, parts // 2 + 1):
        for ring in rings[1:]:
            ring.stage(distance)
    back[me] = results[0]
    take_rows(me)

    def finish(step, carry):
        ahead = lax.rem(me + step, peers)
        last = send_chunk(results.at[step], back.at[ahead], back_send, back_recv, step, ahead)
        last.wait_recv()
        take_rows(ahead)
        send_chunk(out_rows.at[ahead], landed.at[me], out_send, out_recv, step, ahead).wait_send()
        last.wait_send()
        return carry

    lax.fori_loop(1, peers, finish, 0)
    for ring in rings[1:]:
        ring.finish()


def slot_hits(slots, start, shape, axis):
    return slots == start + lax.broadcasted_iota(jnp.int32, shape, axis)


def one_hot(hits):
    return jnp.where(hits, 1.0, 0.0).astype(jnp.bfloat16)


def forward_kernel(peers, parts, follow, *refs):
    rows_ref, across_ref, down_ref, win_ref = refs[:4]
    sources = refs[4 : 5 + follow]
    landed, first, second = refs[5 + follow : 8 + follow]
    targets = refs[8 + follow : 9 + 2 * follow]
    out_rows, back, results, hidden_all, *sems = refs[9 + 2 * follow :]
    wout_ref = targets[0]
    spacing = landed.shape[1]
    tokens = rows_ref.shape[0]
    kinds = (1, 0)[: 1 + follow]
    local_sem = sems[-1]
    rings, copies = [], []
    for order, kind in enumerate(kinds):
        pair = (sources[order], targets[order])
        rings.append(weight_ring(parts, kind, *pair, sems[4 + 2 * order], sems[5 + 2 * order]))
        copies.append(own_weight(kind, *pair, local_sem.at[order]))
    for copy in copies:
        copy.start()
    copies[0].wait()
    width = win_ref.shape[1] // parts
    first[...] = jnp.zeros_like(first)
    second[...] = jnp.zeros_like(second)

    def make_rows(peer):
        shape = (spacing, tokens)
        hits = [slot_hits(across_ref[k : k + 1], peer * spacing, shape, 0) for k in range(2)]
        return jnp.dot(
            one_hot(hits[0] | hits[1]), rows_ref[...], preferred_element_type=jnp.float32
        ).astype(jnp.bfloat16)

    def early(step, peer):
        chunk = landed[peer]
        for part in range(parts):
            cols = slice(part * width, (part + 1) * width)
            before = jnp.dot(chunk, win_ref[:, cols], preferred_element_type=jnp.float32)
            hidden_all[step, :, cols] = gelu_exact(before).astype(jnp.bfloat16)

    def work(step, peer):
        results[step] = jnp.dot(
            hidden_all[step], wout_ref[...], preferred_element_type=jnp.float32
        ).astype(jnp.bfloat16)

    def take_rows(slab):
        rows_back = back[slab]
        for k, kept in enumerate((first, second)):
            hits = slot_hits(down_ref[:, k : k + 1], slab * spacing, (tokens, spacing), 1)
            kept[...] += jnp.dot(
                one_hot(hits), rows_back, preferred_element_type=jnp.float32
            ).astype(jnp.bfloat16)

    exchange_chunks(
        peers,
        make_rows,
        work,
        take_rows,
        out_rows,
        landed,
        results,
        back,
        sems[:4],
        parts=parts,
        rings=rings,
        early=early,
    )
    for copy in copies[1:]:
        copy.wait()


def backward_kernel(
    peers,
    parts,
    first_ref,
    second_ref,
    across_ref,
    down_ref,
    arrived_ref,
    win_ref,
    wout_ref,
    token_grad,
    win_grad,
    wout_grad,
    out_rows,
    landed,
    back,
    results,
    total,
    hidden_all,
    before_all,
    *sems,
):
    width = win_ref.shape[1] // parts
    spacing = landed.shape[1]
    tokens = first_ref.shape[0]
    own = lax.axis_index("tensor") * width
    win_grad[...] = jnp.zeros_like(win_grad)
    wout_grad[...] = jnp.zeros_like(wout_grad)
    token_grad[...] = jnp.zeros_like(token_grad)

    def make_rows(peer):
        made = 0.0
        for k, rows_ref in enumerate((first_ref, second_ref)):
            hits = slot_hits(across_ref[k : k + 1], peer * spacing, (spacing, tokens), 0)
            made += jnp.dot(one_hot(hits), rows_ref[...], preferred_element_type=jnp.float32)
        return made.astype(jnp.bfloat16)

    def work(step, peer):
        chunk = arrived_ref[peer]
        grad_chunk = landed[peer]
        for part in range(parts):
            cols = slice(part * width, (part + 1) * width)
            before = jnp.dot(chunk, win_ref[:, cols], preferred_element_type=jnp.float32)
            value, slope = gelu_parts(before)
            grad_hidden = contract_last(grad_chunk, wout_ref[cols, :])
            grad_before = (grad_hidden * slope).astype(jnp.bfloat16)
            hidden_all[:, cols] = value.astype(jnp.bfloat16)
            before_all[:, cols] = grad_before
            term = contract_last(grad_before, win_ref[:, cols])
            if part == 0:
                total[...] = term
            elif part < parts - 1:
                total[...] += term
            else:
                results[step] = (total[...] + term).astype(jnp.bfloat16)
        mine = pl.ds(pl.multiple_of(own, width), width)
        wout_grad[...] += contract_rows(hidden_all[:, mine], grad_chunk)
        win_grad[...] += contract_rows(chunk, before_all[:, mine])

    def take_rows(slab):
        shape = (tokens, spacing)
        hits = [slot_hits(down_ref[:, k : k + 1], slab * spacing, shape, 1) for k in range(2)]
        token_grad[...] += jnp.dot(
            one_hot(hits[0] | hits[1]), back[slab], preferred_element_type=jnp.float32
        )

    exchange_chunks(peers, make_rows, work, take_rows, out_rows, landed, results, back, sems)


def sum_kernel(peers, rows_ref, sum_ref, landed, sends, arrivals):
    me = lax.axis_index("expert")
    meet_peers(me, peers)

    def start_out(step, carry):
        peer = lax.rem(me + step, peers)
        send_chunk(rows_ref.at[peer], landed.at[me], sends, arrivals, step, peer).start()
        return carry

    lax.fori_loop(1, peers, start_out, 0)
    landed[me] = rows_ref[me]

    def finish(step, carry):
        peer = lax.rem(me + peers - step, peers)
        one = send_chunk(rows_ref.at[peer], landed.at[peer], sends, arrivals, step, peer)
        one.wait_send()
        one.wait_recv()
        return carry

    lax.fori_loop(1, peers, finish, 0)
    sum_ref[...] = landed[0].astype(jnp.float32)

    def add_one(source, carry):
        sum_ref[...] += landed[source].astype(jnp.float32)
        return carry

    lax.fori_loop(1, peers, add_one, 0)


def sum_shares(rows):
    peers = rows.shape[0]
    return pl.pallas_call(
        functools.partial(sum_kernel, peers),
        out_shape=jax.ShapeDtypeStruct(rows.shape[1:], jnp.float32),
        in_specs=whole_in_vmem(1),
        out_specs=whole_in_vmem(1)[0],
        scratch_shapes=[pltpu.VMEM(rows.shape, rows.dtype)] + [pltpu.SemaphoreType.DMA((peers,))] * 2,
        compiler_params=pltpu.CompilerParams(collective_id=2, has_side_effects=True),
    )(rows)


def whole_in_vmem(count):
    return [pl.BlockSpec(memory_space=pltpu.VMEM)] * count


def exchange_sems(peers):
    return [pltpu.SemaphoreType.DMA((peers,)) for _ in range(4)]


def experts_forward(rows, slots, peers, spacing, win, wout_part, parts, following=()):
    tokens, width = rows.shape
    chunks = (peers, spacing, width)
    follow = len(following)
    wholes = (jax.ShapeDtypeStruct(win.shape[::-1], win.dtype),)
    wholes += (jax.ShapeDtypeStruct(win.shape, win.dtype),) * follow
    outs = tuple(
        jax.ShapeDtypeStruct(shape, jnp.bfloat16) for shape in (chunks, rows.shape, rows.shape)
    )
    return pl.pallas_call(
        functools.partial(forward_kernel, peers, parts, follow),
        out_shape=outs + wholes,
        in_specs=whole_in_vmem(5 + follow),
        out_specs=tuple(whole_in_vmem(4 + follow)),
        scratch_shapes=[pltpu.VMEM(chunks, jnp.bfloat16)] * 3
        + [pltpu.VMEM((peers, spacing, win.shape[1]), jnp.bfloat16)]
        + exchange_sems(peers)
        + [pltpu.SemaphoreType.DMA((parts,))] * (2 + 2 * follow)
        + [pltpu.SemaphoreType.DMA((2,))],
        compiler_params=pltpu.CompilerParams(
            collective_id=4 if follow else 0, has_side_effects=True
        ),
    )(rows, slots.T, slots, win, wout_part, *following)


def experts_backward(first, second, slots, arrived, win, wout, parts):
    peers, spacing, width = arrived.shape
    inner = win.shape[1]
    return pl.pallas_call(
        functools.partial(backward_kernel, peers, parts),
        out_shape=(
            jax.ShapeDtypeStruct(first.shape, jnp.float32),
            jax.ShapeDtypeStruct((width, inner // parts), jnp.float32),
            jax.ShapeDtypeStruct((inner // parts, width), jnp.float32),
        ),
        in_specs=whole_in_vmem(7),
        out_specs=tuple(whole_in_vmem(3)),
        scratch_shapes=[pltpu.VMEM(arrived.shape, jnp.bfloat16)] * 4
        + [pltpu.VMEM((spacing, width), jnp.float32)]
        + [pltpu.VMEM((spacing, inner), jnp.bfloat16)] * 2
        + exchange_sems(peers),
        compiler_params=pltpu.CompilerParams(collective_id=1, has_side_effects=True),
    )(first, second, slots.T, slots, arrived, win, wout)


def norm_parts(rows_in):
    centred = rows_in - jnp.mean(rows_in, axis=-1, keepdims=True)
    inverse = lax.rsqrt(jnp.mean(centred * centred, axis=-1, keepdims=True) + 1e-06)
    return centred * inverse, inverse


def norm_back(unit, inverse, gain_row, grad_rows):
    scaled = grad_rows * gain_row
    inner = scaled - jnp.mean(scaled, axis=-1, keepdims=True)
    return inverse * (inner - unit * jnp.mean(scaled * unit, axis=-1, keepdims=True))


def two_heads(rows):
    low_half = lax.broadcasted_iota(jnp.int32, rows.shape, 1) < HEAD_DIM
    none = jnp.zeros_like(rows)
    return jnp.concatenate([jnp.where(low_half, rows, none), jnp.where(low_half, none, rows)], 0)


def join_heads(stacked):
    rows = stacked.shape[0] // 2
    low_half = lax.broadcasted_iota(jnp.int32, (rows, stacked.shape[1]), 1) < HEAD_DIM
    return jnp.where(low_half, stacked[:rows], stacked[rows:])


def pair_attention(query_two, key_pair):
    scores = contract_last(query_two, key_pair) * (HEAD_DIM ** (-0.5))
    real_key = lax.broadcasted_iota(jnp.int32, scores.shape, 1) < SEQ
    scores = jnp.where(real_key, scores, -jnp.inf)
    weights = jnp.exp(scores - jnp.max(scores, axis=-1, keepdims=True))
    return weights * (1.0 / jnp.sum(weights, axis=-1, keepdims=True))


def project_qkv(normed, mats_ref):
    return [
        jnp.dot(normed, mats_ref[part], preferred_element_type=jnp.float32).astype(jnp.bfloat16)
        for part in range(3)
    ]


def attend_kernel(
    experts, stream_ref, mats_ref, gains_ref, router_ref, middle_ref, normed_ref, probs_ref, mixed_ref
):
    rows = stream_ref[0]
    normed = (norm_parts(rows)[0] * gains_ref[0:1]).astype(jnp.bfloat16)
    query, keys, values = project_qkv(normed, mats_ref)
    for pair in range(query.shape[1] // (2 * HEAD_DIM)):
        cols = slice(pair * 2 * HEAD_DIM, (pair + 1) * 2 * HEAD_DIM)
        attention = pair_attention(two_heads(query[:, cols]), keys[:, cols]).astype(jnp.bfloat16)
        mixed = jnp.dot(attention, values[:, cols], preferred_element_type=jnp.float32)
        mixed_ref[0, :, cols] = join_heads(mixed).astype(jnp.bfloat16)
    middle = rows + contract_last(mixed_ref[0], mats_ref[3])
    middle_ref[0] = middle
    normed_two = (norm_parts(middle)[0] * gains_ref[1:2]).astype(jnp.bfloat16)
    normed_ref[0] = normed_two
    logits = jnp.dot(normed_two, router_ref[...], preferred_element_type=jnp.float32)
    real = lax.broadcasted_iota(jnp.int32, logits.shape, 1) < experts
    logits = jnp.where(real, logits, -jnp.inf)
    odds = jnp.exp(logits - jnp.max(logits, axis=-1, keepdims=True))
    probs_ref[0] = odds * (1.0 / jnp.sum(odds, axis=-1, keepdims=True))


def attend_back_kernel(
    own_ref,
    upstream_ref,
    grad_ref,
    grad_logits_ref,
    stream_ref,
    middle_ref,
    mixed_ref,
    mats_ref,
    gains_ref,
    router_ref,
    down_ref,
    mats_grad,
    router_grad,
    gains_grad,
    triple,
):
    @pl.when(pl.program_id(0) == 0)
    def _():
        mats_grad[...] = jnp.zeros_like(mats_grad)
        router_grad[...] = jnp.zeros_like(router_grad)
        gains_grad[...] = jnp.zeros_like(gains_grad)

    head_cols = mats_grad.shape[2]
    mine = pl.ds(pl.multiple_of(own_ref[0] * head_cols, head_cols), head_cols)
    gain_one, gain_two = gains_ref[0:1], gains_ref[1:2]
    unit_two, inverse_two = norm_parts(middle_ref[0])
    grad_logits = grad_logits_ref[0]
    router_grad[...] += contract_rows(
        grad_logits, (unit_two * gain_two).astype(jnp.bfloat16)
    )
    grad_normed = grad_ref[0] + contract_last(grad_logits, router_ref[...])
    gains_grad[1:2] += jnp.sum(grad_normed * unit_two, axis=0, keepdims=True)
    grad_middle = upstream_ref[0] + norm_back(unit_two, inverse_two, gain_two, grad_normed)
    grad_branch = grad_middle.astype(jnp.bfloat16)
    mats_grad[3] += contract_rows(grad_branch, mixed_ref[0, :, mine])
    grad_mixed = jnp.dot(
        grad_branch, mats_ref[3], preferred_element_type=jnp.float32
    ).astype(jnp.bfloat16)
    unit_one, inverse_one = norm_parts(stream_ref[0])
    normed = (unit_one * gain_one).astype(jnp.bfloat16)
    query, keys, values = project_qkv(normed, mats_ref)
    scale = HEAD_DIM ** (-0.5)
    for pair in range(query.shape[1] // (2 * HEAD_DIM)):
        cols = slice(pair * 2 * HEAD_DIM, (pair + 1) * 2 * HEAD_DIM)
        query_two = two_heads(query[:, cols])
        attention = pair_attention(query_two, keys[:, cols])
        grad_two = two_heads(grad_mixed[:, cols])
        triple[2, :, cols] = contract_rows(attention.astype(jnp.bfloat16), grad_two).astype(
            jnp.bfloat16
        )
        grad_attention = contract_last(grad_two, values[:, cols])
        grad_scores = (
            attention
            * (grad_attention - jnp.sum(attention * grad_attention, axis=-1, keepdims=True))
        ).astype(jnp.bfloat16)
        grad_query = jnp.dot(grad_scores, keys[:, cols], preferred_element_type=jnp.float32)
        triple[0, :, cols] = (join_heads(grad_query) * scale).astype(jnp.bfloat16)
        triple[1, :, cols] = (contract_rows(grad_scores, query_two) * scale).astype(jnp.bfloat16)
    grad_one = contract_last(triple[0], mats_ref[0])
    for part in range(3):
        if part:
            grad_one += contract_last(triple[part], mats_ref[part])
        mats_grad[part] += contract_rows(normed, triple[part, :, mine])
    gains_grad[0:1] += jnp.sum(grad_one * unit_one, axis=0, keepdims=True)
    down_ref[0] = grad_middle + norm_back(unit_one, inverse_one, gain_one, grad_one)


def image_spec(array):
    return pl.BlockSpec((1,) + array.shape[1:], lambda image: (image, 0, 0))


def fixed_spec(array):
    return pl.BlockSpec(array.shape, lambda image: (0,) * len(array.shape))


def attend(stream, mats, gains, router, experts):
    images, rows, width = stream.shape
    outs = (
        jax.ShapeDtypeStruct(stream.shape, jnp.float32),
        jax.ShapeDtypeStruct(stream.shape, jnp.bfloat16),
        jax.ShapeDtypeStruct((images, rows, router.shape[1]), jnp.float32),
        jax.ShapeDtypeStruct((images, rows, mats.shape[2]), jnp.bfloat16),
    )
    return pl.pallas_call(
        functools.partial(attend_kernel, experts),
        grid=(images,),
        out_shape=outs,
        in_specs=[image_spec(stream), fixed_spec(mats), fixed_spec(gains), fixed_spec(router)],
        out_specs=tuple(image_spec(one) for one in outs),
    )(stream, mats, gains, router)


def attend_back(upstream, grad_normed, grad_logits, stream, middle, mixed, mats, gains, router, head_cols):
    images, rows, width = stream.shape
    own = lax.axis_index("tensor").astype(jnp.int32).reshape(1)
    sums = (
        jax.ShapeDtypeStruct((4, width, head_cols), jnp.float32),
        jax.ShapeDtypeStruct((router.shape[1], width), jnp.float32),
        jax.ShapeDtypeStruct(gains.shape, jnp.float32),
    )
    per_image = [upstream, grad_normed, grad_logits, stream, middle, mixed]
    fixed = [mats, gains, router]
    return pl.pallas_call(
        attend_back_kernel,
        grid=(images,),
        out_shape=(jax.ShapeDtypeStruct(stream.shape, jnp.float32),) + sums,
        in_specs=[pl.BlockSpec(memory_space=pltpu.SMEM)]
        + [image_spec(one) for one in per_image]
        + [fixed_spec(one) for one in fixed],
        out_specs=(image_spec(stream),) + tuple(fixed_spec(one) for one in sums),
        scratch_shapes=[pltpu.VMEM((3, rows, mats.shape[2]), jnp.bfloat16)],
    )(own, *per_image, *fixed)


def slot_plan(chosen, rank_rows, experts, capacity, spacing):
    columns = lax.broadcasted_iota(jnp.int32, (1, experts), 1)
    first_hot = (chosen[:, 0:1] == columns).astype(jnp.bfloat16)
    second = (chosen[:, 1:2] == columns).astype(jnp.bfloat16)
    earlier = (rank_rows[None, :] < rank_rows[:, None]).astype(jnp.bfloat16)
    count_first = jnp.dot(earlier, first_hot, preferred_element_type=jnp.float32)
    count_second = jnp.dot(earlier, second, preferred_element_type=jnp.float32)
    first_f = first_hot.astype(jnp.float32)
    second_f = second.astype(jnp.float32)
    filled = jnp.sum(first_f, axis=0, keepdims=True)
    slot_first = jnp.sum(count_first * first_f, axis=1)
    slot_second = jnp.sum((filled + count_second) * second_f, axis=1)
    slot_nums = jnp.stack([slot_first, slot_second], axis=1).astype(jnp.int32)
    target = jnp.where(slot_nums < capacity, chosen * spacing + slot_nums, experts * spacing)
    return (target, first_f, second_f)


def local(
    inputs,
    cotangent,
    routes,
    priority,
    attend_in,
    attend_out,
    router,
    norm_gains,
    expert_in,
    expert_out,
):
    experts = lax.axis_size("expert")
    tokens = inputs.shape[0]
    model_width = inputs.shape[1]
    images = tokens // SEQ
    head_cols = attend_in.shape[3]
    layers = attend_in.shape[0]
    capacity = max(2, (10 * tokens + 4 * experts - 1) // (4 * experts))
    peers_tensor = lax.axis_size("tensor")
    spacing = -(-capacity // 16) * 16
    row_share = attend_in.shape[2]
    gain_share = norm_gains.shape[2]
    image_rows = -(-SEQ // 16) * 16
    tokens_all = images * image_rows

    def spread(rows, fill):
        shaped = rows.reshape((images, SEQ) + rows.shape[1:])
        edges = ((0, 0), (0, image_rows - SEQ)) + ((0, 0),) * (rows.ndim - 1)
        return jnp.pad(shaped, edges, constant_values=fill)

    smalls = jnp.concatenate([router.reshape(-1), norm_gains.reshape(-1)])
    block = row_share * head_cols
    smalls = jnp.pad(smalls, (0, -smalls.shape[0] % block)).reshape(-1, row_share, head_cols)
    packed = jnp.concatenate(
        [
            jnp.concatenate([attend_in, attend_out.transpose(0, 2, 1)[:, None]], axis=1).reshape(
                -1, row_share, head_cols
            ),
            smalls,
        ]
    )
    whole, win_first = gather_start(
        packed.astype(jnp.bfloat16),
        expert_in[0, 0].astype(jnp.bfloat16),
        experts,
        peers_tensor,
    )
    whole = whole.reshape(whole.shape[0], model_width, model_width)
    small_rows = whole[4 * layers :, :, :head_cols].reshape(-1, experts, block)
    small_rows = small_rows.transpose(1, 0, 2).reshape(experts, -1)
    router_all = small_rows[:, : layers * model_width].reshape(experts, layers, model_width)
    gains_all = small_rows[:, layers * model_width :][:, : layers * 2 * gain_share]
    gains_all = gains_all.reshape(experts, layers, 2, gain_share).transpose(1, 2, 0, 3)
    gains_all = gains_all.reshape(layers, 2, model_width).astype(jnp.float32)
    router_all = jnp.pad(router_all.transpose(1, 2, 0), ((0, 0), (0, 0), (0, -experts % 128)))
    win_full, wout_full = [win_first], []
    stream = spread(inputs, 0)
    stash_list = []
    for layer_index in range(layers):
        mats = whole[4 * layer_index : 4 * layer_index + 4]
        gains_now = gains_all[layer_index]
        router_now = router_all[layer_index]
        middle, normed_two, probs_all, mixed_heads = attend(
            stream, mats, gains_now, router_now, experts
        )
        probs_all = probs_all.reshape(tokens_all, -1)[:, :experts]
        chosen = spread(routes[layer_index], -1).reshape(tokens_all, 2)
        ranks = spread(priority[layer_index], tokens).reshape(tokens_all)
        target, first_f, second_f = slot_plan(chosen, ranks, experts, capacity, spacing)
        gate_values = jnp.stack(
            [jnp.sum(probs_all * first_f, axis=1), jnp.sum(probs_all * second_f, axis=1)], axis=1
        )
        following = ()
        if layer_index + 1 < layers:
            following = (expert_in[layer_index + 1, 0].astype(jnp.bfloat16),)
        arrived, rows_first, rows_second, wout_now, *gathered = experts_forward(
            normed_two.reshape(tokens_all, model_width),
            target,
            experts,
            spacing,
            win_full[layer_index],
            expert_out[layer_index, 0].astype(jnp.bfloat16),
            peers_tensor,
            following,
        )
        win_full.extend(gathered)
        wout_full.append(wout_now)
        rows_first = rows_first.astype(jnp.float32)
        rows_second = rows_second.astype(jnp.float32)
        output = (
            middle.reshape(tokens_all, model_width)
            + gate_values[:, 0:1] * rows_first
            + gate_values[:, 1:2] * rows_second
        )
        stash_list.append(
            (
                stream,
                mats,
                gains_now,
                router_now,
                mixed_heads,
                middle,
                probs_all,
                gate_values,
                first_f,
                second_f,
                target,
                arrived,
                rows_first,
                rows_second,
            )
        )
        stream = output.reshape(images, image_rows, model_width)
    upstream = spread(cotangent, 0).reshape(tokens_all, model_width)
    grads_in, grads_out, grads_router, grads_gain, grads_win, grads_wout = ([], [], [], [], [], [])
    grads_shared = []
    for layer_index in reversed(range(layers)):
        (
            stream_in,
            mats,
            gains_now,
            router_now,
            mixed_heads,
            middle,
            probs_all,
            gate_values,
            first_f,
            second_f,
            target,
            arrived,
            rows_first,
            rows_second,
        ) = stash_list[layer_index]
        gate_first = jnp.sum(upstream * rows_first, axis=1)
        gate_second = jnp.sum(upstream * rows_second, axis=1)
        scaled_first = (gate_values[:, 0:1] * upstream).astype(jnp.bfloat16)
        scaled_second = (gate_values[:, 1:2] * upstream).astype(jnp.bfloat16)
        grad_normed, win_grad, wout_grad = experts_backward(
            scaled_first,
            scaled_second,
            target,
            arrived,
            win_full[layer_index],
            wout_full[layer_index],
            peers_tensor,
        )
        grads_win.append(win_grad)
        grads_wout.append(wout_grad)
        grad_probs = first_f * gate_first[:, None] + second_f * gate_second[:, None]
        grad_logits = (
            probs_all * (grad_probs - jnp.sum(probs_all * grad_probs, axis=1, keepdims=True))
        ).astype(jnp.bfloat16)
        grad_logits = jnp.pad(grad_logits, ((0, 0), (0, router_now.shape[1] - experts)))
        shape = stream_in.shape
        down, mats_grad, router_grad, gain_grad = attend_back(
            upstream.reshape(shape),
            grad_normed.reshape(shape),
            grad_logits.reshape(images, image_rows, -1),
            stream_in,
            middle,
            mixed_heads,
            mats,
            gains_now,
            router_now,
            head_cols,
        )
        mats_grad = mats_grad.reshape(4, experts, row_share, head_cols).transpose(1, 0, 2, 3)
        router_grad = router_grad[:experts]
        gain_grad = gain_grad.reshape(2, experts, gain_share)
        smalls = jnp.concatenate(
            [router_grad, gain_grad.transpose(1, 0, 2).reshape(experts, -1)], axis=1
        )
        smalls = jnp.pad(smalls, ((0, 0), (0, -smalls.shape[1] % 2048)))
        grads_shared.append(
            jnp.concatenate(
                [mats_grad.reshape(experts, -1, 128), smalls.reshape(experts, -1, 128)], axis=1
            ).astype(jnp.bfloat16)
        )
        upstream = down.reshape(tokens_all, model_width)
    total_rows = grads_shared[0].shape[1]
    mat_rows = 4 * row_share * head_cols // 128
    shared_all = sum_shares(jnp.concatenate(grads_shared, axis=1))
    for order in range(layers):
        shared = shared_all[order * total_rows : (order + 1) * total_rows]
        mats_own = shared[:mat_rows].reshape(4, row_share, head_cols)
        small_own = shared[mat_rows:].reshape(-1)
        grads_in.append(mats_own[:3])
        grads_out.append(mats_own[3].T)
        grads_router.append(small_own[:model_width, None])
        grads_gain.append(
            small_own[model_width : model_width + 2 * gain_share].reshape(2, gain_share)
        )
    win_grad_all = jnp.stack(grads_win[::-1])[:, None]
    wout_grad_all = jnp.stack(grads_wout[::-1])[:, None]
    return (
        stream[:, :SEQ].reshape(tokens, model_width),
        upstream.reshape(stream.shape)[:, :SEQ].reshape(tokens, model_width),
        jnp.stack(grads_in[::-1]),
        jnp.stack(grads_out[::-1]),
        jnp.stack(grads_router[::-1]),
        jnp.stack(grads_gain[::-1]),
        win_grad_all,
        wout_grad_all,
    )


def solution(mesh):
    placed = (
        P("expert", None),
        P("expert", None),
        P(None, "expert", None),
        P(None, "expert"),
        P(None, None, "expert", "tensor"),
        P(None, "tensor", "expert"),
        P(None, None, "expert"),
        P(None, None, "expert"),
        P(None, "expert", None, "tensor"),
        P(None, "expert", "tensor", None),
    )
    return jax.shard_map(
        local,
        mesh=mesh,
        in_specs=placed,
        out_specs=(
            P("expert", None),
            P("expert", None),
            P(None, None, "expert", "tensor"),
            P(None, "tensor", "expert"),
            P(None, None, "expert"),
            P(None, None, "expert"),
            P(None, "expert", None, "tensor"),
            P(None, "expert", "tensor", None),
        ),
        check_vma=False,
    )
```

```python
import functools

import jax
import jax.numpy as jnp
from jax import lax
from jax.experimental import pallas as pl
from jax.experimental.pallas import tpu as pltpu
from jax.sharding import PartitionSpec as P

HEAD_DIM = 64
SEQ = 197


def gelu_exact(rows_in):
    return 0.5 * rows_in * (1.0 + lax.erf(rows_in * 0.7071067811865476))


def contract_rows(left_side, right_side):
    return lax.dot_general(
        left_side, right_side, (((0,), (0,)), ((), ())), preferred_element_type=jnp.float32
    )


def contract_last(left_side, right_side):
    return lax.dot_general(
        left_side, right_side, (((1,), (1,)), ((), ())), preferred_element_type=jnp.float32
    )


def gelu_parts(rows_in):
    half = 0.5 * (1.0 + lax.erf(rows_in * 0.7071067811865476))
    slope = half + rows_in * (jnp.exp(-0.5 * rows_in * rows_in) * 0.3989422804014327)
    return rows_in * half, slope


def greet(barrier, axis, index):
    pl.semaphore_signal(
        barrier, inc=1, device_id={axis: index}, device_id_type=pl.DeviceIdType.MESH
    )


def greet_axis(barrier, axis, me, peers):
    def one(step, carry):
        greet(barrier, axis, lax.rem(me + step, peers))
        return carry

    lax.fori_loop(1, peers, one, 0)


def send(source, landing, send_sem, recv_sem, axis, index):
    return pltpu.make_async_remote_copy(
        src_ref=source,
        dst_ref=landing,
        send_sem=send_sem,
        recv_sem=recv_sem,
        device_id={axis: index},
        device_id_type=pl.DeviceIdType.MESH,
    )


def send_chunk(source, landing, sends, arrivals, step, peer):
    return send(source, landing, sends.at[step], arrivals.at[step], "expert", peer)


def meet_peers(me, peers):
    barrier = pltpu.get_barrier_semaphore()
    greet_axis(barrier, "expert", me, peers)
    pl.semaphore_wait(barrier, peers - 1)


class Ring:
    def __init__(self, parts, place, own, sends, arrivals, both=True):
        self.parts, self.place, self.own = parts, place, own
        self.sends, self.arrivals = sends, arrivals
        self.side = lax.axis_index("tensor")
        self.hops = []
        for distance in range(1, parts // 2 + 1):
            if 2 * distance < parts:
                self.hops += [(distance, 1, None), (distance, -1, None)]
            elif both:
                self.hops += [(distance, 1, 0), (distance, -1, 1)]
            else:
                self.hops += [(distance, 1, None)]

    def wrap(self, index):
        return lax.rem(self.side + self.parts + index, self.parts)

    def outgoing(self, number):
        distance, way, half = self.hops[number]
        landing = self.place(self.wrap(-way * (distance - 1)), half)
        source = landing if distance > 1 else self.own(half)
        return send(
            source,
            landing,
            self.sends(number),
            self.arrivals(number),
            "tensor",
            self.wrap(way),
        )

    def incoming(self, number):
        distance, way, half = self.hops[number]
        landing = self.place(self.wrap(-way * distance), half)
        return send(
            landing,
            landing,
            self.sends(number),
            self.arrivals(number),
            "tensor",
            self.wrap(way),
        )

    def stage(self, wanted):
        for number, (distance, way, _) in enumerate(self.hops):
            if distance == wanted:
                for earlier, (before, same, _) in enumerate(self.hops):
                    if before == distance - 1 and same == way:
                        self.incoming(earlier).wait_recv()
                self.outgoing(number).start()

    def finish(self):
        kept = {(distance, way) for distance, way, _ in self.hops}
        for number, (distance, way, _) in enumerate(self.hops):
            self.outgoing(number).wait_send()
            if (distance + 1, way) not in kept:
                self.incoming(number).wait_recv()


def weight_ring(parts, kind, source, target, sends, arrivals):
    length = source.shape[1 - kind]

    def cut(ref, start, half):
        size = length if half is None else length // 2
        start = start + (0 if half is None else half * size)
        span = pl.ds(pl.multiple_of(start, size), size)
        return ref.at[:, span] if kind == 0 else ref.at[span, :]

    return Ring(
        parts,
        lambda owner, half: cut(target, owner * length, half),
        lambda half: cut(source, 0, half),
        lambda number: sends.at[number],
        lambda number: arrivals.at[number],
    )


def own_weight(kind, source, target, local_sem):
    length = source.shape[1 - kind]
    span = pl.ds(pl.multiple_of(lax.axis_index("tensor") * length, length), length)
    place = target.at[:, span] if kind == 0 else target.at[span, :]
    return pltpu.make_async_copy(source, place, local_sem)


def gather_kernel(
    experts,
    parts,
    small_ref,
    win_ref,
    whole,
    win_full,
    side_send,
    side_recv,
    ring_send,
    ring_recv,
    chip_send,
    chip_recv,
    twin_send,
    twin_recv,
    local_sem,
):
    me = lax.axis_index("expert")
    side = lax.axis_index("tensor")
    twin = me + 1 - 2 * lax.rem(me, 2)
    chips = experts // 2
    cols = small_ref.shape[2]
    barrier = pltpu.get_barrier_semaphore()
    greet_axis(barrier, "tensor", side, parts)
    greet(barrier, "expert", twin)
    for step in range(1, chips):
        greet(barrier, "expert", lax.rem(me + 2 * step, experts))
    pl.semaphore_wait(barrier, parts - 1 + chips)

    def place(index):
        return whole.at[:, me, :, pl.ds(pl.multiple_of(index * cols, cols), cols)]

    def side_copy(step, owner, target):
        return send(
            small_ref, place(owner), side_send.at[step], side_recv.at[step], "tensor", target
        )

    for step in range(1, parts):
        side_copy(step, side, lax.rem(side + step, parts)).start()
    ring = weight_ring(parts, 0, win_ref, win_full, ring_send, ring_recv)
    ring.stage(1)
    own_win = own_weight(0, win_ref, win_full, local_sem.at[0])
    own_small = pltpu.make_async_copy(small_ref, place(side), local_sem.at[1])
    own_win.start()
    own_small.start()
    own_small.wait()
    for step in range(1, parts):
        side_copy(step, lax.rem(side + parts - step, parts), side).wait_recv()

    def chip_copy(step, owner, target):
        return send_chunk(whole.at[:, owner], whole.at[:, owner], chip_send, chip_recv, step, target)

    def twin_copy(step, owner):
        return send_chunk(whole.at[:, owner], whole.at[:, owner], twin_send, twin_recv, step, twin)

    for step in range(1, chips):
        chip_copy(step, me, lax.rem(me + 2 * step, experts)).start()
    twin_copy(0, me).start()
    for distance in range(2, parts // 2 + 1):
        ring.stage(distance)
    for step in range(1, chips):
        owner = lax.rem(me + experts - 2 * step, experts)
        chip_copy(step, owner, owner).wait_recv()
        twin_copy(step, owner).start()
    for step in range(chips):
        twin_copy(step, lax.rem(twin + experts - 2 * step, experts)).wait_recv()
        twin_copy(step, lax.rem(me + experts - 2 * step, experts)).wait_send()
        if step:
            chip_copy(step, me, lax.rem(me + 2 * step, experts)).wait_send()
    for step in range(1, parts):
        side_copy(step, side, lax.rem(side + step, parts)).wait_send()
    ring.finish()
    own_win.wait()


def gather_start(small, win, experts, parts):
    count, rows, cols = small.shape
    depth, width = win.shape
    chips = experts // 2
    return pl.pallas_call(
        functools.partial(gather_kernel, experts, parts),
        out_shape=(
            jax.ShapeDtypeStruct((count, experts, rows, cols * parts), jnp.bfloat16),
            jax.ShapeDtypeStruct((depth, width * parts), jnp.bfloat16),
        ),
        in_specs=whole_in_vmem(2),
        out_specs=tuple(whole_in_vmem(2)),
        scratch_shapes=[pltpu.SemaphoreType.DMA((parts,))] * 4
        + [pltpu.SemaphoreType.DMA((chips,))] * 4
        + [pltpu.SemaphoreType.DMA((2,))],
        compiler_params=pltpu.CompilerParams(collective_id=3, has_side_effects=True),
    )(small, win)


def exchange_chunks(
    peers,
    make_rows,
    work,
    take_rows,
    out_rows,
    landed,
    results,
    back,
    sems,
    parts=1,
    rings=(),
    early=None,
):
    out_send, out_recv, back_send, back_recv = sems
    me = lax.axis_index("expert")
    barrier = pltpu.get_barrier_semaphore()
    greet_axis(barrier, "expert", me, peers)
    if rings:
        greet_axis(barrier, "tensor", lax.axis_index("tensor"), parts)
    pl.semaphore_wait(barrier, peers - 1 + (parts - 1 if rings else 0))
    for ring in rings[:1]:
        ring.stage(1)

    def start_out(step):
        peer = lax.rem(me + step, peers)
        send_chunk(out_rows.at[peer], landed.at[me], out_send, out_recv, step, peer).start()

    def make_out(step, carry):
        peer = lax.rem(me + step, peers)
        out_rows[peer] = make_rows(peer)

        @pl.when(step > 1)
        def _():
            start_out(step - 1)

        return carry

    lax.fori_loop(1, peers, make_out, 0)
    landed[me] = make_rows(me)
    start_out(peers - 1)

    def await_chunk(step):
        peer = lax.rem(me + peers - step, peers)

        @pl.when(step > 0)
        def _():
            send_chunk(
                out_rows.at[peer], landed.at[peer], out_send, out_recv, step, peer
            ).wait_recv()

        return peer

    if early is not None:

        def early_chunk(step, carry):
            for distance in range(2, parts // 2 + 1):

                @pl.when(step == (5 * peers) // 8 + distance - 2)
                def _(distance=distance):
                    for ring in rings[:1]:
                        ring.stage(distance)

            early(step, await_chunk(step))
            return carry

        lax.fori_loop(0, peers, early_chunk, 0)
    for ring in rings[:1]:
        ring.finish()
    for ring in rings[1:]:
        ring.stage(1)

    def one_chunk(step, carry):
        if early is None:
            peer = await_chunk(step)
        else:
            peer = lax.rem(me + peers - step, peers)
        work(step, peer)

        @pl.when(step > 0)
        def _():
            send_chunk(results.at[step], back.at[me], back_send, back_recv, step, peer).start()

        return carry

    lax.fori_loop(0, peers, one_chunk, 0)
    for distance in range(2, parts // 2 + 1):
        for ring in rings[1:]:
            ring.stage(distance)
    back[me] = results[0]
    take_rows(me)

    def finish(step, carry):
        ahead = lax.rem(me + step, peers)
        last = send_chunk(results.at[step], back.at[ahead], back_send, back_recv, step, ahead)
        last.wait_recv()
        take_rows(ahead)
        send_chunk(out_rows.at[ahead], landed.at[me], out_send, out_recv, step, ahead).wait_send()
        last.wait_send()
        return carry

    lax.fori_loop(1, peers, finish, 0)
    for ring in rings[1:]:
        ring.finish()


def exchange_paired(peers, make_rows, work, take_rows, out_rows, landed, results, back, sems):
    out_sems, back_sems = sems[:2], sems[2:]
    me = lax.axis_index("expert")
    side = lax.axis_index("tensor")
    parity = lax.rem(side, 2)
    partner = side + 1 - 2 * parity
    spacing = landed.shape[1]
    half = spacing * 2 // 5 // 16 * 16
    common = spacing - 2 * half
    barrier = pltpu.get_barrier_semaphore()
    greet_axis(barrier, "expert", me, peers)
    greet(barrier, "tensor", partner)
    pl.semaphore_wait(barrier, peers)

    def piece(ref, index, kind):
        if kind == 0:
            return ref.at[index, pl.ds(0, common)]
        start = common + half * (parity if kind == 1 else 1 - parity)
        return ref.at[index, pl.ds(pl.multiple_of(start, 16), half)]

    def cross(pair, source, held, target, slab, step, peer):
        return [
            send(
                piece(source, held, kind),
                piece(target, slab, kind),
                pair[0].at[kind, step],
                pair[1].at[kind, step],
                "expert",
                peer,
            )
            for kind in range(2)
        ]

    def over(pair, target, slab, step, kind):
        place = piece(target, slab, kind)
        return send(place, place, pair[0].at[2, step], pair[1].at[2, step], "tensor", partner)

    def ahead_of(step):
        return lax.rem(me + step, peers)

    def behind(step):
        return lax.rem(me + peers - step, peers)

    def out_copies(step, peer):
        return cross(out_sems, out_rows, peer, landed, me, step, peer)

    def back_copies(step, peer, slab):
        return cross(back_sems, results, step, back, slab, step, peer)

    def start_out(step):
        for copy in out_copies(step, ahead_of(step)):
            copy.start()

    def make_out(step, carry):
        peer = ahead_of(step)
        out_rows[peer] = make_rows(peer)

        @pl.when(step > 1)
        def _():
            start_out(step - 1)

        return carry

    lax.fori_loop(1, peers, make_out, 0)
    landed[me] = make_rows(me)
    start_out(peers - 1)

    def pass_out(step):
        peer = behind(step)
        for copy in cross(out_sems, out_rows, peer, landed, peer, step, peer):
            copy.wait_recv()
        over(out_sems, landed, peer, step, 1).start()

    def pass_back(step):
        slab = ahead_of(step)
        for copy in back_copies(step, slab, slab):
            copy.wait_recv()
        over(back_sems, back, slab, step, 1).start()

    lag = 5

    def one_chunk(turn, carry):
        @pl.when((turn > 0) & (turn < peers))
        def _():
            pass_out(turn)

        step = turn - 1
        peer = behind(step)

        @pl.when(step > 0)
        def _():
            over(out_sems, landed, peer, step, 2).wait_recv()

        @pl.when(step >= 0)
        def _():
            work(step, peer)

        @pl.when(step > 0)
        def _():
            for copy in back_copies(step, peer, me):
                copy.start()

        @pl.when(turn > lag)
        def _():
            pass_back(turn - lag)

        return carry

    lax.fori_loop(0, peers + 1, one_chunk, 0)
    back[me] = results[0]
    take_rows(me)
    passed = max(1, peers - lag + 1)

    def collect(turn, carry):
        @pl.when((turn >= passed) & (turn < peers))
        def _():
            pass_back(turn)

        @pl.when(turn > 1)
        def _():
            slab = ahead_of(turn - 1)
            over(back_sems, back, slab, turn - 1, 2).wait_recv()
            take_rows(slab)

        return carry

    lax.fori_loop(1, peers + 1, collect, 0)

    def finish(step, carry):
        slab = ahead_of(step)
        sent = out_copies(step, slab) + back_copies(step, slab, slab)
        sent.append(over(out_sems, landed, behind(step), step, 1))
        sent.append(over(back_sems, back, slab, step, 1))
        for copy in sent:
            copy.wait_send()
        return carry

    lax.fori_loop(1, peers, finish, 0)


def slot_hits(slots, start, shape, axis):
    return slots == start + lax.broadcasted_iota(jnp.int32, shape, axis)


def one_hot(hits):
    return jnp.where(hits, 1.0, 0.0).astype(jnp.bfloat16)


def forward_kernel(peers, parts, follow, *refs):
    rows_ref, across_ref, down_ref, win_ref = refs[:4]
    sources = refs[4 : 5 + follow]
    landed, first, second = refs[5 + follow : 8 + follow]
    targets = refs[8 + follow : 9 + 2 * follow]
    out_rows, back, results, hidden_all, *sems = refs[9 + 2 * follow :]
    wout_ref = targets[0]
    spacing = landed.shape[1]
    tokens = rows_ref.shape[0]
    kinds = (1, 0)[: 1 + follow]
    local_sem = sems[-1]
    rings, copies = [], []
    for order, kind in enumerate(kinds):
        pair = (sources[order], targets[order])
        rings.append(weight_ring(parts, kind, *pair, sems[4 + 2 * order], sems[5 + 2 * order]))
        copies.append(own_weight(kind, *pair, local_sem.at[order]))
    for copy in copies:
        copy.start()
    copies[0].wait()
    width = win_ref.shape[1] // parts
    first[...] = jnp.zeros_like(first)
    second[...] = jnp.zeros_like(second)

    def make_rows(peer):
        shape = (spacing, tokens)
        hits = [slot_hits(across_ref[k : k + 1], peer * spacing, shape, 0) for k in range(2)]
        return jnp.dot(
            one_hot(hits[0] | hits[1]), rows_ref[...], preferred_element_type=jnp.float32
        ).astype(jnp.bfloat16)

    def early(step, peer):
        chunk = landed[peer]
        for part in range(parts):
            cols = slice(part * width, (part + 1) * width)
            before = jnp.dot(chunk, win_ref[:, cols], preferred_element_type=jnp.float32)
            hidden_all[step, :, cols] = gelu_exact(before).astype(jnp.bfloat16)

    def work(step, peer):
        results[step] = jnp.dot(
            hidden_all[step], wout_ref[...], preferred_element_type=jnp.float32
        ).astype(jnp.bfloat16)

    def take_rows(slab):
        rows_back = back[slab]
        for k, kept in enumerate((first, second)):
            hits = slot_hits(down_ref[:, k : k + 1], slab * spacing, (tokens, spacing), 1)
            kept[...] += jnp.dot(
                one_hot(hits), rows_back, preferred_element_type=jnp.float32
            ).astype(jnp.bfloat16)

    exchange_chunks(
        peers,
        make_rows,
        work,
        take_rows,
        out_rows,
        landed,
        results,
        back,
        sems[:4],
        parts=parts,
        rings=rings,
        early=early,
    )
    for copy in copies[1:]:
        copy.wait()


def backward_kernel(
    peers,
    parts,
    first_ref,
    second_ref,
    across_ref,
    down_ref,
    arrived_ref,
    win_ref,
    wout_ref,
    token_grad,
    win_grad,
    wout_grad,
    out_rows,
    landed,
    back,
    results,
    total,
    hidden_all,
    before_all,
    *sems,
):
    width = win_ref.shape[1] // parts
    spacing = landed.shape[1]
    tokens = first_ref.shape[0]
    own = lax.axis_index("tensor") * width
    win_grad[...] = jnp.zeros_like(win_grad)
    wout_grad[...] = jnp.zeros_like(wout_grad)
    token_grad[...] = jnp.zeros_like(token_grad)

    def make_rows(peer):
        made = 0.0
        for k, rows_ref in enumerate((first_ref, second_ref)):
            hits = slot_hits(across_ref[k : k + 1], peer * spacing, (spacing, tokens), 0)
            made += jnp.dot(one_hot(hits), rows_ref[...], preferred_element_type=jnp.float32)
        return made.astype(jnp.bfloat16)

    def work(step, peer):
        chunk = arrived_ref[peer]
        grad_chunk = landed[peer]
        for part in range(parts):
            cols = slice(part * width, (part + 1) * width)
            before = jnp.dot(chunk, win_ref[:, cols], preferred_element_type=jnp.float32)
            value, slope = gelu_parts(before)
            grad_hidden = contract_last(grad_chunk, wout_ref[cols, :])
            grad_before = (grad_hidden * slope).astype(jnp.bfloat16)
            hidden_all[:, cols] = value.astype(jnp.bfloat16)
            before_all[:, cols] = grad_before
            term = contract_last(grad_before, win_ref[:, cols])
            if part == 0:
                total[...] = term
            elif part < parts - 1:
                total[...] += term
            else:
                results[step] = (total[...] + term).astype(jnp.bfloat16)
        mine = pl.ds(pl.multiple_of(own, width), width)
        wout_grad[...] += contract_rows(hidden_all[:, mine], grad_chunk)
        win_grad[...] += contract_rows(chunk, before_all[:, mine])

    def take_rows(slab):
        shape = (tokens, spacing)
        hits = [slot_hits(down_ref[:, k : k + 1], slab * spacing, shape, 1) for k in range(2)]
        token_grad[...] += jnp.dot(
            one_hot(hits[0] | hits[1]), back[slab], preferred_element_type=jnp.float32
        )

    exchange_paired(peers, make_rows, work, take_rows, out_rows, landed, results, back, sems)


def sum_kernel(peers, rows_ref, sum_ref, landed, sends, arrivals):
    me = lax.axis_index("expert")
    meet_peers(me, peers)

    def start_out(step, carry):
        peer = lax.rem(me + step, peers)
        send_chunk(rows_ref.at[peer], landed.at[me], sends, arrivals, step, peer).start()
        return carry

    lax.fori_loop(1, peers, start_out, 0)
    landed[me] = rows_ref[me]

    def finish(step, carry):
        peer = lax.rem(me + peers - step, peers)
        one = send_chunk(rows_ref.at[peer], landed.at[peer], sends, arrivals, step, peer)
        one.wait_send()
        one.wait_recv()
        return carry

    lax.fori_loop(1, peers, finish, 0)
    sum_ref[...] = landed[0].astype(jnp.float32)

    def add_one(source, carry):
        sum_ref[...] += landed[source].astype(jnp.float32)
        return carry

    lax.fori_loop(1, peers, add_one, 0)


def sum_shares(rows):
    peers = rows.shape[0]
    return pl.pallas_call(
        functools.partial(sum_kernel, peers),
        out_shape=jax.ShapeDtypeStruct(rows.shape[1:], jnp.float32),
        in_specs=whole_in_vmem(1),
        out_specs=whole_in_vmem(1)[0],
        scratch_shapes=[pltpu.VMEM(rows.shape, rows.dtype)] + [pltpu.SemaphoreType.DMA((peers,))] * 2,
        compiler_params=pltpu.CompilerParams(collective_id=2, has_side_effects=True),
    )(rows)


def whole_in_vmem(count):
    return [pl.BlockSpec(memory_space=pltpu.VMEM)] * count


def exchange_sems(peers):
    return [pltpu.SemaphoreType.DMA((peers,)) for _ in range(4)]


def experts_forward(rows, slots, peers, spacing, win, wout_part, parts, following=()):
    tokens, width = rows.shape
    chunks = (peers, spacing, width)
    follow = len(following)
    wholes = (jax.ShapeDtypeStruct(win.shape[::-1], win.dtype),)
    wholes += (jax.ShapeDtypeStruct(win.shape, win.dtype),) * follow
    outs = tuple(
        jax.ShapeDtypeStruct(shape, jnp.bfloat16) for shape in (chunks, rows.shape, rows.shape)
    )
    return pl.pallas_call(
        functools.partial(forward_kernel, peers, parts, follow),
        out_shape=outs + wholes,
        in_specs=whole_in_vmem(5 + follow),
        out_specs=tuple(whole_in_vmem(4 + follow)),
        scratch_shapes=[pltpu.VMEM(chunks, jnp.bfloat16)] * 3
        + [pltpu.VMEM((peers, spacing, win.shape[1]), jnp.bfloat16)]
        + exchange_sems(peers)
        + [pltpu.SemaphoreType.DMA((parts,))] * (2 + 2 * follow)
        + [pltpu.SemaphoreType.DMA((2,))],
        compiler_params=pltpu.CompilerParams(
            collective_id=4 if follow else 0, has_side_effects=True
        ),
    )(rows, slots.T, slots, win, wout_part, *following)


def experts_backward(first, second, slots, arrived, win, wout, parts):
    peers, spacing, width = arrived.shape
    inner = win.shape[1]
    return pl.pallas_call(
        functools.partial(backward_kernel, peers, parts),
        out_shape=(
            jax.ShapeDtypeStruct(first.shape, jnp.float32),
            jax.ShapeDtypeStruct((width, inner // parts), jnp.float32),
            jax.ShapeDtypeStruct((inner // parts, width), jnp.float32),
        ),
        in_specs=whole_in_vmem(7),
        out_specs=tuple(whole_in_vmem(3)),
        scratch_shapes=[pltpu.VMEM(arrived.shape, jnp.bfloat16)] * 4
        + [pltpu.VMEM((spacing, width), jnp.float32)]
        + [pltpu.VMEM((spacing, inner), jnp.bfloat16)] * 2
        + [pltpu.SemaphoreType.DMA((3, peers))] * 4,
        compiler_params=pltpu.CompilerParams(collective_id=1, has_side_effects=True),
    )(first, second, slots.T, slots, arrived, win, wout)


def norm_parts(rows_in):
    centred = rows_in - jnp.mean(rows_in, axis=-1, keepdims=True)
    inverse = lax.rsqrt(jnp.mean(centred * centred, axis=-1, keepdims=True) + 1e-06)
    return centred * inverse, inverse


def norm_back(unit, inverse, gain_row, grad_rows):
    scaled = grad_rows * gain_row
    inner = scaled - jnp.mean(scaled, axis=-1, keepdims=True)
    return inverse * (inner - unit * jnp.mean(scaled * unit, axis=-1, keepdims=True))


def two_heads(rows):
    low_half = lax.broadcasted_iota(jnp.int32, rows.shape, 1) < HEAD_DIM
    none = jnp.zeros_like(rows)
    return jnp.concatenate([jnp.where(low_half, rows, none), jnp.where(low_half, none, rows)], 0)


def join_heads(stacked):
    rows = stacked.shape[0] // 2
    low_half = lax.broadcasted_iota(jnp.int32, (rows, stacked.shape[1]), 1) < HEAD_DIM
    return jnp.where(low_half, stacked[:rows], stacked[rows:])


def pair_attention(query_two, key_pair):
    scores = contract_last(query_two, key_pair) * (HEAD_DIM ** (-0.5))
    real_key = lax.broadcasted_iota(jnp.int32, scores.shape, 1) < SEQ
    scores = jnp.where(real_key, scores, -jnp.inf)
    weights = jnp.exp(scores - jnp.max(scores, axis=-1, keepdims=True))
    return weights * (1.0 / jnp.sum(weights, axis=-1, keepdims=True))


def project_qkv(normed, mats_ref):
    return [
        jnp.dot(normed, mats_ref[part], preferred_element_type=jnp.float32).astype(jnp.bfloat16)
        for part in range(3)
    ]


def attend_kernel(
    experts, stream_ref, mats_ref, gains_ref, router_ref, middle_ref, normed_ref, probs_ref, mixed_ref
):
    rows = stream_ref[0]
    normed = (norm_parts(rows)[0] * gains_ref[0:1]).astype(jnp.bfloat16)
    query, keys, values = project_qkv(normed, mats_ref)
    for pair in range(query.shape[1] // (2 * HEAD_DIM)):
        cols = slice(pair * 2 * HEAD_DIM, (pair + 1) * 2 * HEAD_DIM)
        attention = pair_attention(two_heads(query[:, cols]), keys[:, cols]).astype(jnp.bfloat16)
        mixed = jnp.dot(attention, values[:, cols], preferred_element_type=jnp.float32)
        mixed_ref[0, :, cols] = join_heads(mixed).astype(jnp.bfloat16)
    middle = rows + contract_last(mixed_ref[0], mats_ref[3])
    middle_ref[0] = middle
    normed_two = (norm_parts(middle)[0] * gains_ref[1:2]).astype(jnp.bfloat16)
    normed_ref[0] = normed_two
    logits = jnp.dot(normed_two, router_ref[...], preferred_element_type=jnp.float32)
    real = lax.broadcasted_iota(jnp.int32, logits.shape, 1) < experts
    logits = jnp.where(real, logits, -jnp.inf)
    odds = jnp.exp(logits - jnp.max(logits, axis=-1, keepdims=True))
    probs_ref[0] = odds * (1.0 / jnp.sum(odds, axis=-1, keepdims=True))


def attend_back_kernel(
    own_ref,
    upstream_ref,
    grad_ref,
    grad_logits_ref,
    stream_ref,
    middle_ref,
    mixed_ref,
    mats_ref,
    gains_ref,
    router_ref,
    down_ref,
    mats_grad,
    router_grad,
    gains_grad,
    triple,
):
    @pl.when(pl.program_id(0) == 0)
    def _():
        mats_grad[...] = jnp.zeros_like(mats_grad)
        router_grad[...] = jnp.zeros_like(router_grad)
        gains_grad[...] = jnp.zeros_like(gains_grad)

    head_cols = mats_grad.shape[2]
    mine = pl.ds(pl.multiple_of(own_ref[0] * head_cols, head_cols), head_cols)
    gain_one, gain_two = gains_ref[0:1], gains_ref[1:2]
    unit_two, inverse_two = norm_parts(middle_ref[0])
    grad_logits = grad_logits_ref[0]
    router_grad[...] += contract_rows(
        grad_logits, (unit_two * gain_two).astype(jnp.bfloat16)
    )
    grad_normed = grad_ref[0] + contract_last(grad_logits, router_ref[...])
    gains_grad[1:2] += jnp.sum(grad_normed * unit_two, axis=0, keepdims=True)
    grad_middle = upstream_ref[0] + norm_back(unit_two, inverse_two, gain_two, grad_normed)
    grad_branch = grad_middle.astype(jnp.bfloat16)
    mats_grad[3] += contract_rows(grad_branch, mixed_ref[0, :, mine])
    grad_mixed = jnp.dot(
        grad_branch, mats_ref[3], preferred_element_type=jnp.float32
    ).astype(jnp.bfloat16)
    unit_one, inverse_one = norm_parts(stream_ref[0])
    normed = (unit_one * gain_one).astype(jnp.bfloat16)
    query, keys, values = project_qkv(normed, mats_ref)
    scale = HEAD_DIM ** (-0.5)
    for pair in range(query.shape[1] // (2 * HEAD_DIM)):
        cols = slice(pair * 2 * HEAD_DIM, (pair + 1) * 2 * HEAD_DIM)
        query_two = two_heads(query[:, cols])
        attention = pair_attention(query_two, keys[:, cols])
        grad_two = two_heads(grad_mixed[:, cols])
        triple[2, :, cols] = contract_rows(attention.astype(jnp.bfloat16), grad_two).astype(
            jnp.bfloat16
        )
        grad_attention = contract_last(grad_two, values[:, cols])
        grad_scores = (
            attention
            * (grad_attention - jnp.sum(attention * grad_attention, axis=-1, keepdims=True))
        ).astype(jnp.bfloat16)
        grad_query = jnp.dot(grad_scores, keys[:, cols], preferred_element_type=jnp.float32)
        triple[0, :, cols] = (join_heads(grad_query) * scale).astype(jnp.bfloat16)
        triple[1, :, cols] = (contract_rows(grad_scores, query_two) * scale).astype(jnp.bfloat16)
    grad_one = contract_last(triple[0], mats_ref[0])
    for part in range(3):
        if part:
            grad_one += contract_last(triple[part], mats_ref[part])
        mats_grad[part] += contract_rows(normed, triple[part, :, mine])
    gains_grad[0:1] += jnp.sum(grad_one * unit_one, axis=0, keepdims=True)
    down_ref[0] = grad_middle + norm_back(unit_one, inverse_one, gain_one, grad_one)


def image_spec(array):
    return pl.BlockSpec((1,) + array.shape[1:], lambda image: (image, 0, 0))


def fixed_spec(array):
    return pl.BlockSpec(array.shape, lambda image: (0,) * len(array.shape))


def attend(stream, mats, gains, router, experts):
    images, rows, width = stream.shape
    outs = (
        jax.ShapeDtypeStruct(stream.shape, jnp.float32),
        jax.ShapeDtypeStruct(stream.shape, jnp.bfloat16),
        jax.ShapeDtypeStruct((images, rows, router.shape[1]), jnp.float32),
        jax.ShapeDtypeStruct((images, rows, mats.shape[2]), jnp.bfloat16),
    )
    return pl.pallas_call(
        functools.partial(attend_kernel, experts),
        grid=(images,),
        out_shape=outs,
        in_specs=[image_spec(stream), fixed_spec(mats), fixed_spec(gains), fixed_spec(router)],
        out_specs=tuple(image_spec(one) for one in outs),
    )(stream, mats, gains, router)


def attend_back(upstream, grad_normed, grad_logits, stream, middle, mixed, mats, gains, router, head_cols):
    images, rows, width = stream.shape
    own = lax.axis_index("tensor").astype(jnp.int32).reshape(1)
    sums = (
        jax.ShapeDtypeStruct((4, width, head_cols), jnp.float32),
        jax.ShapeDtypeStruct((router.shape[1], width), jnp.float32),
        jax.ShapeDtypeStruct(gains.shape, jnp.float32),
    )
    per_image = [upstream, grad_normed, grad_logits, stream, middle, mixed]
    fixed = [mats, gains, router]
    return pl.pallas_call(
        attend_back_kernel,
        grid=(images,),
        out_shape=(jax.ShapeDtypeStruct(stream.shape, jnp.float32),) + sums,
        in_specs=[pl.BlockSpec(memory_space=pltpu.SMEM)]
        + [image_spec(one) for one in per_image]
        + [fixed_spec(one) for one in fixed],
        out_specs=(image_spec(stream),) + tuple(fixed_spec(one) for one in sums),
        scratch_shapes=[pltpu.VMEM((3, rows, mats.shape[2]), jnp.bfloat16)],
    )(own, *per_image, *fixed)


def slot_plan(chosen, rank_rows, experts, capacity, spacing):
    columns = lax.broadcasted_iota(jnp.int32, (1, experts), 1)
    first_hot = (chosen[:, 0:1] == columns).astype(jnp.bfloat16)
    second = (chosen[:, 1:2] == columns).astype(jnp.bfloat16)
    earlier = (rank_rows[None, :] < rank_rows[:, None]).astype(jnp.bfloat16)
    count_first = jnp.dot(earlier, first_hot, preferred_element_type=jnp.float32)
    count_second = jnp.dot(earlier, second, preferred_element_type=jnp.float32)
    first_f = first_hot.astype(jnp.float32)
    second_f = second.astype(jnp.float32)
    filled = jnp.sum(first_f, axis=0, keepdims=True)
    slot_first = jnp.sum(count_first * first_f, axis=1)
    slot_second = jnp.sum((filled + count_second) * second_f, axis=1)
    slot_nums = jnp.stack([slot_first, slot_second], axis=1).astype(jnp.int32)
    target = jnp.where(slot_nums < capacity, chosen * spacing + slot_nums, experts * spacing)
    return (target, first_f, second_f)


def local(
    inputs,
    cotangent,
    routes,
    priority,
    attend_in,
    attend_out,
    router,
    norm_gains,
    expert_in,
    expert_out,
):
    experts = lax.axis_size("expert")
    tokens = inputs.shape[0]
    model_width = inputs.shape[1]
    images = tokens // SEQ
    head_cols = attend_in.shape[3]
    layers = attend_in.shape[0]
    capacity = max(2, (10 * tokens + 4 * experts - 1) // (4 * experts))
    peers_tensor = lax.axis_size("tensor")
    spacing = -(-capacity // 16) * 16
    row_share = attend_in.shape[2]
    gain_share = norm_gains.shape[2]
    image_rows = -(-SEQ // 16) * 16
    tokens_all = images * image_rows

    def spread(rows, fill):
        shaped = rows.reshape((images, SEQ) + rows.shape[1:])
        edges = ((0, 0), (0, image_rows - SEQ)) + ((0, 0),) * (rows.ndim - 1)
        return jnp.pad(shaped, edges, constant_values=fill)

    smalls = jnp.concatenate([router.reshape(-1), norm_gains.reshape(-1)])
    block = row_share * head_cols
    smalls = jnp.pad(smalls, (0, -smalls.shape[0] % block)).reshape(-1, row_share, head_cols)
    packed = jnp.concatenate(
        [
            jnp.concatenate([attend_in, attend_out.transpose(0, 2, 1)[:, None]], axis=1).reshape(
                -1, row_share, head_cols
            ),
            smalls,
        ]
    )
    whole, win_first = gather_start(
        packed.astype(jnp.bfloat16),
        expert_in[0, 0].astype(jnp.bfloat16),
        experts,
        peers_tensor,
    )
    whole = whole.reshape(whole.shape[0], model_width, model_width)
    small_rows = whole[4 * layers :, :, :head_cols].reshape(-1, experts, block)
    small_rows = small_rows.transpose(1, 0, 2).reshape(experts, -1)
    router_all = small_rows[:, : layers * model_width].reshape(experts, layers, model_width)
    gains_all = small_rows[:, layers * model_width :][:, : layers * 2 * gain_share]
    gains_all = gains_all.reshape(experts, layers, 2, gain_share).transpose(1, 2, 0, 3)
    gains_all = gains_all.reshape(layers, 2, model_width).astype(jnp.float32)
    router_all = jnp.pad(router_all.transpose(1, 2, 0), ((0, 0), (0, 0), (0, -experts % 128)))
    win_full, wout_full = [win_first], []
    stream = spread(inputs, 0)
    stash_list = []
    for layer_index in range(layers):
        mats = whole[4 * layer_index : 4 * layer_index + 4]
        gains_now = gains_all[layer_index]
        router_now = router_all[layer_index]
        middle, normed_two, probs_all, mixed_heads = attend(
            stream, mats, gains_now, router_now, experts
        )
        probs_all = probs_all.reshape(tokens_all, -1)[:, :experts]
        chosen = spread(routes[layer_index], -1).reshape(tokens_all, 2)
        ranks = spread(priority[layer_index], tokens).reshape(tokens_all)
        target, first_f, second_f = slot_plan(chosen, ranks, experts, capacity, spacing)
        gate_values = jnp.stack(
            [jnp.sum(probs_all * first_f, axis=1), jnp.sum(probs_all * second_f, axis=1)], axis=1
        )
        following = ()
        if layer_index + 1 < layers:
            following = (expert_in[layer_index + 1, 0].astype(jnp.bfloat16),)
        arrived, rows_first, rows_second, wout_now, *gathered = experts_forward(
            normed_two.reshape(tokens_all, model_width),
            target,
            experts,
            spacing,
            win_full[layer_index],
            expert_out[layer_index, 0].astype(jnp.bfloat16),
            peers_tensor,
            following,
        )
        win_full.extend(gathered)
        wout_full.append(wout_now)
        rows_first = rows_first.astype(jnp.float32)
        rows_second = rows_second.astype(jnp.float32)
        output = (
            middle.reshape(tokens_all, model_width)
            + gate_values[:, 0:1] * rows_first
            + gate_values[:, 1:2] * rows_second
        )
        stash_list.append(
            (
                stream,
                mats,
                gains_now,
                router_now,
                mixed_heads,
                middle,
                probs_all,
                gate_values,
                first_f,
                second_f,
                target,
                arrived,
                rows_first,
                rows_second,
            )
        )
        stream = output.reshape(images, image_rows, model_width)
    upstream = spread(cotangent, 0).reshape(tokens_all, model_width)
    grads_in, grads_out, grads_router, grads_gain, grads_win, grads_wout = ([], [], [], [], [], [])
    grads_shared = []
    for layer_index in reversed(range(layers)):
        (
            stream_in,
            mats,
            gains_now,
            router_now,
            mixed_heads,
            middle,
            probs_all,
            gate_values,
            first_f,
            second_f,
            target,
            arrived,
            rows_first,
            rows_second,
        ) = stash_list[layer_index]
        gate_first = jnp.sum(upstream * rows_first, axis=1)
        gate_second = jnp.sum(upstream * rows_second, axis=1)
        scaled_first = (gate_values[:, 0:1] * upstream).astype(jnp.bfloat16)
        scaled_second = (gate_values[:, 1:2] * upstream).astype(jnp.bfloat16)
        grad_normed, win_grad, wout_grad = experts_backward(
            scaled_first,
            scaled_second,
            target,
            arrived,
            win_full[layer_index],
            wout_full[layer_index],
            peers_tensor,
        )
        grads_win.append(win_grad)
        grads_wout.append(wout_grad)
        grad_probs = first_f * gate_first[:, None] + second_f * gate_second[:, None]
        grad_logits = (
            probs_all * (grad_probs - jnp.sum(probs_all * grad_probs, axis=1, keepdims=True))
        ).astype(jnp.bfloat16)
        grad_logits = jnp.pad(grad_logits, ((0, 0), (0, router_now.shape[1] - experts)))
        shape = stream_in.shape
        down, mats_grad, router_grad, gain_grad = attend_back(
            upstream.reshape(shape),
            grad_normed.reshape(shape),
            grad_logits.reshape(images, image_rows, -1),
            stream_in,
            middle,
            mixed_heads,
            mats,
            gains_now,
            router_now,
            head_cols,
        )
        mats_grad = mats_grad.reshape(4, experts, row_share, head_cols).transpose(1, 0, 2, 3)
        router_grad = router_grad[:experts]
        gain_grad = gain_grad.reshape(2, experts, gain_share)
        smalls = jnp.concatenate(
            [router_grad, gain_grad.transpose(1, 0, 2).reshape(experts, -1)], axis=1
        )
        smalls = jnp.pad(smalls, ((0, 0), (0, -smalls.shape[1] % 2048)))
        grads_shared.append(
            jnp.concatenate(
                [mats_grad.reshape(experts, -1, 128), smalls.reshape(experts, -1, 128)], axis=1
            ).astype(jnp.bfloat16)
        )
        upstream = down.reshape(tokens_all, model_width)
    total_rows = grads_shared[0].shape[1]
    mat_rows = 4 * row_share * head_cols // 128
    shared_all = sum_shares(jnp.concatenate(grads_shared, axis=1))
    for order in range(layers):
        shared = shared_all[order * total_rows : (order + 1) * total_rows]
        mats_own = shared[:mat_rows].reshape(4, row_share, head_cols)
        small_own = shared[mat_rows:].reshape(-1)
        grads_in.append(mats_own[:3])
        grads_out.append(mats_own[3].T)
        grads_router.append(small_own[:model_width, None])
        grads_gain.append(
            small_own[model_width : model_width + 2 * gain_share].reshape(2, gain_share)
        )
    win_grad_all = jnp.stack(grads_win[::-1])[:, None]
    wout_grad_all = jnp.stack(grads_wout[::-1])[:, None]
    return (
        stream[:, :SEQ].reshape(tokens, model_width),
        upstream.reshape(stream.shape)[:, :SEQ].reshape(tokens, model_width),
        jnp.stack(grads_in[::-1]),
        jnp.stack(grads_out[::-1]),
        jnp.stack(grads_router[::-1]),
        jnp.stack(grads_gain[::-1]),
        win_grad_all,
        wout_grad_all,
    )


def solution(mesh):
    placed = (
        P("expert", None),
        P("expert", None),
        P(None, "expert", None),
        P(None, "expert"),
        P(None, None, "expert", "tensor"),
        P(None, "tensor", "expert"),
        P(None, None, "expert"),
        P(None, None, "expert"),
        P(None, "expert", None, "tensor"),
        P(None, "expert", "tensor", None),
    )
    return jax.shard_map(
        local,
        mesh=mesh,
        in_specs=placed,
        out_specs=(
            P("expert", None),
            P("expert", None),
            P(None, None, "expert", "tensor"),
            P(None, "tensor", "expert"),
            P(None, None, "expert"),
            P(None, None, "expert"),
            P(None, "expert", None, "tensor"),
            P(None, "expert", "tensor", None),
        ),
        check_vma=False,
    )
```
